32 devices in a mesh: sub: 8 (over y, x, core), in: 4 (over z).
Axes of the slice: x: 2, y: 2, z: 4, core: 2. Of those that a mesh axis runs over, the one named last changes fastest.
Arguments:
- body_load: float32 [4, 32, 32, 1024], P(None, 'in', None, 'sub'), may hold values from -6 to 6
- materials: int32 [32, 32, 1024], P('in', None, 'sub'), may hold values from 0 to 7
- material_tables: float32 [8, 4, 4], replicated
- corner_index: int32 [256], P(('sub', 'in')), may hold values from 0 to 1023
- coarse_inverse: float32 [256, 256], P(('sub', 'in')), as said below
Outputs:
- interior_solution: float32 [4, 32, 32, 1024], P(None, 'in', None, 'sub')
- interface_sum: float32 [8, 4, 32, 32], P('sub', None, 'in')
The draws below stay inside these ranges and needn't reach their ends.
Inputs may be any that keep to these rules, and one draw needn't show every extreme that they name: coarse_inverse is symmetric.
All inputs are finite; a program needn't handle non-finite values.
Results may differ from the reference program's by a relative error of at most 0.0003.
Values sent between devices are 32-bit elements; how exact they have to be, the bound alone decides.
No kernel may reach another device: no remote copies, remote signals or barrier semaphores. Data moves between devices by JAX's collectives and lax.ppermute only.
A program may use at most 64 MiB of HBM per device.

```python
import jax
import jax.numpy as jnp
from jax import lax

COMP = 4
NMAT = 8
ITERS = 3
CZ = 8
PY = 32
PX = 128
KC = 8
NZ = 32
NX = 1024
COARSE = 256
N_SUB = 8
N_IN = 4


def draw_material_tables(key, part):
    base_draw = jax.random.normal(key, (NMAT, COMP, COMP), jnp.float32)
    square = jnp.einsum('kcd,ked->kce', base_draw, base_draw)
    return 0.5 * square + 0.5 * jnp.eye(COMP, dtype=jnp.float32)[None]


def draw_coarse_inverse(key, part):
    first_key = jax.random.fold_in(key, 11)
    second_key = jax.random.fold_in(key, 23)
    base_draw = jax.random.normal(first_key, (COARSE, COARSE), jnp.float32)
    base_draw = base_draw / jnp.sqrt(jnp.float32(COARSE))
    symmetric = (base_draw + base_draw.T) * 0.5
    on_diagonal = jnp.exp(jax.random.uniform(second_key, (COARSE,), jnp.float32, jnp.log(0.5), jnp.log(2.0)))
    return symmetric + jnp.diag(on_diagonal)


def with_ends(entries, own_key, smallest, high):
    spot = [jax.random.randint(jax.random.fold_in(own_key, axis), (), 0, length) for axis, length in enumerate(entries.shape)]
    main_axis = entries.shape.index(max(entries.shape))
    neighbour = spot[:main_axis] + [(spot[main_axis] + 1) % entries.shape[main_axis]] + spot[main_axis + 1:]
    return entries.at[tuple(spot)].set(smallest).at[tuple(neighbour)].set(high)


def level_of(rng, shape, cuts, smallest, high):
    def one(position, parts):
        heights = jax.random.uniform(jax.random.fold_in(jax.random.fold_in(rng, 6), position), (parts,), jnp.float32, smallest / len(cuts), high / len(cuts))
        return jnp.repeat(jnp.exp(heights), shape[position] // parts).reshape((-1,) + (1,) * (len(shape) - position - 1))

    gain = one(*cuts[0])
    for cut in cuts[1:]:
        gain = gain * one(*cut)
    return gain


def bell_draw(key, extent, scale, reach, cuts=(), kind=jnp.bfloat16):
    result = scale * jax.random.normal(key, extent, jnp.float32)
    if cuts:
        result = result * level_of(key, extent, cuts, -0.22, 0.18)
    return jnp.clip(result, -reach, reach).astype(kind)


def setup_inputs(seed: int = 0) -> dict:
    key_list = jax.random.split(jax.random.key(seed), 6)
    body_load = bell_draw(key_list[0], (COMP, NZ, PY, NX), 1.0, 6.0, ((1, 4), (3, 8)), jnp.float32)
    materials = with_ends(jax.random.randint(key_list[1], (NZ, PY, NX), 0, NMAT), jax.random.fold_in(key_list[1], 1), 0, NMAT - 1).astype(jnp.int32)
    material_tables = draw_material_tables(jax.random.fold_in(key_list[5], 71), 0)
    corner_index = with_ends(jax.random.randint(key_list[3], (COARSE,), 0, COMP * CZ * PY), jax.random.fold_in(key_list[3], 1), 0, (COMP * CZ * PY) - 1).astype(jnp.int32)
    coarse_inverse = draw_coarse_inverse(jax.random.fold_in(key_list[5], 71), 0)
    return {"body_load": body_load, "materials": materials, "material_tables": material_tables, "corner_index": corner_index, "coarse_inverse": coarse_inverse}


def node_tables(material, tables):
    total = jnp.zeros((COMP, COMP) + material.shape, jnp.float32)
    for material_kind in range(NMAT):
        chosen = (material == material_kind).astype(jnp.float32)
        total = total + chosen[None, None] * tables[material_kind][:, :, None, None, None]
    return total


def operate(values, gains):
    padded = jnp.pad(values, ((0, 0), (1, 1), (1, 1), (1, 1)))
    beside = padded[:, 2:, 1:-1, 1:-1] + padded[:, :-2, 1:-1, 1:-1]
    beside = beside + padded[:, 1:-1, 2:, 1:-1] + padded[:, 1:-1, :-2, 1:-1]
    beside = beside + padded[:, 1:-1, 1:-1, 2:] + padded[:, 1:-1, 1:-1, :-2]
    coupled = jnp.sum(gains * values[None], axis=1)
    return 6.0 * values + coupled - beside


def conjugate(right_side, gains):
    solution = jnp.zeros_like(right_side)
    residual = right_side
    direction = right_side
    norm_now = jnp.sum(residual * residual)
    for repeat in range(ITERS):
        applied = operate(direction, gains)
        step_size = norm_now / jnp.sum(direction * applied)
        solution = solution + step_size * direction
        residual = residual - step_size * applied
        norm_next = jnp.sum(residual * residual)
        direction = residual + (norm_next / norm_now) * direction
        norm_now = norm_next
    return solution, residual


def reference(body_load, materials, material_tables, corner_index, coarse_inverse):
    loads = body_load.reshape(COMP, NZ, PY, N_SUB, PX).transpose(3, 0, 1, 2, 4)
    kinds = materials.reshape(NZ, PY, N_SUB, PX).transpose(2, 0, 1, 3)

    def solve_block(pieces):
        gains = node_tables(pieces[1], material_tables)
        return conjugate(pieces[0], gains)

    solutions, residuals = lax.map(solve_block, (loads, kinds))
    interior_solution = solutions.transpose(1, 2, 3, 0, 4).reshape(COMP, NZ, PY, NX)
    right_face = residuals[..., PX - 1]
    left_face = residuals[..., 0]
    summed = right_face + jnp.roll(left_face, -1, axis=0)
    blocks = summed.reshape(N_SUB, COMP, N_IN, CZ, PY).transpose(0, 2, 1, 3, 4)
    blocks = blocks.reshape(N_SUB * N_IN, COMP * CZ * PY)
    corner_ids = corner_index.reshape(N_SUB * N_IN, KC).astype(jnp.int32)
    coarse_residual = jnp.take_along_axis(blocks, corner_ids, axis=1).reshape(COARSE)
    coarse_solution = jnp.dot(coarse_inverse, coarse_residual, precision=lax.Precision.HIGHEST)
    row_ids = jnp.arange(N_SUB * N_IN, dtype=jnp.int32)[:, None]
    blocks = blocks.at[row_ids, corner_ids].add(coarse_solution.reshape(N_SUB * N_IN, KC))
    interface_sum = blocks.reshape(N_SUB, N_IN, COMP, CZ, PY).transpose(0, 2, 1, 3, 4).reshape(N_SUB, COMP, NZ, PY)
    return interior_solution, interface_sum
```

```python
import functools

import jax
import jax.numpy as jnp
from jax import lax
from jax.experimental import pallas as pl
from jax.experimental.pallas import tpu as pltpu
from jax.sharding import PartitionSpec as P

ITERS = 3
LANES = 128
MAT_DEPTH = ITERS - 1
PAIRS = [(i, j) for i in range(ITERS) for j in range(i, ITERS + 1)]
GRAM_LANE = 64
VMEM = pl.BlockSpec(memory_space=pltpu.VMEM)
SMEM = pl.BlockSpec(memory_space=pltpu.SMEM)
HBM = pl.BlockSpec(memory_space=pl.ANY)


def spectrum(table, comp, kinds):
    rows = lax.broadcasted_iota(jnp.int32, table.shape, 0)
    live = lax.broadcasted_iota(jnp.int32, table.shape, 1) < kinds
    diagonal = live & (lax.rem(rows, comp + 1) == 0)
    table = jnp.where(live, table, 0.0)
    mean = jnp.sum(jnp.where(diagonal, table, 0.0)) / (comp * kinds)
    centred = jnp.where(diagonal, table - mean, table)
    size = jnp.abs(centred)
    widest = 0.0
    for c in range(comp):
        widest = jnp.maximum(widest, jnp.max(jnp.sum(size[comp * c : comp * (c + 1)], axis=0, keepdims=True)))
    scale = 6.0 + widest
    return mean, scale, centred


def pack_kernel(body, mats, a_out, b_out, kinds, sems):
    comp, depth = body.shape[0], body.shape[1]
    odd = lax.rem(lax.axis_index("in"), 2)
    copies = []
    for slot, (out, low) in enumerate(((a_out, odd), (b_out, 1 - odd))):
        first = (1 - low) * (depth - ITERS)
        for c in range(comp):
            copies.append(pltpu.make_async_copy(
                body.at[c, pl.ds(first, ITERS)], out.at[pl.ds(ITERS * c, ITERS)], sems.at[slot, c]))
        first = (1 - low) * (depth - MAT_DEPTH)
        copies.append(pltpu.make_async_copy(
            mats.at[pl.ds(first, MAT_DEPTH)], kinds.at[slot], sems.at[slot, comp]))
    for copy in copies:
        copy.start()
    for copy in copies:
        copy.wait()
    for slot, out in enumerate((a_out, b_out)):
        out[pl.ds(ITERS * comp, MAT_DEPTH)] = kinds[slot].astype(jnp.float32)


def basis_kernel(kinds, body, mats, halo_a, halo_b, table, corners, corners_before,
                 v1, v2, left_out, right_out, message,
                 v0, gains, packed):
    comp, depth, py, px = body.shape
    ext = depth + 2 * ITERS
    place = lax.axis_index("in")
    last = lax.axis_size("in") - 1
    odd = lax.rem(place, 2) == 1

    mean, scale, centred = spectrum(table[...], comp, kinds)
    inverse = 1.0 / scale
    scaled = centred * inverse

    lane = lax.broadcasted_iota(jnp.int32, (py, px), 1)
    row = lax.broadcasted_iota(jnp.int32, (py, px), 0)
    first_x, last_x = lane == 0, lane == px - 1
    first_y, last_y = row == 0, row == py - 1

    for c in range(comp):
        for t in range(ITERS):
            a = halo_a[ITERS * c + t]
            b = halo_b[ITERS * c + t]
            v0[c, t] = jnp.where(odd, a, b)
            v0[c, ITERS + depth + t] = jnp.where(odd, b, a)

    def own(z, carry):
        for c in range(comp):
            v0[c, ITERS + z] = body[c, z]
        return carry
    lax.fori_loop(0, depth, own, 0)

    def neighbours(source, c, at, value):
        total = source[c, at - 1] + source[c, at + 1]
        total += jnp.where(first_x, 0.0, pltpu.roll(value, 1, 1)) + jnp.where(last_x, 0.0, pltpu.roll(value, px - 1, 1))
        total += jnp.where(first_y, 0.0, pltpu.roll(value, 1, 0)) + jnp.where(last_y, 0.0, pltpu.roll(value, py - 1, 0))
        return total

    def applied(source, at, gain):
        values = [source[c, at] for c in range(comp)]
        results = []
        for c in range(comp):
            total = gain(c, 0) * values[0]
            for d in range(1, comp):
                total += gain(c, d) * values[d]
            results.append(total - inverse * neighbours(source, c, at, values[c]))
        return values, results

    def look_up(kind, at):
        for c in range(comp):
            for d in range(comp):
                line = jnp.broadcast_to(scaled[comp * c + d : comp * c + d + 1], (py, px))
                gains[comp * c + d, at] = jnp.take_along_axis(line, kind, axis=1)

    for t in range(MAT_DEPTH):
        a = halo_a[ITERS * comp + t]
        b = halo_b[ITERS * comp + t]
        look_up(jnp.where(odd, a, b).astype(jnp.int32), 1 + t)
        look_up(jnp.where(odd, b, a).astype(jnp.int32), ITERS + depth + t)

    def own_gains(z, carry):
        look_up(mats[z], ITERS + z)
        return carry
    lax.fori_loop(0, depth, own_gains, 0)

    def first_level(at, carry):
        _, results = applied(v0, at, lambda c, d: gains[comp * c + d, at])
        for c in range(comp):
            v1[c, at] = results[c]
        return carry
    lax.fori_loop(1, ext - 1, first_level, 0)

    def clear(ref, lows, highs):
        @pl.when(place == 0)
        def _():
            for c in range(comp):
                for t in lows:
                    ref[c, t] = jnp.zeros((py, px), jnp.float32)

        @pl.when(place == last)
        def _():
            for c in range(comp):
                for t in highs:
                    ref[c, t] = jnp.zeros((py, px), jnp.float32)

    clear(v1, (1, 2), (ext - 3, ext - 2))

    def second_level(at, carry):
        _, results = applied(v1, at, lambda c, d: gains[comp * c + d, at])
        for c in range(comp):
            v2[c, at] = results[c]
        return carry
    lax.fori_loop(2, ext - 2, second_level, 0)
    clear(v2, (2,), (ext - 3,))

    def fold(value):
        total = value[0:8]
        for t in range(1, py // 8):
            total += value[8 * t : 8 * (t + 1)]
        return total

    def third_level(z, sums):
        at = ITERS + z
        thirds, fourths = applied(v2, at, lambda c, d: gains[comp * c + d, at])
        sums = list(sums)
        for c in range(comp):
            basis = [v0[c, at], v1[c, at], thirds[c], fourths[c]]
            for g, (i, j) in enumerate(PAIRS):
                sums[g] = sums[g] + fold(basis[i] * basis[j])
            block = basis[0]
            for k in range(1, ITERS + 1):
                block = jnp.where((lane == 2 * k) | (lane == 2 * k - 1), pltpu.roll(basis[k], 2 * k, 1), block)
            packed[z, pl.ds(py * c, py)] = block
        return tuple(sums)
    zero = jnp.zeros((8, px), jnp.float32)
    sums = lax.fori_loop(0, depth, third_level, tuple(zero for _ in PAIRS))

    for z in range(depth):
        turned = packed[z].T
        for k in range(ITERS + 1):
            left_out[k, pl.ds(z, 1)] = turned[2 * k : 2 * k + 1]
            at = (2 * k - 1) % px
            right_out[k, pl.ds(z, 1)] = turned[at : at + 1]

    spots = lax.broadcasted_iota(jnp.int32, (1, px), 1)
    line = jnp.zeros((1, px), jnp.float32)
    even = lax.rem(spots, 2) == 0
    slab = depth * py

    def corner_row(index):
        c = index // slab
        z = (index - c * slab) // py
        y = index - c * slab - z * py
        return packed[z, pl.ds(c * py + y, 1)]

    count = corners.shape[0]
    for j in range(count):
        mine = pltpu.roll(corner_row(corners[j]), 8 * j + 1, 1)
        before = pltpu.roll(corner_row(corners_before[j]), 8 * j + 1, 1)
        line = jnp.where(spots // 8 == j, jnp.where(even, mine, before), line)
    for g in range(len(PAIRS)):
        line = jnp.where(spots == GRAM_LANE + g, jnp.sum(sums[g]), line)
    message[...] = jnp.broadcast_to(line, message.shape)


def coefficients(gram, mean, scale):
    centre = 6.0 + mean

    def inner(u, w):
        total = None
        for i, a in enumerate(u):
            part = None
            for j, b in enumerate(w):
                term = gram[(min(i, j), max(i, j))] * b
                part = term if part is None else part + term
            part = a * part
            total = part if total is None else total + part
        return total

    one = jnp.ones_like(gram[(0, 0)])
    residual, direction, found = [one], [one], []
    norm = gram[(0, 0)]
    for repeat in range(ITERS):
        size = len(direction)
        image = [centre * direction[0]]
        for j in range(1, size):
            image.append(centre * direction[j] + scale * direction[j - 1])
        image.append(scale * direction[size - 1])
        step = norm / inner(direction, image)
        found = [
            (found[j] if j < len(found) else 0.0) + step * direction[j] for j in range(size)
        ]
        residual = [
            (residual[j] if j < size else 0.0) - step * image[j] for j in range(size + 1)
        ]
        if repeat + 1 < ITERS:
            fresh = inner(residual, residual)
            ratio = fresh / norm
            direction = [
                residual[j] + (ratio * direction[j] if j < size else 0.0) for j in range(size + 1)
            ]
            norm = fresh
    return found, residual


def final_kernel(kinds, messages, body, v1, v2, right, left_next, table, coarse, corners,
                 solution_out, interface_out, book):
    comp, depth, py, px = body.shape
    devices = messages.shape[0]
    n_in = lax.axis_size("in")
    me = lax.axis_index("sub") * n_in + lax.axis_index("in")
    following = lax.rem(me + n_in, devices)
    mean, scale, _ = spectrum(table[...], comp, kinds)

    got = messages[...]
    lane = lax.broadcasted_iota(jnp.int32, got.shape, 1)
    row = lax.broadcasted_iota(jnp.int32, got.shape, 0)
    groups = got.reshape(devices // n_in, n_in, px) if n_in % 8 == 0 else None
    if groups is not None:
        summed = jnp.broadcast_to(jnp.sum(groups, axis=1, keepdims=True), groups.shape).reshape(got.shape)
    else:
        summed = got
        reach = 1
        while reach < n_in:
            partner = jnp.where(
                lax.rem(row // reach, 2) == 0,
                pltpu.roll(summed, devices - reach, 0),
                pltpu.roll(summed, reach, 0))
            summed = summed + partner
            reach *= 2
    gram = {}
    for g, pair in enumerate(PAIRS):
        gram[pair] = summed[:, GRAM_LANE + g : GRAM_LANE + g + 1]
    found, residual = coefficients(gram, mean, scale)

    kind = lax.rem(lane, 8) // 2
    spread = jnp.zeros_like(got)
    sheet = jnp.zeros_like(got)
    for k in range(ITERS + 1):
        spread = jnp.where(kind == k, residual[k], spread)
        sheet = jnp.where(lane == k, residual[k], sheet)
    for k in range(ITERS):
        sheet = jnp.where(lane == ITERS + 1 + k, found[k], sheet)
    book[...] = sheet
    product = got * spread
    product = jnp.where(lax.rem(lane, 2) == 0, product, pltpu.roll(product, devices - n_in, 0))
    for reach in (1, 2, 4):
        product = product + pltpu.roll(product, px - reach, 1)
    count = corners.shape[0]
    spots = jnp.minimum(lane * 8, px - 1)
    product = jnp.take_along_axis(product, spots, axis=1)[:, :count]

    mine = book[pl.ds(me, 1)]
    other = book[pl.ds(following, 1)]

    face = None
    for k in range(ITERS + 1):
        part = mine[:, k : k + 1] * right[k] + other[:, k : k + 1] * left_next[k]
        face = part if face is None else face + part

    zs = lax.broadcasted_iota(jnp.int32, face.shape, 0)
    ls = lax.broadcasted_iota(jnp.int32, face.shape, 1)
    slab = depth * py
    add = jnp.zeros_like(face)
    for j in range(count):
        value = jnp.sum(coarse[j] * product)
        index = corners[j]
        c = index // slab
        z = (index - c * slab) // py
        y = index - c * slab - z * py
        add = add + jnp.where((zs == z) & (ls == c * py + y), value, 0.0)
    face = face + add
    for c in range(comp):
        interface_out[0, c] = face[:, py * c : py * (c + 1)]

    def combine(z, carry):
        at = ITERS + z
        for c in range(comp):
            total = jnp.broadcast_to(mine[:, 4:5], (py, px)) * body[c, z]
            total += jnp.broadcast_to(mine[:, 5:6], (py, px)) * v1[c, at]
            total += jnp.broadcast_to(mine[:, 6:7], (py, px)) * v2[c, at]
            solution_out[c, z] = total
        return carry
    lax.fori_loop(0, depth, combine, 0)


def on_device(body_load, materials, material_tables, corner_index, coarse_inverse):
    comp, depth, py, px = body_load.shape
    kinds = material_tables.shape[0]
    n_in, n_sub = lax.axis_size("in"), lax.axis_size("sub")
    devices = n_in * n_sub
    count = corner_index.shape[0]
    ext = depth + 2 * ITERS
    f32 = jnp.float32
    shape = jax.ShapeDtypeStruct
    halo = shape((ITERS * comp + MAT_DEPTH, py, px), f32)

    table = jnp.pad(material_tables.transpose(1, 2, 0).reshape(comp * comp, kinds), ((0, 0), (0, LANES - kinds)))
    coarse = coarse_inverse.reshape(count, devices, count)

    send_a, send_b = pl.pallas_call(
        pack_kernel,
        out_shape=(halo, halo),
        in_specs=[HBM, HBM],
        out_specs=(VMEM, VMEM),
        scratch_shapes=[
            pltpu.VMEM((2, MAT_DEPTH, py, px), jnp.int32),
            pltpu.SemaphoreType.DMA((2, comp + 1)),
        ],
        name="pack",
    )(body_load, materials)

    def swaps(start):
        pairs = [(i, i + 1) for i in range(start, n_in - 1, 2)]
        return pairs + [(j, i) for i, j in pairs]

    halo_a = lax.ppermute(send_a, "in", swaps(0))
    halo_b = lax.ppermute(send_b, "in", swaps(1))
    corners_before = lax.ppermute(corner_index, "sub", [(i, (i + 1) % n_sub) for i in range(n_sub)])

    extended = shape((comp, ext, py, px), f32)
    faces = shape((ITERS + 1, depth, comp * py), f32)
    v1, v2, left, right, message = pl.pallas_call(
        functools.partial(basis_kernel, kinds),
        out_shape=(extended, extended, faces, faces, shape((devices, LANES), f32)),
        in_specs=[VMEM, VMEM, VMEM, VMEM, VMEM, SMEM, SMEM],
        out_specs=(VMEM,) * 5,
        scratch_shapes=[
            pltpu.VMEM((comp, ext, py, px), f32),
            pltpu.VMEM((comp * comp, ext, py, px), f32),
            pltpu.VMEM((depth, comp * py, px), f32),
        ],
        name="basis",
    )(body_load, materials, halo_a, halo_b, table, corner_index, corners_before)

    left_next = lax.ppermute(left, "sub", [((i + 1) % n_sub, i) for i in range(n_sub)])
    messages = lax.all_to_all(message, ("sub", "in"), 0, 0, tiled=True)

    return pl.pallas_call(
        functools.partial(final_kernel, kinds),
        out_shape=(shape(body_load.shape, f32), shape((1, comp, depth, py), f32)),
        in_specs=[VMEM] * 8 + [SMEM],
        out_specs=(VMEM, VMEM),
        scratch_shapes=[pltpu.VMEM((devices, LANES), f32)],
        name="final",
    )(messages, body_load, v1, v2, right, left_next, table, coarse, corner_index)


def solution(mesh):
    return jax.shard_map(
        on_device,
        mesh=mesh,
        in_specs=(
            P(None, "in", None, "sub"),
            P("in", None, "sub"),
            P(),
            P(("sub", "in")),
            P(("sub", "in"), None),
        ),
        out_specs=(P(None, "in", None, "sub"), P("sub", None, "in", None)),
        check_vma=False,
    )
```

```python
import functools

import jax
import jax.numpy as jnp
from jax import lax
from jax.experimental import pallas as pl
from jax.experimental.pallas import tpu as pltpu
from jax.sharding import PartitionSpec as P

ITERS = 3
LANES = 128
MAT_DEPTH = ITERS - 1
PAIRS = [(i, j) for i in range(ITERS) for j in range(i, ITERS + 1)]
GRAM_LANE = 64
VMEM = pl.BlockSpec(memory_space=pltpu.VMEM)
SMEM = pl.BlockSpec(memory_space=pltpu.SMEM)
HBM = pl.BlockSpec(memory_space=pl.ANY)


def spectrum(table, comp):
    kinds = table.shape[1]
    rows = lax.broadcasted_iota(jnp.int32, table.shape, 0)
    diagonal = lax.rem(rows, comp + 1) == 0
    picked = jnp.where(diagonal, table, 0.0)
    mean = jnp.sum(jnp.sum(picked, axis=0, keepdims=True), axis=1, keepdims=True) / (comp * kinds)
    centred = jnp.where(diagonal, table - mean, table)
    size = jnp.abs(centred)
    widest = jnp.zeros((1, kinds), jnp.float32)
    for c in range(comp):
        widest = jnp.maximum(widest, jnp.sum(size[comp * c : comp * (c + 1)], axis=0, keepdims=True))
    scale = 6.0 + jnp.max(widest, axis=1, keepdims=True)
    return mean, scale, centred


def split(index, size):
    if size & (size - 1):
        return lax.div(index, size), lax.rem(index, size)
    return lax.shift_right_logical(index, size.bit_length() - 1), index & (size - 1)


def pack_kernel(body, mats, table, a_out, b_out, body_out, mats_out, table_out, kinds, sems, whole):
    comp, depth = body.shape[0], body.shape[1]
    odd = lax.rem(lax.axis_index("in"), 2)
    copies = []
    for slot, (out, low) in enumerate(((a_out, odd), (b_out, 1 - odd))):
        first = (1 - low) * (depth - MAT_DEPTH)
        copies.append(pltpu.make_async_copy(
            mats.at[pl.ds(first, MAT_DEPTH)], kinds.at[slot], sems.at[slot, comp]))
        first = (1 - low) * (depth - ITERS)
        for c in range(comp):
            copies.append(pltpu.make_async_copy(
                body.at[c, pl.ds(first, ITERS)], out.at[pl.ds(ITERS * c, ITERS)], sems.at[slot, c]))
    copies.append(pltpu.make_async_copy(table, table_out, whole.at[0]))
    copies.append(pltpu.make_async_copy(mats, mats_out, whole.at[1]))
    copies.append(pltpu.make_async_copy(body, body_out, whole.at[2]))
    for copy in copies:
        copy.start()
    for copy in copies:
        copy.wait()
    for slot, out in enumerate((a_out, b_out)):
        out[pl.ds(ITERS * comp, MAT_DEPTH)] = kinds[slot].astype(jnp.float32)


class Slab:
    def __init__(self, comp, py, px):
        self.comp, self.px, self.parts = comp, px, py // 8
        lane = lax.broadcasted_iota(jnp.int32, (8, px), 1)
        row = lax.broadcasted_iota(jnp.int32, (8, px), 0)
        self.lane = lane
        self.first_x, self.last_x = lane == 0, lane == px - 1
        self.first_y, self.last_y = row == 0, row == 7

    def natural(self, ref, *at):
        return [ref[(*at, pl.ds(r, 8, stride=self.parts))] for r in range(self.parts)]

    def load(self, ref, *at):
        return [ref[(*at, pl.ds(8 * r, 8))] for r in range(self.parts)]

    def store(self, ref, values, *at):
        for r in range(self.parts):
            ref[(*at, pl.ds(8 * r, 8))] = values[r]

    def neighbours(self, below, above, value):
        parts, px = self.parts, self.px
        totals = []
        for r in range(parts):
            total = below[r] + above[r]
            total += jnp.where(self.first_x, 0.0, pltpu.roll(value[r], 1, 1))
            total += jnp.where(self.last_x, 0.0, pltpu.roll(value[r], px - 1, 1))
            total += value[r - 1] if r else jnp.where(self.first_y, 0.0, pltpu.roll(value[parts - 1], 1, 0))
            total += value[r + 1] if r + 1 < parts else jnp.where(self.last_y, 0.0, pltpu.roll(value[0], 7, 0))
            totals.append(total)
        return totals

    def applied(self, source, at, gains, gains_at, inverse, alive=None):
        comp, parts = self.comp, self.parts
        values = [self.load(source, c, at) for c in range(comp)]
        for c in range(comp):
            around = self.neighbours(self.load(source, c, at - 1), self.load(source, c, at + 1), values[c])
            out = []
            for r in range(parts):
                total = None
                for d in range(comp):
                    term = gains[comp * c + d, gains_at, pl.ds(8 * r, 8)] * values[d][r]
                    total = term if total is None else total + term
                total = total - inverse * around[r]
                out.append(total if alive is None else alive * total)
            yield c, values[c], out

    def products(self, total, left, right):
        for r in range(self.parts):
            total = total + left[r] * right[r]
        return total

    def look_up(self, kinds, tab, gains, at, count):
        bits = [[(kind & (1 << b)) != 0 for kind in kinds] for b in range((count - 1).bit_length())]
        entries = self.comp * self.comp
        for e in range(entries):
            lines = [tab[pl.ds(k * entries + e, 8, stride=0)] for k in range(count)]
            out = []
            for r in range(self.parts):
                level = lines
                for bit in bits:
                    level = [
                        jnp.where(bit[r], level[k + 1], level[k]) if k + 1 < len(level) else level[k]
                        for k in range(0, len(level), 2)
                    ]
                out.append(level[0])
            self.store(gains, out, e, at)

    def pack(self, packed, z, c, basis):
        rows = self.parts * 8
        for r in range(self.parts):
            block = basis[0][r]
            for k in range(1, len(basis)):
                here = (self.lane == 2 * k) | (self.lane == 2 * k - 1)
                block = jnp.where(here, pltpu.roll(basis[k][r], 2 * k, 1), block)
            packed[z, pl.ds(rows * c + 8 * r, 8)] = block


def levels(slab, v0, v1, v2, gains, packed, inverse):
    def first(z, sums):
        g01, g11 = sums
        for c, v, w in slab.applied(v0, z + 3, gains, z + 2, inverse):
            slab.store(v1, w, c, z + 2)
            g01, g11 = slab.products(g01, v, w), slab.products(g11, w, w)
        return g01, g11

    def second(z, sums):
        g02, g12, g22 = sums
        for c, v, w in slab.applied(v1, z + 2, gains, z + 2, inverse):
            slab.store(v2, w, c, z + 1)
            u = slab.load(v0, c, z + 3)
            g02, g12, g22 = slab.products(g02, u, w), slab.products(g12, v, w), slab.products(g22, w, w)
        return g02, g12, g22

    def third(z, sums):
        g03, g13, g23 = sums
        for c, v, w in slab.applied(v2, z + 1, gains, z + 2, inverse):
            t, u = slab.load(v0, c, z + 3), slab.load(v1, c, z + 2)
            slab.pack(packed, z, c, (t, u, v, w))
            g03, g13, g23 = slab.products(g03, t, w), slab.products(g13, u, w), slab.products(g23, v, w)
        return g03, g13, g23

    return first, second, third


def interior_kernel(body, mats, table, v0, v1, v2, gains, packed, gram, tab):
    comp, depth, py, px = body.shape
    kinds = table.shape[1]
    entries = comp * comp
    slab = Slab(comp, py, px)
    mean, scale, centred = spectrum(table[...], comp)
    inverse = jnp.broadcast_to(1.0 / scale, (8, px))
    scaled = centred / scale
    for k in range(kinds):
        tab[pl.ds(k * entries, entries)] = jnp.broadcast_to(scaled[:, k : k + 1], (entries, px))
    for t, value in enumerate((inverse, mean, scale)):
        tab[pl.ds(kinds * entries + 8 * t, 8)] = jnp.broadcast_to(value, (8, px))
    zero = jnp.zeros((8, px), jnp.float32)

    def own(z, g00):
        for c in range(comp):
            value = slab.natural(body, c, z)
            slab.store(v0, value, c, ITERS + z)
            g00 = slab.products(g00, value, value)
        slab.look_up(slab.natural(mats, z), tab, gains, MAT_DEPTH + z, kinds)
        return g00
    g00 = lax.fori_loop(0, depth, own, zero)

    first, second, third = levels(slab, v0, v1, v2, gains, packed, inverse)
    g01, g11 = lax.fori_loop(1, depth - 1, first, (zero,) * 2)
    g02, g12, g22 = lax.fori_loop(2, depth - 2, second, (zero,) * 3)
    g03, g13, g23 = lax.fori_loop(3, depth - 3, third, (zero,) * 3)
    for g, value in enumerate((g00, g01, g02, g03, g11, g12, g13, g22, g23)):
        gram[g] = value


def edge_kernel(kinds, halo_a, halo_b, tab, corners_hbm, before_hbm, v0_in, v1_in, v2_in, gains_in, packed_in, gram_in,
                v0, v1, v2, gains, packed, message, corners, before, sems):
    comp, py, px = v0.shape[0], v0.shape[2], v0.shape[3]
    depth = packed.shape[0]
    fetch = (
        pltpu.make_async_copy(corners_hbm, corners, sems.at[0]),
        pltpu.make_async_copy(before_hbm, before, sems.at[1]),
    )
    for copy in fetch:
        copy.start()
    slab = Slab(comp, py, px)
    parts = slab.parts
    place = lax.axis_index("in")
    odd = lax.rem(place, 2) == 1
    inverse = tab[pl.ds(kinds * comp * comp, 8)]
    alive = (
        (place > 0).astype(jnp.float32),
        (place < lax.axis_size("in") - 1).astype(jnp.float32),
    )

    for t in range(ITERS):
        for c in range(comp):
            a = slab.natural(halo_a, ITERS * c + t)
            b = slab.natural(halo_b, ITERS * c + t)
            slab.store(v0, [jnp.where(odd, x, y) for x, y in zip(a, b)], c, t)
            slab.store(v0, [jnp.where(odd, y, x) for x, y in zip(a, b)], c, ITERS + depth + t)

    def halo_gains(t, carry):
        a = slab.natural(halo_a, ITERS * comp + t)
        b = slab.natural(halo_b, ITERS * comp + t)
        low = [jnp.where(odd, x, y).astype(jnp.int32) for x, y in zip(a, b)]
        high = [jnp.where(odd, y, x).astype(jnp.int32) for x, y in zip(a, b)]
        slab.look_up(low, tab, gains, t, kinds)
        slab.look_up(high, tab, gains, MAT_DEPTH + depth + t, kinds)
        return carry
    lax.fori_loop(0, MAT_DEPTH, halo_gains, 0)

    g00, g01, g02, g03, g11, g12, g13, g22, g23 = [gram_in[g] for g in range(len(PAIRS))]
    first, second, third = levels(slab, v0, v1, v2, gains, packed, inverse)

    def first_halo(i, carry):
        for side, z in enumerate((i - 2, depth + i)):
            for c, _, w in slab.applied(v0, z + 3, gains, z + 2, inverse, alive[side]):
                slab.store(v1, w, c, z + 2)
        return carry
    lax.fori_loop(0, 2, first_halo, 0)
    g01, g11 = lax.fori_loop(0, 2, lambda i, sums: first(i * (depth - 1), sums), (g01, g11))
    for side, z in enumerate((-1, depth)):
        for c, _, w in slab.applied(v1, z + 2, gains, z + 2, inverse, alive[side]):
            slab.store(v2, w, c, z + 1)
    g02, g12, g22 = lax.fori_loop(
        0, 2, lambda i, sums: second(depth - 2 + i, second(i, sums)), (g02, g12, g22))
    g03, g13, g23 = lax.fori_loop(
        0, 3, lambda i, sums: third(depth - 3 + i, third(i, sums)), (g03, g13, g23))

    spots = lax.broadcasted_iota(jnp.int32, (1, px), 1)
    line = jnp.zeros((1, px), jnp.float32)
    even = lax.rem(spots, 2) == 0
    for g, value in enumerate((g00, g01, g02, g03, g11, g12, g13, g22, g23)):
        total = jnp.sum(jnp.sum(value, axis=0, keepdims=True), axis=1, keepdims=True)
        line = jnp.where(spots == GRAM_LANE + g, total, line)

    for copy in fetch:
        copy.wait()

    def corner_row(index):
        c, rest = split(index, depth * py)
        z, y = split(rest, py)
        t, r = split(y, parts)
        return packed[z, pl.ds(c * py + r * 8 + t, 1)]

    for j in range(corners.shape[0]):
        mine = corner_row(corners[j])
        other = corner_row(before[j])
        odd_lanes = pltpu.roll(jnp.where(even, other, mine), 8 * j + 1, 1)
        line = jnp.where(spots // 8 == j, odd_lanes, line)
    message[...] = jnp.broadcast_to(line, message.shape)


def faces_kernel(packed, left, right):
    depth, _, px = packed.shape
    for z in range(depth):
        turned = packed[z].T
        for k in range(ITERS + 1):
            at = (2 * k - 1) % px
            left[k, pl.ds(z, 1)] = turned[2 * k : 2 * k + 1]
            right[k, pl.ds(z, 1)] = turned[at : at + 1]


def coefficients(gram, mean, scale):
    centre = 6.0 + mean

    def inner(u, w):
        total = None
        for i, a in enumerate(u):
            part = None
            for j, b in enumerate(w):
                term = gram[(min(i, j), max(i, j))] * b
                part = term if part is None else part + term
            part = a * part
            total = part if total is None else total + part
        return total

    one = jnp.ones_like(gram[(0, 0)])
    residual, direction, found = [one], [one], []
    norm = gram[(0, 0)]
    for repeat in range(ITERS):
        size = len(direction)
        image = [centre * direction[0]]
        for j in range(1, size):
            image.append(centre * direction[j] + scale * direction[j - 1])
        image.append(scale * direction[size - 1])
        step = norm / inner(direction, image)
        found = [
            (found[j] if j < len(found) else 0.0) + step * direction[j] for j in range(size)
        ]
        residual = [
            (residual[j] if j < size else 0.0) - step * image[j] for j in range(size + 1)
        ]
        if repeat + 1 < ITERS:
            fresh = inner(residual, residual)
            ratio = fresh / norm
            direction = [
                residual[j] + (ratio * direction[j] if j < size else 0.0) for j in range(size + 1)
            ]
            norm = fresh
    return found, residual


def final_kernel(kinds, messages, v0, v1, v2, right, left_next, tab, coarse, corners,
                 solution_hbm, interface_out, found_book, solution_out, sems):
    comp, py, px = v0.shape[0], v0.shape[2], v0.shape[3]
    depth = right.shape[1]
    n_in, n_sub = lax.axis_size("in"), lax.axis_size("sub")
    sub = lax.axis_index("sub")
    following = lax.rem(sub + 1, n_sub)
    slab = Slab(comp, py, px)
    base = kinds * comp * comp
    mean, scale = tab[pl.ds(base + 8, 1)][:, :1], tab[pl.ds(base + 16, 1)][:, :1]

    got = [messages[pl.ds(i, n_sub, stride=n_in)] for i in range(n_in)]
    summed = got[0]
    for i in range(1, n_in):
        summed = summed + got[i]
    gram = {}
    for g, pair in enumerate(PAIRS):
        gram[pair] = summed[:, GRAM_LANE + g : GRAM_LANE + g + 1]
    found, residual = coefficients(gram, mean, scale)

    lane = lax.broadcasted_iota(jnp.int32, summed.shape, 1)
    kind = lax.rem(lane, 8) // 2
    spread = jnp.zeros_like(summed)
    sheet = jnp.zeros_like(summed)
    for k in range(ITERS + 1):
        spread = jnp.where(kind == k, residual[k], spread)
        sheet = jnp.where(lane == k, residual[k], sheet)
    for k in range(ITERS):
        sheet = jnp.where(lane == ITERS + 1 + k, found[k], sheet)
    found_book[...] = sheet
    mine = found_book[pl.ds(sub, 1)]
    other = found_book[pl.ds(following, 1)]

    weights = [jnp.broadcast_to(mine[:, ITERS + 1 + k : ITERS + 2 + k], (8, px)) for k in range(ITERS)]
    copies = [
        pltpu.make_async_copy(solution_out.at[:, z], solution_hbm.at[:, z], sems.at[z]) for z in range(depth)
    ]
    for z in range(depth):
        for c in range(comp):
            fields = slab.load(v0, c, z + 3), slab.load(v1, c, z + 2), slab.load(v2, c, z + 1)
            for r in range(slab.parts):
                total = weights[0] * fields[0][r] + weights[1] * fields[1][r] + weights[2] * fields[2][r]
                solution_out[c, z, pl.ds(r, 8, stride=slab.parts)] = total
        copies[z].start()

    count = corners.shape[1]
    spots = jnp.minimum(lane * 8, px - 1)
    values = []
    for i in range(n_in):
        product = got[i] * spread
        product = jnp.where(lax.rem(lane, 2) == 0, product, pltpu.roll(product, n_sub - 1, 0))
        for reach in (1, 2, 4):
            product = product + pltpu.roll(product, px - reach, 1)
        values.append(jnp.take_along_axis(product, spots, axis=1, mode="promise_in_bounds")[:, :count])

    face = None
    for k in range(ITERS + 1):
        part = mine[:, k : k + 1] * right[k] + other[:, k : k + 1] * left_next[k]
        face = part if face is None else face + part

    zs = lax.broadcasted_iota(jnp.int32, face.shape, 0)
    ls = lax.broadcasted_iota(jnp.int32, face.shape, 1)
    y = lax.rem(ls, py)
    face = jnp.take_along_axis(
        face, ls - y + lax.rem(y, slab.parts) * 8 + y // slab.parts, axis=1, mode="promise_in_bounds")
    flat = (ls // py) * (depth * py) + zs * py + y
    picks = corners[...]
    for j in range(count):
        total = None
        for i in range(n_in):
            part = coarse[j, i] * values[i]
            total = part if total is None else total + part
        value = jnp.sum(jnp.sum(total, axis=0, keepdims=True), axis=1, keepdims=True)
        face = face + jnp.where(flat == picks[:, j : j + 1], value, 0.0)
    for c in range(comp):
        interface_out[0, c] = face[:, py * c : py * (c + 1)]
    for copy in copies:
        copy.wait()


def params(mib):
    return pltpu.CompilerParams(vmem_limit_bytes=mib * 2**20)


def on_device(body_load, materials, material_tables, corner_index, coarse_inverse):
    comp, depth, py, px = body_load.shape
    kinds = material_tables.shape[0]
    n_in, n_sub = lax.axis_size("in"), lax.axis_size("sub")
    devices = n_in * n_sub
    count = corner_index.shape[0]
    f32 = jnp.float32
    shape = jax.ShapeDtypeStruct
    halo = shape((ITERS * comp + MAT_DEPTH, py, px), f32)

    table = material_tables.transpose(1, 2, 0).reshape(comp * comp, kinds)
    coarse = coarse_inverse.reshape(count, n_sub, n_in, count).transpose(0, 2, 1, 3)

    def hbm(x):
        return pltpu.with_memory_space_constraint(x, pltpu.HBM)

    send_a, send_b, body, mats, table = pl.pallas_call(
        pack_kernel,
        out_shape=(halo, halo, shape(body_load.shape, f32), shape(materials.shape, jnp.int32), shape(table.shape, f32)),
        in_specs=[HBM] * 3,
        out_specs=(VMEM,) * 5,
        scratch_shapes=[
            pltpu.VMEM((2, MAT_DEPTH, py, px), jnp.int32),
            pltpu.SemaphoreType.DMA((2, comp + 1)),
            pltpu.SemaphoreType.DMA((3,)),
        ],
        compiler_params=params(4),
        name="pack",
    )(hbm(body_load), hbm(materials), hbm(table))

    def swaps(start):
        pairs = [(i, i + 1) for i in range(start, n_in - 1, 2)]
        return pairs + [(j, i) for i, j in pairs]

    halo_a = lax.ppermute(send_a, "in", swaps(0))
    halo_b = lax.ppermute(send_b, "in", swaps(1))
    before = lax.ppermute(corner_index, "sub", [(i, (i + 1) % n_sub) for i in range(n_sub)])

    fields = (
        shape((comp, depth + 2 * ITERS, py, px), f32),
        shape((comp, depth + 2 * ITERS - 2, py, px), f32),
        shape((comp, depth + 2 * ITERS - 4, py, px), f32),
        shape((comp * comp, depth + 2 * MAT_DEPTH, py, px), f32),
        shape((depth, comp * py, px), f32),
    )
    *inner, tab = pl.pallas_call(
        interior_kernel,
        out_shape=(*fields, shape((len(PAIRS), 8, px), f32), shape((kinds * comp * comp + 24, px), f32)),
        in_specs=[VMEM] * 3,
        out_specs=(VMEM,) * 7,
        compiler_params=params(4),
        name="interior",
    )(body, mats, table)

    v0, v1, v2, _, packed, message = pl.pallas_call(
        functools.partial(edge_kernel, kinds),
        out_shape=(*fields, shape((devices, LANES), f32)),
        in_specs=[VMEM] * 3 + [HBM] * 2 + [VMEM] * 6,
        out_specs=(VMEM,) * 6,
        input_output_aliases={5: 0, 6: 1, 7: 2, 8: 3, 9: 4},
        scratch_shapes=[
            pltpu.SMEM((count,), jnp.int32),
            pltpu.SMEM((count,), jnp.int32),
            pltpu.SemaphoreType.DMA((2,)),
        ],
        compiler_params=params(4),
        name="edge",
    )(halo_a, halo_b, tab, hbm(corner_index), before, *inner)

    messages = lax.all_to_all(message, ("sub", "in"), 0, 0, tiled=True)
    faces = shape((ITERS + 1, depth, comp * py), f32)
    left, right = pl.pallas_call(
        faces_kernel,
        out_shape=(faces, faces),
        in_specs=[VMEM],
        out_specs=(VMEM, VMEM),
        compiler_params=params(4),
        name="faces",
    )(packed)
    left_next = lax.ppermute(left, "sub", [((i + 1) % n_sub, i) for i in range(n_sub)])

    return pl.pallas_call(
        functools.partial(final_kernel, kinds),
        out_shape=(shape(body_load.shape, f32), shape((1, comp, depth, py), f32)),
        in_specs=[VMEM] * 9,
        out_specs=(HBM, VMEM),
        scratch_shapes=[
            pltpu.VMEM((n_sub, LANES), f32),
            pltpu.VMEM(body_load.shape, f32),
            pltpu.SemaphoreType.DMA((depth,)),
        ],
        compiler_params=params(16),
        name="final",
    )(messages, v0, v1, v2, right, left_next, tab, coarse, corner_index.reshape(1, count))


def solution(mesh):
    return jax.shard_map(
        on_device,
        mesh=mesh,
        in_specs=(
            P(None, "in", None, "sub"),
            P("in", None, "sub"),
            P(),
            P(("sub", "in")),
            P(("sub", "in"), None),
        ),
        out_specs=(P(None, "in", None, "sub"), P("sub", None, "in", None)),
        check_vma=False,
    )
```

```python
import functools

import jax
import jax.numpy as jnp
from jax import lax
from jax.experimental import pallas as pl
from jax.experimental.pallas import tpu as pltpu
from jax.sharding import PartitionSpec as P

ITERS = 3
LANES = 128
MAT_DEPTH = ITERS - 1
PAIRS = [(i, j) for i in range(ITERS) for j in range(i, ITERS + 1)]
GRAM_LANE = 64
VMEM = pl.BlockSpec(memory_space=pltpu.VMEM)
SMEM = pl.BlockSpec(memory_space=pltpu.SMEM)
HBM = pl.BlockSpec(memory_space=pl.ANY)


def spectrum(table, comp):
    kinds = table.shape[1]
    rows = lax.broadcasted_iota(jnp.int32, table.shape, 0)
    diagonal = lax.rem(rows, comp + 1) == 0
    picked = jnp.where(diagonal, table, 0.0)
    mean = jnp.sum(jnp.sum(picked, axis=0, keepdims=True), axis=1, keepdims=True) / (comp * kinds)
    centred = jnp.where(diagonal, table - mean, table)
    size = jnp.abs(centred)
    widest = jnp.zeros((1, kinds), jnp.float32)
    for c in range(comp):
        widest = jnp.maximum(widest, jnp.sum(size[comp * c : comp * (c + 1)], axis=0, keepdims=True))
    scale = 6.0 + jnp.max(widest, axis=1, keepdims=True)
    return mean, scale, centred


def split(index, size):
    if size & (size - 1):
        return lax.div(index, size), lax.rem(index, size)
    return lax.shift_right_logical(index, size.bit_length() - 1), index & (size - 1)


def pack_kernel(body, mats, table, a_out, b_out, body_out, mats_out, table_out, kinds, sems, whole):
    comp, depth = body.shape[0], body.shape[1]
    odd = lax.rem(lax.axis_index("in"), 2)
    copies = []
    for slot, (out, low) in enumerate(((a_out, odd), (b_out, 1 - odd))):
        first = (1 - low) * (depth - MAT_DEPTH)
        copies.append(pltpu.make_async_copy(
            mats.at[pl.ds(first, MAT_DEPTH)], kinds.at[slot], sems.at[slot, comp]))
        first = (1 - low) * (depth - ITERS)
        for c in range(comp):
            copies.append(pltpu.make_async_copy(
                body.at[c, pl.ds(first, ITERS)], out.at[pl.ds(ITERS * c, ITERS)], sems.at[slot, c]))
    copies.append(pltpu.make_async_copy(table, table_out, whole.at[0]))
    copies.append(pltpu.make_async_copy(mats, mats_out, whole.at[1]))
    copies.append(pltpu.make_async_copy(body, body_out, whole.at[2]))
    for copy in copies:
        copy.start()
    for copy in copies:
        copy.wait()
    for slot, out in enumerate((a_out, b_out)):
        out[pl.ds(ITERS * comp, MAT_DEPTH)] = kinds[slot].astype(jnp.float32)


class Slab:
    def __init__(self, comp, py, px):
        self.comp, self.px, self.parts = comp, px, py // 8
        lane = lax.broadcasted_iota(jnp.int32, (8, px), 1)
        row = lax.broadcasted_iota(jnp.int32, (8, px), 0)
        self.lane = lane
        self.first_x, self.last_x = lane == 0, lane == px - 1
        self.first_y, self.last_y = row == 0, row == 7

    def natural(self, ref, *at):
        return [ref[(*at, pl.ds(r, 8, stride=self.parts))] for r in range(self.parts)]

    def load(self, ref, *at):
        return [ref[(*at, pl.ds(8 * r, 8))] for r in range(self.parts)]

    def store(self, ref, values, *at):
        for r in range(self.parts):
            ref[(*at, pl.ds(8 * r, 8))] = values[r]

    def neighbours(self, below, above, value):
        parts, px = self.parts, self.px
        totals = []
        for r in range(parts):
            total = below[r] + above[r]
            total += jnp.where(self.first_x, 0.0, pltpu.roll(value[r], 1, 1))
            total += jnp.where(self.last_x, 0.0, pltpu.roll(value[r], px - 1, 1))
            total += value[r - 1] if r else jnp.where(self.first_y, 0.0, pltpu.roll(value[parts - 1], 1, 0))
            total += value[r + 1] if r + 1 < parts else jnp.where(self.last_y, 0.0, pltpu.roll(value[0], 7, 0))
            totals.append(total)
        return totals

    def applied(self, source, at, gains, gains_at, inverse, alive=None):
        comp, parts = self.comp, self.parts
        values = [self.load(source, c, at) for c in range(comp)]
        for c in range(comp):
            around = self.neighbours(self.load(source, c, at - 1), self.load(source, c, at + 1), values[c])
            out = []
            for r in range(parts):
                total = None
                for d in range(comp):
                    term = gains[comp * c + d, gains_at, pl.ds(8 * r, 8)] * values[d][r]
                    total = term if total is None else total + term
                total = total - inverse * around[r]
                out.append(total if alive is None else alive * total)
            yield c, values[c], out

    def products(self, total, left, right):
        for r in range(self.parts):
            total = total + left[r] * right[r]
        return total

    def look_up(self, kinds, tab, gains, at, count):
        bits = [[(kind & (1 << b)) != 0 for kind in kinds] for b in range((count - 1).bit_length())]
        entries = self.comp * self.comp
        for e in range(entries):
            lines = [tab[pl.ds(k * entries + e, 8, stride=0)] for k in range(count)]
            out = []
            for r in range(self.parts):
                level = lines
                for bit in bits:
                    level = [
                        jnp.where(bit[r], level[k + 1], level[k]) if k + 1 < len(level) else level[k]
                        for k in range(0, len(level), 2)
                    ]
                out.append(level[0])
            self.store(gains, out, e, at)

    def pack(self, packed, z, c, basis):
        rows = self.parts * 8
        for r in range(self.parts):
            block = basis[0][r]
            for k in range(1, len(basis)):
                here = (self.lane == 2 * k) | (self.lane == 2 * k - 1)
                block = jnp.where(here, pltpu.roll(basis[k][r], 2 * k, 1), block)
            packed[z, pl.ds(rows * c + 8 * r, 8)] = block


def levels(slab, v0, v1, v2, gains, packed, inverse):
    def first(z, sums):
        g01, g11 = sums
        for c, v, w in slab.applied(v0, z + 3, gains, z + 2, inverse):
            slab.store(v1, w, c, z + 2)
            g01, g11 = slab.products(g01, v, w), slab.products(g11, w, w)
        return g01, g11

    def second(z, sums):
        g02, g12, g22 = sums
        for c, v, w in slab.applied(v1, z + 2, gains, z + 2, inverse):
            slab.store(v2, w, c, z + 1)
            u = slab.load(v0, c, z + 3)
            g02, g12, g22 = slab.products(g02, u, w), slab.products(g12, v, w), slab.products(g22, w, w)
        return g02, g12, g22

    def third(z, sums):
        g03, g13, g23 = sums
        for c, v, w in slab.applied(v2, z + 1, gains, z + 2, inverse):
            t, u = slab.load(v0, c, z + 3), slab.load(v1, c, z + 2)
            slab.pack(packed, z, c, (t, u, v, w))
            g03, g13, g23 = slab.products(g03, t, w), slab.products(g13, u, w), slab.products(g23, v, w)
        return g03, g13, g23

    return first, second, third


def interior_kernel(body, mats, table, v0, v1, v2, gains, packed, gram, tab, v3):
    comp, depth, py, px = body.shape
    kinds = table.shape[1]
    entries = comp * comp
    slab = Slab(comp, py, px)
    mean, scale, centred = spectrum(table[...], comp)
    inverse = jnp.broadcast_to(1.0 / scale, (8, px))
    scaled = centred / scale
    for k in range(kinds):
        tab[pl.ds(k * entries, entries)] = jnp.broadcast_to(scaled[:, k : k + 1], (entries, px))
    for t, value in enumerate((inverse, mean, scale)):
        tab[pl.ds(kinds * entries + 8 * t, 8)] = jnp.broadcast_to(value, (8, px))
    zero = jnp.zeros((8, px), jnp.float32)
    for c in range(comp):
        for at in (ITERS - 1, ITERS + depth):
            slab.store(v0, [zero] * slab.parts, c, at)

    def own(z, g00):
        for c in range(comp):
            value = slab.natural(body, c, z)
            slab.store(v0, value, c, ITERS + z)
            g00 = slab.products(g00, value, value)
        slab.look_up(slab.natural(mats, z), tab, gains, MAT_DEPTH + z, kinds)
        return g00
    g00 = lax.fori_loop(0, depth, own, zero)

    def partial(i, carry):
        z = i * (depth - 1)
        for c, _, w in slab.applied(v0, z + 3, gains, z + 2, inverse):
            slab.store(v1, w, c, z + 2)
        return carry

    def partial_second(i, carry):
        z = 1 + i * (depth - 3)
        for c, _, w in slab.applied(v1, z + 2, gains, z + 2, inverse):
            slab.store(v2, w, c, z + 1)
        return carry

    def partial_third(i, carry):
        z = 2 + i * (depth - 5)
        for c, _, w in slab.applied(v2, z + 1, gains, z + 2, inverse):
            slab.store(v3, w, c, i)
        return carry

    first, second, third = levels(slab, v0, v1, v2, gains, packed, inverse)
    lax.fori_loop(0, 2, partial, 0)
    g01, g11 = lax.fori_loop(1, depth - 1, first, (zero,) * 2)
    lax.fori_loop(0, 2, partial_second, 0)
    g02, g12, g22 = lax.fori_loop(2, depth - 2, second, (zero,) * 3)
    lax.fori_loop(0, 2, partial_third, 0)
    g03, g13, g23 = lax.fori_loop(3, depth - 3, third, (zero,) * 3)
    for g, value in enumerate((g00, g01, g02, g03, g11, g12, g13, g22, g23)):
        gram[g] = value


def one_side(kinds, slot, halo, tab, v3, gram, v0, v1, v2, gains, packed):
    comp, py, px = v0.shape[0], v0.shape[2], v0.shape[3]
    depth = packed.shape[0]
    slab = Slab(comp, py, px)
    place = lax.axis_index("in")
    low = lax.rem(place + 1 + slot, 2) == 0
    alive = jnp.where(low, place > 0, place < lax.axis_size("in") - 1).astype(jnp.float32)
    inverse = tab[pl.ds(kinds * comp * comp, 8)]

    def layer(q):
        return jnp.where(low, q, depth - 1 - q)

    base = jnp.where(low, 0, ITERS + depth)
    for t in range(ITERS):
        for c in range(comp):
            slab.store(v0, slab.natural(halo, ITERS * c + t), c, base + t)

    base_gains = jnp.where(low, 0, MAT_DEPTH + depth)

    def halo_gains(t, carry):
        kind = [x.astype(jnp.int32) for x in slab.natural(halo, ITERS * comp + t)]
        slab.look_up(kind, tab, gains, base_gains + t, kinds)
        return carry
    lax.fori_loop(0, MAT_DEPTH, halo_gains, 0)

    g00, g01, g02, g03, g11, g12, g13, g22, g23 = [gram[g] for g in range(len(PAIRS))]
    first, second, third = levels(slab, v0, v1, v2, gains, packed, inverse)

    def first_halo(i, carry):
        z = layer(i - 2)
        for c, _, w in slab.applied(v0, z + 3, gains, z + 2, inverse, alive):
            slab.store(v1, w, c, z + 2)
        return carry
    lax.fori_loop(0, 2, first_halo, 0)

    z0, z1, z2, out = layer(0), layer(1), layer(2), layer(-1)
    side = jnp.where(low, 0, 1)

    def mend(c, sums):
        g01, g11, g02, g12, g22, g03, g13, g23 = sums
        term = [inverse * x for x in slab.load(v0, c, out + 3)]
        w = [a - b for a, b in zip(slab.load(v1, c, z0 + 2), term)]
        slab.store(v1, w, c, z0 + 2)
        g01, g11 = slab.products(g01, slab.load(v0, c, z0 + 3), w), slab.products(g11, w, w)
        term = [inverse * x for x in term]
        w = [a + b for a, b in zip(slab.load(v2, c, z1 + 1), term)]
        slab.store(v2, w, c, z1 + 1)
        g02 = slab.products(g02, slab.load(v0, c, z1 + 3), w)
        g12 = slab.products(g12, slab.load(v1, c, z1 + 2), w)
        g22 = slab.products(g22, w, w)
        term = [inverse * x for x in term]
        w = [a - b for a, b in zip(slab.load(v3, c, side), term)]
        t, u, v = slab.load(v0, c, z2 + 3), slab.load(v1, c, z2 + 2), slab.load(v2, c, z2 + 1)
        slab.pack(packed, z2, c, (t, u, v, w))
        g03, g13, g23 = slab.products(g03, t, w), slab.products(g13, u, w), slab.products(g23, v, w)
        return g01, g11, g02, g12, g22, g03, g13, g23
    sums = (g01, g11, g02, g12, g22, g03, g13, g23)
    for c in range(comp):
        sums = mend(c, sums)
    g01, g11, g02, g12, g22, g03, g13, g23 = sums

    for c, _, w in slab.applied(v1, out + 2, gains, out + 2, inverse, alive):
        slab.store(v2, w, c, out + 1)
    g02, g12, g22 = second(z0, (g02, g12, g22))
    g03, g13, g23 = lax.fori_loop(0, 2, lambda i, sums: third(layer(i), sums), (g03, g13, g23))
    return g00, g01, g02, g03, g11, g12, g13, g22, g23


def near_kernel(kinds, halo, tab, v3, v0_in, v1_in, v2_in, gains_in, packed_in, gram_in,
                v0, v1, v2, gains, packed, gram):
    sums = one_side(kinds, 0, halo, tab, v3, gram_in, v0, v1, v2, gains, packed)
    for g, value in enumerate(sums):
        gram[g] = value


def far_kernel(kinds, halo, tab, v3, corners_hbm, before_hbm, v0_in, v1_in, v2_in, gains_in, packed_in, gram_in,
               v0, v1, v2, gains, packed, message, corners, before, sems):
    fetch = (
        pltpu.make_async_copy(corners_hbm, corners, sems.at[0]),
        pltpu.make_async_copy(before_hbm, before, sems.at[1]),
    )
    for copy in fetch:
        copy.start()
    py, px = v0.shape[2], v0.shape[3]
    depth, parts = packed.shape[0], py // 8
    sums = one_side(kinds, 1, halo, tab, v3, gram_in, v0, v1, v2, gains, packed)

    spots = lax.broadcasted_iota(jnp.int32, (1, px), 1)
    line = jnp.zeros((1, px), jnp.float32)
    even = lax.rem(spots, 2) == 0
    for g, value in enumerate(sums):
        total = jnp.sum(jnp.sum(value, axis=0, keepdims=True), axis=1, keepdims=True)
        line = jnp.where(spots == GRAM_LANE + g, total, line)

    for copy in fetch:
        copy.wait()

    def corner_row(index):
        c, rest = split(index, depth * py)
        z, y = split(rest, py)
        t, r = split(y, parts)
        return packed[z, pl.ds(c * py + r * 8 + t, 1)]

    for j in range(corners.shape[0]):
        mine = corner_row(corners[j])
        other = corner_row(before[j])
        moved = pltpu.roll(jnp.where(even, other, mine), 8 * j + 1, 1)
        line = jnp.where(spots // 8 == j, moved, line)
    message[...] = jnp.broadcast_to(line, message.shape)


def faces_kernel(packed, left, right):
    depth, _, px = packed.shape
    for z in range(depth):
        turned = packed[z].T
        for k in range(ITERS + 1):
            at = (2 * k - 1) % px
            left[k, pl.ds(z, 1)] = turned[2 * k : 2 * k + 1]
            right[k, pl.ds(z, 1)] = turned[at : at + 1]


def total_of(terms):
    while len(terms) > 1:
        terms = [sum(terms[k : k + 2][1:], terms[k]) for k in range(0, len(terms), 2)]
    return terms[0]


def coefficients(gram, centre, scale):
    norms, images = {}, {}
    for i in range(ITERS):
        for j in range(i, ITERS):
            forward = centre * gram[(i, j)] + scale * gram[(i, j + 1)]
            if i == j:
                norms[(i, j)], images[(i, j)] = gram[(i, j)], forward
            else:
                back = centre * gram[(i, j)] + scale * gram[(i + 1, j)]
                norms[(i, j)], images[(i, j)] = 2.0 * gram[(i, j)], forward + back

    def quadratic(form, u):
        size = len(u)
        return total_of([(u[i] * u[j]) * form[(i, j)] for i in range(size) for j in range(i, size)])

    one = jnp.ones_like(centre)
    residual, direction, found = [one], [one], []
    norm = gram[(0, 0)]
    for repeat in range(ITERS):
        size = len(direction)
        step = norm / (quadratic(images, direction) if repeat else images[(0, 0)])
        image = [centre * direction[0]]
        for j in range(1, size):
            image.append(centre * direction[j] + scale * direction[j - 1])
        image.append(scale * direction[size - 1])
        found = [
            (found[j] if j < len(found) else 0.0) + step * direction[j] for j in range(size)
        ]
        residual = [
            (residual[j] if j < size else 0.0) - step * image[j] for j in range(size + 1)
        ]
        if repeat + 1 < ITERS:
            inverse = 1.0 / norm
            norm = quadratic(norms, residual)
            ratio = norm * inverse
            direction = [
                residual[j] + (ratio * direction[j] if j < size else 0.0) for j in range(size + 1)
            ]
    return found, residual


def final_kernel(kinds, messages, v0, v1, v2, right, left_next, tab, coarse, corners,
                 solution_hbm, interface_hbm, book, solution_out, interface_out, sems):
    comp, py, px = v0.shape[0], v0.shape[2], v0.shape[3]
    depth = right.shape[1]
    n_in, n_sub = lax.axis_size("in"), lax.axis_size("sub")
    sub = lax.axis_index("sub")
    following = lax.rem(sub + 1, n_sub)
    slab = Slab(comp, py, px)
    base = kinds * comp * comp

    got = [messages[pl.ds(i, n_sub, stride=n_in)] for i in range(n_in)]
    summed = total_of(got)
    mean = jnp.broadcast_to(tab[pl.ds(base + 8, 1)], summed.shape)
    scale = jnp.broadcast_to(tab[pl.ds(base + 16, 1)], summed.shape)
    gram = {}
    for g, pair in enumerate(PAIRS):
        gram[pair] = jnp.broadcast_to(summed[:, GRAM_LANE + g : GRAM_LANE + g + 1], summed.shape)
    found, residual = coefficients(gram, 6.0 + mean, scale)

    for k, value in enumerate(residual + found):
        book[k] = value
    weights = [book[ITERS + 1 + k, pl.ds(sub, 8, stride=0)] for k in range(ITERS)]
    mine = [book[k, pl.ds(sub, depth, stride=0)] for k in range(ITERS + 1)]
    other = [book[k, pl.ds(following, depth, stride=0)] for k in range(ITERS + 1)]

    copies = [
        pltpu.make_async_copy(solution_out.at[:, z], solution_hbm.at[:, z], sems.at[z]) for z in range(depth)
    ]
    for z in range(depth):
        for c in range(comp):
            fields = slab.load(v0, c, z + 3), slab.load(v1, c, z + 2), slab.load(v2, c, z + 1)
            for r in range(slab.parts):
                total = weights[0] * fields[0][r] + weights[1] * fields[1][r] + weights[2] * fields[2][r]
                solution_out[c, z, pl.ds(r, 8, stride=slab.parts)] = total
        copies[z].start()

    lane = lax.broadcasted_iota(jnp.int32, summed.shape, 1)
    kind = lax.rem(lane, 8) // 2
    spread = residual[0]
    for k in range(1, ITERS + 1):
        spread = jnp.where(kind == k, residual[k], spread)
    count = corners.shape[1]
    spots = jnp.minimum(lane * 8, px - 1)
    values = []
    for i in range(n_in):
        product = got[i] * spread
        product = jnp.where(lax.rem(lane, 2) == 0, product, pltpu.roll(product, n_sub - 1, 0))
        for reach in (1, 2, 4):
            product = product + pltpu.roll(product, px - reach, 1)
        values.append(jnp.take_along_axis(product, spots, axis=1, mode="promise_in_bounds")[:, :count])

    face = None
    for k in range(ITERS + 1):
        part = mine[k] * right[k] + other[k] * left_next[k]
        face = part if face is None else face + part

    zs = lax.broadcasted_iota(jnp.int32, face.shape, 0)
    ls = lax.broadcasted_iota(jnp.int32, face.shape, 1)
    y = lax.rem(ls, py)
    face = jnp.take_along_axis(
        face, ls - y + lax.rem(y, slab.parts) * 8 + y // slab.parts, axis=1, mode="promise_in_bounds")
    flat = (ls // py) * (depth * py) + zs * py + y
    picks = corners[...]
    for j in range(count):
        total = None
        for i in range(n_in):
            part = coarse[j, i] * values[i]
            total = part if total is None else total + part
        value = jnp.sum(jnp.sum(total, axis=0, keepdims=True), axis=1, keepdims=True)
        face = face + jnp.where(flat == picks[:, j : j + 1], value, 0.0)
    for c in range(comp):
        interface_out[0, c] = face[:, py * c : py * (c + 1)]
    copies.append(pltpu.make_async_copy(interface_out, interface_hbm, sems.at[depth]))
    copies[depth].start()
    for copy in copies:
        copy.wait()


def params(mib):
    return pltpu.CompilerParams(vmem_limit_bytes=mib * 2**20)


def on_device(body_load, materials, material_tables, corner_index, coarse_inverse):
    comp, depth, py, px = body_load.shape
    kinds = material_tables.shape[0]
    n_in, n_sub = lax.axis_size("in"), lax.axis_size("sub")
    devices = n_in * n_sub
    count = corner_index.shape[0]
    f32 = jnp.float32
    shape = jax.ShapeDtypeStruct
    halo = shape((ITERS * comp + MAT_DEPTH, py, px), f32)

    table = material_tables.transpose(1, 2, 0).reshape(comp * comp, kinds)
    coarse = coarse_inverse.reshape(count, n_sub, n_in, count).transpose(0, 2, 1, 3)

    def hbm(x):
        return pltpu.with_memory_space_constraint(x, pltpu.HBM)

    send_a, send_b, body, mats, table = pl.pallas_call(
        pack_kernel,
        out_shape=(halo, halo, shape(body_load.shape, f32), shape(materials.shape, jnp.int32), shape(table.shape, f32)),
        in_specs=[HBM] * 3,
        out_specs=(VMEM,) * 5,
        scratch_shapes=[
            pltpu.VMEM((2, MAT_DEPTH, py, px), jnp.int32),
            pltpu.SemaphoreType.DMA((2, comp + 1)),
            pltpu.SemaphoreType.DMA((3,)),
        ],
        compiler_params=params(4),
        name="pack",
    )(hbm(body_load), hbm(materials), hbm(table))

    def swaps(start):
        pairs = [(i, i + 1) for i in range(start, n_in - 1, 2)]
        return pairs + [(j, i) for i, j in pairs]

    halo_a = lax.ppermute(send_a, "in", swaps(0))
    halo_b = lax.ppermute(send_b, "in", swaps(1))
    before = lax.ppermute(corner_index, "sub", [(i, (i + 1) % n_sub) for i in range(n_sub)])

    fields = (
        shape((comp, depth + 2 * ITERS, py, px), f32),
        shape((comp, depth + 2 * ITERS - 2, py, px), f32),
        shape((comp, depth + 2 * ITERS - 4, py, px), f32),
        shape((comp * comp, depth + 2 * MAT_DEPTH, py, px), f32),
        shape((depth, comp * py, px), f32),
    )
    fields += (shape((len(PAIRS), 8, px), f32),)
    *inner, tab, v3 = pl.pallas_call(
        interior_kernel,
        out_shape=(
            *fields, shape((kinds * comp * comp + 24, px), f32), shape((comp, 2, py, px), f32)),
        in_specs=[VMEM] * 3,
        out_specs=(VMEM,) * 8,
        compiler_params=params(4),
        name="interior",
    )(body, mats, table)

    inner = pl.pallas_call(
        functools.partial(near_kernel, kinds),
        out_shape=fields,
        in_specs=[VMEM] * 9,
        out_specs=(VMEM,) * 6,
        input_output_aliases={3 + k: k for k in range(6)},
        compiler_params=params(4),
        name="near",
    )(halo_a, tab, v3, *inner)

    v0, v1, v2, _, packed, message = pl.pallas_call(
        functools.partial(far_kernel, kinds),
        out_shape=(*fields[:5], shape((devices, LANES), f32)),
        in_specs=[VMEM] * 3 + [HBM] * 2 + [VMEM] * 6,
        out_specs=(VMEM,) * 6,
        input_output_aliases={5 + k: k for k in range(5)},
        scratch_shapes=[
            pltpu.SMEM((count,), jnp.int32),
            pltpu.SMEM((count,), jnp.int32),
            pltpu.SemaphoreType.DMA((2,)),
        ],
        compiler_params=params(4),
        name="far",
    )(halo_b, tab, v3, hbm(corner_index), before, *inner)

    messages = lax.all_to_all(message, ("sub", "in"), 0, 0, tiled=True)
    faces = shape((ITERS + 1, depth, comp * py), f32)
    left, right = pl.pallas_call(
        faces_kernel,
        out_shape=(faces, faces),
        in_specs=[VMEM],
        out_specs=(VMEM, VMEM),
        compiler_params=params(4),
        name="faces",
    )(packed)
    left_next = lax.ppermute(left, "sub", [((i + 1) % n_sub, i) for i in range(n_sub)])

    return pl.pallas_call(
        functools.partial(final_kernel, kinds),
        out_shape=(shape(body_load.shape, f32), shape((1, comp, depth, py), f32)),
        in_specs=[VMEM] * 9,
        out_specs=(HBM, HBM),
        scratch_shapes=[
            pltpu.VMEM((2 * ITERS + 1, n_sub, LANES), f32),
            pltpu.VMEM(body_load.shape, f32),
            pltpu.VMEM((1, comp, depth, py), f32),
            pltpu.SemaphoreType.DMA((depth + 1,)),
        ],
        compiler_params=params(16),
        name="final",
    )(messages, v0, v1, v2, right, left_next, tab, coarse, corner_index.reshape(1, count))


def solution(mesh):
    return jax.shard_map(
        on_device,
        mesh=mesh,
        in_specs=(
            P(None, "in", None, "sub"),
            P("in", None, "sub"),
            P(),
            P(("sub", "in")),
            P(("sub", "in"), None),
        ),
        out_specs=(P(None, "in", None, "sub"), P("sub", None, "in", None)),
        check_vma=False,
    )
```

```python
import functools

import jax
import jax.numpy as jnp
from jax import lax
from jax.experimental import pallas as pl
from jax.experimental.pallas import tpu as pltpu
from jax.sharding import PartitionSpec as P

ITERS = 3
LANES = 128
MAT_DEPTH = ITERS - 1
PAIRS = [(i, j) for i in range(ITERS) for j in range(i, ITERS + 1)]
GRAM_LANE = 64
VMEM = pl.BlockSpec(memory_space=pltpu.VMEM)
SMEM = pl.BlockSpec(memory_space=pltpu.SMEM)
HBM = pl.BlockSpec(memory_space=pl.ANY)


def spectrum(table, comp):
    kinds = table.shape[1]
    rows = lax.broadcasted_iota(jnp.int32, table.shape, 0)
    diagonal = lax.rem(rows, comp + 1) == 0
    picked = jnp.where(diagonal, table, 0.0)
    mean = jnp.sum(jnp.sum(picked, axis=0, keepdims=True), axis=1, keepdims=True) / (comp * kinds)
    centred = jnp.where(diagonal, table - mean, table)
    size = jnp.abs(centred)
    widest = jnp.zeros((1, kinds), jnp.float32)
    for c in range(comp):
        widest = jnp.maximum(widest, jnp.sum(size[comp * c : comp * (c + 1)], axis=0, keepdims=True))
    scale = 6.0 + jnp.max(widest, axis=1, keepdims=True)
    return mean, scale, centred


def split(index, size):
    if size & (size - 1):
        return lax.div(index, size), lax.rem(index, size)
    return lax.shift_right_logical(index, size.bit_length() - 1), index & (size - 1)


def pack_kernel(body, mats, table, a_out, b_out, middle_out, mats_out, table_out, sems, rest):
    comp, depth = body.shape[0], body.shape[1]
    odd = lax.rem(lax.axis_index("in"), 2)
    sides = ((a_out, odd), (b_out, 1 - odd))
    copies = []
    for slot, (out, low) in enumerate(sides):
        first = (1 - low) * (depth - ITERS)
        for c in range(comp):
            copies.append(pltpu.make_async_copy(
                body.at[c, pl.ds(first, ITERS)], out.at[pl.ds(ITERS * c, ITERS)], sems.at[slot, c]))
    copies.append(pltpu.make_async_copy(mats, mats_out, rest.at[0]))
    copies.append(pltpu.make_async_copy(body.at[:, pl.ds(ITERS, depth - 2 * ITERS)], middle_out, rest.at[1]))
    copies.append(pltpu.make_async_copy(table, table_out, rest.at[2]))
    for copy in copies:
        copy.start()
    for copy in copies:
        copy.wait()
    for out, low in sides:
        first = (1 - low) * (depth - MAT_DEPTH)
        for t in range(MAT_DEPTH):
            out[ITERS * comp + t] = mats_out[first + t].astype(jnp.float32)


class Slab:
    def __init__(self, comp, py, px):
        self.comp, self.px, self.parts = comp, px, py // 8
        lane = lax.broadcasted_iota(jnp.int32, (8, px), 1)
        row = lax.broadcasted_iota(jnp.int32, (8, px), 0)
        self.lane = lane
        self.first_x, self.last_x = lane == 0, lane == px - 1
        self.first_y, self.last_y = row == 0, row == 7

    def natural(self, ref, *at):
        return [ref[(*at, pl.ds(r, 8, stride=self.parts))] for r in range(self.parts)]

    def load(self, ref, *at):
        return [ref[(*at, pl.ds(8 * r, 8))] for r in range(self.parts)]

    def store(self, ref, values, *at):
        for r in range(self.parts):
            ref[(*at, pl.ds(8 * r, 8))] = values[r]

    def neighbours(self, below, above, value):
        parts, px = self.parts, self.px
        totals = []
        for r in range(parts):
            total = below[r] + above[r]
            total += jnp.where(self.first_x, 0.0, pltpu.roll(value[r], 1, 1))
            total += jnp.where(self.last_x, 0.0, pltpu.roll(value[r], px - 1, 1))
            total += value[r - 1] if r else jnp.where(self.first_y, 0.0, pltpu.roll(value[parts - 1], 1, 0))
            total += value[r + 1] if r + 1 < parts else jnp.where(self.last_y, 0.0, pltpu.roll(value[0], 7, 0))
            totals.append(total)
        return totals

    def applied(self, source, at, gains, gains_at, inverse, alive=None):
        comp, parts = self.comp, self.parts
        values = [self.load(source, c, at) for c in range(comp)]
        for c in range(comp):
            around = self.neighbours(self.load(source, c, at - 1), self.load(source, c, at + 1), values[c])
            out = []
            for r in range(parts):
                total = None
                for d in range(comp):
                    term = gains[comp * c + d, gains_at, pl.ds(8 * r, 8)] * values[d][r]
                    total = term if total is None else total + term
                total = total - inverse * around[r]
                out.append(total if alive is None else alive * total)
            yield c, values[c], out

    def products(self, total, left, right):
        for r in range(self.parts):
            total = total + left[r] * right[r]
        return total

    def look_up(self, kinds, tab, gains, at, count):
        bits = [[(kind & (1 << b)) != 0 for kind in kinds] for b in range((count - 1).bit_length())]
        entries = self.comp * self.comp
        for e in range(entries):
            lines = [tab[pl.ds(k * entries + e, 8, stride=0)] for k in range(count)]
            out = []
            for r in range(self.parts):
                level = lines
                for bit in bits:
                    level = [
                        jnp.where(bit[r], level[k + 1], level[k]) if k + 1 < len(level) else level[k]
                        for k in range(0, len(level), 2)
                    ]
                out.append(level[0])
            self.store(gains, out, e, at)


def levels(slab, v0, v1, v2, v3, gains, inverse):
    def first(z, sums):
        g01, g11 = sums
        for c, v, w in slab.applied(v0, z + 3, gains, z + 2, inverse):
            slab.store(v1, w, c, z + 2)
            g01, g11 = slab.products(g01, v, w), slab.products(g11, w, w)
        return g01, g11

    def second(z, sums):
        g02, g12, g22 = sums
        for c, v, w in slab.applied(v1, z + 2, gains, z + 2, inverse):
            slab.store(v2, w, c, z + 1)
            u = slab.load(v0, c, z + 3)
            g02, g12, g22 = slab.products(g02, u, w), slab.products(g12, v, w), slab.products(g22, w, w)
        return g02, g12, g22

    def third(z, sums):
        g03, g13, g23 = sums
        for c, v, w in slab.applied(v2, z + 1, gains, z + 2, inverse):
            t, u = slab.load(v0, c, z + 3), slab.load(v1, c, z + 2)
            slab.store(v3, w, c, z)
            g03, g13, g23 = slab.products(g03, t, w), slab.products(g13, u, w), slab.products(g23, v, w)
        return g03, g13, g23

    return first, second, third


def interior_kernel(side_a, side_b, middle, mats, table, v0, v1, v2, v3, gains, gram, tab):
    comp, _, py, px = middle.shape
    depth = mats.shape[0]
    odd = lax.rem(lax.axis_index("in"), 2) == 1
    kinds = table.shape[1]
    entries = comp * comp
    slab = Slab(comp, py, px)
    mean, scale, centred = spectrum(table[...], comp)
    inverse = jnp.broadcast_to(1.0 / scale, (8, px))
    scaled = centred / scale
    for k in range(kinds):
        tab[pl.ds(k * entries, entries)] = jnp.broadcast_to(scaled[:, k : k + 1], (entries, px))
    for t, value in enumerate((inverse, mean, scale)):
        tab[pl.ds(kinds * entries + 8 * t, 8)] = jnp.broadcast_to(value, (8, px))
    zero = jnp.zeros((8, px), jnp.float32)
    for c in range(comp):
        for at in (ITERS - 1, ITERS + depth):
            slab.store(v0, [zero] * slab.parts, c, at)

    def place(values, z, g00):
        for c in range(comp):
            slab.store(v0, values[c], c, ITERS + z)
            g00 = slab.products(g00, values[c], values[c])
        slab.look_up(slab.natural(mats, z), tab, gains, MAT_DEPTH + z, kinds)
        return g00

    def outer(t, g00):
        a = [slab.natural(side_a, ITERS * c + t) for c in range(comp)]
        b = [slab.natural(side_b, ITERS * c + t) for c in range(comp)]
        low = [[jnp.where(odd, x, y) for x, y in zip(a[c], b[c])] for c in range(comp)]
        g00 = place(low, t, g00)
        high = [[jnp.where(odd, y, x) for x, y in zip(a[c], b[c])] for c in range(comp)]
        return place(high, depth - ITERS + t, g00)

    def centre(m, g00):
        return place([slab.natural(middle, c, m) for c in range(comp)], ITERS + m, g00)
    g00 = lax.fori_loop(0, ITERS, outer, zero)
    g00 = lax.fori_loop(0, depth - 2 * ITERS, centre, g00)

    def partial(i, carry):
        z = i * (depth - 1)
        for c, _, w in slab.applied(v0, z + 3, gains, z + 2, inverse):
            slab.store(v1, w, c, z + 2)
        return carry

    def partial_second(i, carry):
        z = 1 + i * (depth - 3)
        for c, _, w in slab.applied(v1, z + 2, gains, z + 2, inverse):
            slab.store(v2, w, c, z + 1)
        return carry

    def partial_third(i, carry):
        z = 2 + i * (depth - 5)
        for c, _, w in slab.applied(v2, z + 1, gains, z + 2, inverse):
            slab.store(v3, w, c, z)
        return carry

    first, second, third = levels(slab, v0, v1, v2, v3, gains, inverse)
    lax.fori_loop(0, 2, partial, 0)
    g01, g11 = lax.fori_loop(1, depth - 1, first, (zero,) * 2)
    lax.fori_loop(0, 2, partial_second, 0)
    g02, g12, g22 = lax.fori_loop(2, depth - 2, second, (zero,) * 3)
    lax.fori_loop(0, 2, partial_third, 0)
    g03, g13, g23 = lax.fori_loop(3, depth - 3, third, (zero,) * 3)
    for g, value in enumerate((g00, g01, g02, g03, g11, g12, g13, g22, g23)):
        gram[g] = value


def one_side(kinds, slot, halo, tab, gram, v0, v1, v2, v3, gains):
    comp, py, px = v0.shape[0], v0.shape[2], v0.shape[3]
    depth = v3.shape[1]
    slab = Slab(comp, py, px)
    place = lax.axis_index("in")
    low = lax.rem(place + 1 + slot, 2) == 0
    alive = jnp.where(low, place > 0, place < lax.axis_size("in") - 1).astype(jnp.float32)
    inverse = tab[pl.ds(kinds * comp * comp, 8)]

    def layer(q):
        return jnp.where(low, q, depth - 1 - q)

    base = jnp.where(low, 0, ITERS + depth)
    for t in range(ITERS):
        for c in range(comp):
            slab.store(v0, slab.natural(halo, ITERS * c + t), c, base + t)

    base_gains = jnp.where(low, 0, MAT_DEPTH + depth)

    def halo_gains(t, carry):
        kind = [x.astype(jnp.int32) for x in slab.natural(halo, ITERS * comp + t)]
        slab.look_up(kind, tab, gains, base_gains + t, kinds)
        return carry
    lax.fori_loop(0, MAT_DEPTH, halo_gains, 0)

    g00, g01, g02, g03, g11, g12, g13, g22, g23 = [gram[g] for g in range(len(PAIRS))]
    first, second, third = levels(slab, v0, v1, v2, v3, gains, inverse)

    def first_halo(i, carry):
        z = layer(i - 2)
        for c, _, w in slab.applied(v0, z + 3, gains, z + 2, inverse, alive):
            slab.store(v1, w, c, z + 2)
        return carry
    lax.fori_loop(0, 2, first_halo, 0)

    z0, z1, z2, out = layer(0), layer(1), layer(2), layer(-1)

    def mend(c, sums):
        g01, g11, g02, g12, g22, g03, g13, g23 = sums
        term = [inverse * x for x in slab.load(v0, c, out + 3)]
        w = [a - b for a, b in zip(slab.load(v1, c, z0 + 2), term)]
        slab.store(v1, w, c, z0 + 2)
        g01, g11 = slab.products(g01, slab.load(v0, c, z0 + 3), w), slab.products(g11, w, w)
        term = [inverse * x for x in term]
        w = [a + b for a, b in zip(slab.load(v2, c, z1 + 1), term)]
        slab.store(v2, w, c, z1 + 1)
        g02 = slab.products(g02, slab.load(v0, c, z1 + 3), w)
        g12 = slab.products(g12, slab.load(v1, c, z1 + 2), w)
        g22 = slab.products(g22, w, w)
        term = [inverse * x for x in term]
        w = [a - b for a, b in zip(slab.load(v3, c, z2), term)]
        slab.store(v3, w, c, z2)
        t, u, v = slab.load(v0, c, z2 + 3), slab.load(v1, c, z2 + 2), slab.load(v2, c, z2 + 1)
        g03, g13, g23 = slab.products(g03, t, w), slab.products(g13, u, w), slab.products(g23, v, w)
        return g01, g11, g02, g12, g22, g03, g13, g23
    sums = (g01, g11, g02, g12, g22, g03, g13, g23)
    for c in range(comp):
        sums = mend(c, sums)
    g01, g11, g02, g12, g22, g03, g13, g23 = sums

    for c, _, w in slab.applied(v1, out + 2, gains, out + 2, inverse, alive):
        slab.store(v2, w, c, out + 1)
    g02, g12, g22 = second(z0, (g02, g12, g22))
    g03, g13, g23 = lax.fori_loop(0, 2, lambda i, sums: third(layer(i), sums), (g03, g13, g23))
    return g00, g01, g02, g03, g11, g12, g13, g22, g23


def near_kernel(kinds, halo, tab, v0_in, v1_in, v2_in, v3_in, gains_in, gram_in, v0, v1, v2, v3, gains, gram):
    sums = one_side(kinds, 0, halo, tab, gram_in, v0, v1, v2, v3, gains)
    for g, value in enumerate(sums):
        gram[g] = value


def far_kernel(kinds, halo, tab, corners_hbm, before_hbm, v0_in, v1_in, v2_in, v3_in, gains_in, gram_in,
               v0, v1, v2, v3, gains, message, corners, before, sems):
    fetch = (
        pltpu.make_async_copy(corners_hbm, corners, sems.at[0]),
        pltpu.make_async_copy(before_hbm, before, sems.at[1]),
    )
    for copy in fetch:
        copy.start()
    py, px = v0.shape[2], v0.shape[3]
    depth, parts = v3.shape[1], py // 8
    sums = one_side(kinds, 1, halo, tab, gram_in, v0, v1, v2, v3, gains)

    spots = lax.broadcasted_iota(jnp.int32, (1, px), 1)
    line = jnp.zeros((1, px), jnp.float32)
    for g, value in enumerate(sums):
        total = jnp.sum(jnp.sum(value, axis=0, keepdims=True), axis=1, keepdims=True)
        line = jnp.where(spots == GRAM_LANE + g, total, line)

    for copy in fetch:
        copy.wait()

    def corner_rows(index):
        c, rest = split(index, depth * py)
        z, y = split(rest, py)
        t, r = split(y, parts)
        row = pl.ds(r * 8 + t, 1)
        return [field[c, z + ITERS - k, row] for k, field in enumerate((v0, v1, v2, v3))]

    for j in range(corners.shape[0]):
        rows = zip(corner_rows(corners[j]), corner_rows(before[j]))
        for k, (mine, other) in enumerate(rows):
            moved = pltpu.roll(jnp.where(spots == px - 1, mine, other), 8 * j + 2 * k + 1, 1)
            line = jnp.where(spots // 2 == 4 * j + k, moved, line)
    message[...] = jnp.broadcast_to(line, message.shape)


def faces_kernel(v0, v1, v2, v3, left, right):
    comp, depth, py, px = v3.shape
    for z in range(depth):
        for k, field in enumerate((v0, v1, v2, v3)):
            turned = jnp.concatenate([field[c, z + ITERS - k] for c in range(comp)], axis=0).T
            left[k, pl.ds(z, 1)] = turned[0:1]
            right[k, pl.ds(z, 1)] = turned[px - 1 : px]


def total_of(terms):
    while len(terms) > 1:
        terms = [sum(terms[k : k + 2][1:], terms[k]) for k in range(0, len(terms), 2)]
    return terms[0]


def coefficients(gram, centre, scale):
    norms, images = {}, {}
    for i in range(ITERS):
        for j in range(i, ITERS):
            forward = centre * gram[(i, j)] + scale * gram[(i, j + 1)]
            if i == j:
                norms[(i, j)], images[(i, j)] = gram[(i, j)], forward
            else:
                back = centre * gram[(i, j)] + scale * gram[(i + 1, j)]
                norms[(i, j)], images[(i, j)] = 2.0 * gram[(i, j)], forward + back

    def quadratic(form, u):
        size = len(u)
        return total_of([(u[i] * u[j]) * form[(i, j)] for i in range(size) for j in range(i, size)])

    one = jnp.ones_like(centre)
    residual, direction, found = [one], [one], []
    norm = gram[(0, 0)]
    for repeat in range(ITERS):
        size = len(direction)
        step = norm / (quadratic(images, direction) if repeat else images[(0, 0)])
        image = [centre * direction[0]]
        for j in range(1, size):
            image.append(centre * direction[j] + scale * direction[j - 1])
        image.append(scale * direction[size - 1])
        found = [
            (found[j] if j < len(found) else 0.0) + step * direction[j] for j in range(size)
        ]
        residual = [
            (residual[j] if j < size else 0.0) - step * image[j] for j in range(size + 1)
        ]
        if repeat + 1 < ITERS:
            inverse = 1.0 / norm
            norm = quadratic(norms, residual)
            ratio = norm * inverse
            direction = [
                residual[j] + (ratio * direction[j] if j < size else 0.0) for j in range(size + 1)
            ]
    return found, residual


def final_kernel(kinds, messages, v0, v1, v2, right, left_next, tab, coarse, corners,
                 solution_hbm, interface_hbm, book, solution_out, interface_out, sems):
    comp, py, px = v0.shape[0], v0.shape[2], v0.shape[3]
    depth = right.shape[1]
    n_in, n_sub = lax.axis_size("in"), lax.axis_size("sub")
    sub = lax.axis_index("sub")
    following = lax.rem(sub + 1, n_sub)
    slab = Slab(comp, py, px)
    base = kinds * comp * comp

    got = [messages[pl.ds(i, n_sub, stride=n_in)] for i in range(n_in)]
    summed = total_of(got)
    mean = jnp.broadcast_to(tab[pl.ds(base + 8, 1)], summed.shape)
    scale = jnp.broadcast_to(tab[pl.ds(base + 16, 1)], summed.shape)
    gram = {}
    for g, pair in enumerate(PAIRS):
        gram[pair] = jnp.broadcast_to(summed[:, GRAM_LANE + g : GRAM_LANE + g + 1], summed.shape)
    found, residual = coefficients(gram, 6.0 + mean, scale)

    for k, value in enumerate(residual + found):
        book[k] = value
    weights = [book[ITERS + 1 + k, pl.ds(sub, 8, stride=0)] for k in range(ITERS)]
    mine = [book[k, pl.ds(sub, depth, stride=0)] for k in range(ITERS + 1)]
    other = [book[k, pl.ds(following, depth, stride=0)] for k in range(ITERS + 1)]

    copies = [
        pltpu.make_async_copy(solution_out.at[:, z], solution_hbm.at[:, z], sems.at[z]) for z in range(depth)
    ]
    for z in range(depth):
        for c in range(comp):
            fields = slab.load(v0, c, z + 3), slab.load(v1, c, z + 2), slab.load(v2, c, z + 1)
            for r in range(slab.parts):
                total = weights[0] * fields[0][r] + weights[1] * fields[1][r] + weights[2] * fields[2][r]
                solution_out[c, z, pl.ds(r, 8, stride=slab.parts)] = total
        copies[z].start()

    lane = lax.broadcasted_iota(jnp.int32, summed.shape, 1)
    kind = lax.rem(lane, 8) // 2
    spread = residual[0]
    for k in range(1, ITERS + 1):
        spread = jnp.where(kind == k, residual[k], spread)
    count = corners.shape[1]
    spots = jnp.minimum(lane * 8, px - 1)
    values = []
    for i in range(n_in):
        product = got[i] * spread
        product = jnp.where(lax.rem(lane, 2) == 0, product, pltpu.roll(product, n_sub - 1, 0))
        for reach in (1, 2, 4):
            product = product + pltpu.roll(product, px - reach, 1)
        values.append(jnp.take_along_axis(product, spots, axis=1, mode="promise_in_bounds")[:, :count])

    face = None
    for k in range(ITERS + 1):
        part = mine[k] * right[k] + other[k] * left_next[k]
        face = part if face is None else face + part

    zs = lax.broadcasted_iota(jnp.int32, face.shape, 0)
    ls = lax.broadcasted_iota(jnp.int32, face.shape, 1)
    y = lax.rem(ls, py)
    face = jnp.take_along_axis(
        face, ls - y + lax.rem(y, slab.parts) * 8 + y // slab.parts, axis=1, mode="promise_in_bounds")
    flat = (ls // py) * (depth * py) + zs * py + y
    picks = corners[...]
    for j in range(count):
        total = None
        for i in range(n_in):
            part = coarse[j, i] * values[i]
            total = part if total is None else total + part
        value = jnp.sum(jnp.sum(total, axis=0, keepdims=True), axis=1, keepdims=True)
        face = face + jnp.where(flat == picks[:, j : j + 1], value, 0.0)
    for c in range(comp):
        interface_out[0, c] = face[:, py * c : py * (c + 1)]
    copies.append(pltpu.make_async_copy(interface_out, interface_hbm, sems.at[depth]))
    copies[depth].start()
    for copy in copies:
        copy.wait()


def params(mib):
    return pltpu.CompilerParams(vmem_limit_bytes=mib * 2**20)


def on_device(body_load, materials, material_tables, corner_index, coarse_inverse):
    comp, depth, py, px = body_load.shape
    kinds = material_tables.shape[0]
    n_in, n_sub = lax.axis_size("in"), lax.axis_size("sub")
    devices = n_in * n_sub
    count = corner_index.shape[0]
    f32 = jnp.float32
    shape = jax.ShapeDtypeStruct
    halo = shape((ITERS * comp + MAT_DEPTH, py, px), f32)

    table = material_tables.transpose(1, 2, 0).reshape(comp * comp, kinds)
    coarse = coarse_inverse.reshape(count, n_sub, n_in, count).transpose(0, 2, 1, 3)

    def hbm(x):
        return pltpu.with_memory_space_constraint(x, pltpu.HBM)

    send_a, send_b, middle, mats, table = pl.pallas_call(
        pack_kernel,
        out_shape=(
            halo, halo, shape((comp, depth - 2 * ITERS, py, px), f32), shape(materials.shape, jnp.int32), shape(table.shape, f32)),
        in_specs=[HBM] * 3,
        out_specs=(VMEM,) * 5,
        scratch_shapes=[
            pltpu.SemaphoreType.DMA((2, comp)),
            pltpu.SemaphoreType.DMA((3,)),
        ],
        compiler_params=params(4),
        name="pack",
    )(hbm(body_load), hbm(materials), hbm(table))

    def swaps(start):
        pairs = [(i, i + 1) for i in range(start, n_in - 1, 2)]
        return pairs + [(j, i) for i, j in pairs]

    halo_a = lax.ppermute(send_a, "in", swaps(0))
    halo_b = lax.ppermute(send_b, "in", swaps(1))
    before = lax.ppermute(corner_index, "sub", [(i, (i + 1) % n_sub) for i in range(n_sub)])

    fields = (
        shape((comp, depth + 2 * ITERS, py, px), f32),
        shape((comp, depth + 2 * ITERS - 2, py, px), f32),
        shape((comp, depth + 2 * ITERS - 4, py, px), f32),
        shape((comp, depth, py, px), f32),
        shape((comp * comp, depth + 2 * MAT_DEPTH, py, px), f32),
        shape((len(PAIRS), 8, px), f32),
    )
    *inner, tab = pl.pallas_call(
        interior_kernel,
        out_shape=(*fields, shape((kinds * comp * comp + 24, px), f32)),
        in_specs=[VMEM] * 5,
        out_specs=(VMEM,) * 7,
        compiler_params=params(4),
        name="interior",
    )(send_a, send_b, middle, mats, table)

    inner = pl.pallas_call(
        functools.partial(near_kernel, kinds),
        out_shape=fields,
        in_specs=[VMEM] * 8,
        out_specs=(VMEM,) * 6,
        input_output_aliases={2 + k: k for k in range(6)},
        compiler_params=params(4),
        name="near",
    )(halo_a, tab, *inner)

    v0, v1, v2, v3, _, message = pl.pallas_call(
        functools.partial(far_kernel, kinds),
        out_shape=(*fields[:5], shape((devices, LANES), f32)),
        in_specs=[VMEM] * 2 + [HBM] * 2 + [VMEM] * 6,
        out_specs=(VMEM,) * 6,
        input_output_aliases={4 + k: k for k in range(5)},
        scratch_shapes=[
            pltpu.SMEM((count,), jnp.int32),
            pltpu.SMEM((count,), jnp.int32),
            pltpu.SemaphoreType.DMA((2,)),
        ],
        compiler_params=params(4),
        name="far",
    )(halo_b, tab, hbm(corner_index), before, *inner)

    messages = lax.all_to_all(message, ("sub", "in"), 0, 0, tiled=True)
    faces = shape((ITERS + 1, depth, comp * py), f32)
    left, right = pl.pallas_call(
        faces_kernel,
        out_shape=(faces, faces),
        in_specs=[VMEM] * 4,
        out_specs=(VMEM, VMEM),
        compiler_params=params(4),
        name="faces",
    )(v0, v1, v2, v3)
    left_next = lax.ppermute(left, "sub", [((i + 1) % n_sub, i) for i in range(n_sub)])

    return pl.pallas_call(
        functools.partial(final_kernel, kinds),
        out_shape=(shape(body_load.shape, f32), shape((1, comp, depth, py), f32)),
        in_specs=[VMEM] * 9,
        out_specs=(HBM, HBM),
        scratch_shapes=[
            pltpu.VMEM((2 * ITERS + 1, n_sub, LANES), f32),
            pltpu.VMEM(body_load.shape, f32),
            pltpu.VMEM((1, comp, depth, py), f32),
            pltpu.SemaphoreType.DMA((depth + 1,)),
        ],
        compiler_params=params(16),
        name="final",
    )(messages, v0, v1, v2, right, left_next, tab, coarse, corner_index.reshape(1, count))


def solution(mesh):
    return jax.shard_map(
        on_device,
        mesh=mesh,
        in_specs=(
            P(None, "in", None, "sub"),
            P("in", None, "sub"),
            P(),
            P(("sub", "in")),
            P(("sub", "in"), None),
        ),
        out_specs=(P(None, "in", None, "sub"), P("sub", None, "in", None)),
        check_vma=False,
    )
```

```python
import functools

import jax
import jax.numpy as jnp
from jax import lax
from jax.experimental import pallas as pl
from jax.experimental.pallas import tpu as pltpu
from jax.sharding import PartitionSpec as P

ITERS = 3
LANES = 128
MAT_DEPTH = ITERS - 1
PAIRS = [(i, j) for i in range(ITERS) for j in range(i, ITERS + 1)]
GRAM_LANE = 64
VMEM = pl.BlockSpec(memory_space=pltpu.VMEM)
SMEM = pl.BlockSpec(memory_space=pltpu.SMEM)
HBM = pl.BlockSpec(memory_space=pl.ANY)


def spectrum(table, comp):
    kinds = table.shape[1]
    rows = lax.broadcasted_iota(jnp.int32, table.shape, 0)
    diagonal = lax.rem(rows, comp + 1) == 0
    picked = jnp.where(diagonal, table, 0.0)
    mean = jnp.sum(jnp.sum(picked, axis=0, keepdims=True), axis=1, keepdims=True) / (comp * kinds)
    centred = jnp.where(diagonal, table - mean, table)
    size = jnp.abs(centred)
    widest = jnp.zeros((1, kinds), jnp.float32)
    for c in range(comp):
        widest = jnp.maximum(widest, jnp.sum(size[comp * c : comp * (c + 1)], axis=0, keepdims=True))
    scale = 6.0 + jnp.max(widest, axis=1, keepdims=True)
    return mean, scale, centred


def split(index, size):
    if size & (size - 1):
        return lax.div(index, size), lax.rem(index, size)
    return lax.shift_right_logical(index, size.bit_length() - 1), index & (size - 1)


def pack_kernel(body, mats, table, a_out, b_out, middle_out, mats_out, table_out, sems, rest):
    comp, depth = body.shape[0], body.shape[1]
    odd = lax.rem(lax.axis_index("in") + 1, 2)
    sides = ((a_out, odd), (b_out, 1 - odd))
    copies = []
    for slot, (out, low) in enumerate(sides):
        first = (1 - low) * (depth - ITERS)
        for c in range(comp):
            copies.append(pltpu.make_async_copy(
                body.at[c, pl.ds(first, ITERS)], out.at[pl.ds(ITERS * c, ITERS)], sems.at[slot, c]))
    copies.append(pltpu.make_async_copy(mats, mats_out, rest.at[0]))
    copies.append(pltpu.make_async_copy(body.at[:, pl.ds(ITERS, depth - 2 * ITERS)], middle_out, rest.at[1]))
    copies.append(pltpu.make_async_copy(table, table_out, rest.at[2]))
    for copy in copies:
        copy.start()
    for copy in copies:
        copy.wait()
    for out, low in sides:
        first = (1 - low) * (depth - MAT_DEPTH)
        for t in range(MAT_DEPTH):
            out[ITERS * comp + t] = mats_out[first + t].astype(jnp.float32)


class Slab:
    def __init__(self, comp, py, px):
        self.comp, self.px, self.parts = comp, px, py // 8
        lane = lax.broadcasted_iota(jnp.int32, (8, px), 1)
        row = lax.broadcasted_iota(jnp.int32, (8, px), 0)
        self.lane = lane
        self.first_x, self.last_x = lane == 0, lane == px - 1
        self.first_y, self.last_y = row == 0, row == 7

    def natural(self, ref, *at):
        return [ref[(*at, pl.ds(r, 8, stride=self.parts))] for r in range(self.parts)]

    def load(self, ref, *at):
        return [ref[(*at, pl.ds(8 * r, 8))] for r in range(self.parts)]

    def store(self, ref, values, *at):
        for r in range(self.parts):
            ref[(*at, pl.ds(8 * r, 8))] = values[r]

    def neighbours(self, below, above, value):
        parts, px = self.parts, self.px
        totals = []
        for r in range(parts):
            total = below[r] + above[r]
            total += jnp.where(self.first_x, 0.0, pltpu.roll(value[r], 1, 1))
            total += jnp.where(self.last_x, 0.0, pltpu.roll(value[r], px - 1, 1))
            total += value[r - 1] if r else jnp.where(self.first_y, 0.0, pltpu.roll(value[parts - 1], 1, 0))
            total += value[r + 1] if r + 1 < parts else jnp.where(self.last_y, 0.0, pltpu.roll(value[0], 7, 0))
            totals.append(total)
        return totals

    def applied(self, source, at, gains, gains_at, inverse, alive=None):
        comp, parts = self.comp, self.parts
        values = [self.load(source, c, at) for c in range(comp)]
        for c in range(comp):
            around = self.neighbours(self.load(source, c, at - 1), self.load(source, c, at + 1), values[c])
            out = []
            for r in range(parts):
                total = None
                for d in range(comp):
                    term = gains[comp * c + d, gains_at, pl.ds(8 * r, 8)] * values[d][r]
                    total = term if total is None else total + term
                total = total - inverse * around[r]
                out.append(total if alive is None else alive * total)
            yield c, values[c], out

    def products(self, total, left, right):
        for r in range(self.parts):
            total = total + left[r] * right[r]
        return total

    def look_up(self, kinds, tab, gains, at, count):
        bits = [[(kind & (1 << b)) != 0 for kind in kinds] for b in range((count - 1).bit_length())]
        entries = self.comp * self.comp
        for e in range(entries):
            lines = [tab[pl.ds(k * entries + e, 8, stride=0)] for k in range(count)]
            out = []
            for r in range(self.parts):
                level = lines
                for bit in bits:
                    level = [
                        jnp.where(bit[r], level[k + 1], level[k]) if k + 1 < len(level) else level[k]
                        for k in range(0, len(level), 2)
                    ]
                out.append(level[0])
            self.store(gains, out, e, at)


def levels(slab, v0, v1, v2, v3, gains, inverse):
    def first(z, sums):
        g01, g11 = sums
        for c, v, w in slab.applied(v0, z + 3, gains, z + 2, inverse):
            slab.store(v1, w, c, z + 2)
            g01, g11 = slab.products(g01, v, w), slab.products(g11, w, w)
        return g01, g11

    def second(z, sums):
        g02, g12, g22 = sums
        for c, v, w in slab.applied(v1, z + 2, gains, z + 2, inverse):
            slab.store(v2, w, c, z + 1)
            u = slab.load(v0, c, z + 3)
            g02, g12, g22 = slab.products(g02, u, w), slab.products(g12, v, w), slab.products(g22, w, w)
        return g02, g12, g22

    def third(z, sums):
        g03, g13, g23 = sums
        for c, v, w in slab.applied(v2, z + 1, gains, z + 2, inverse):
            t, u = slab.load(v0, c, z + 3), slab.load(v1, c, z + 2)
            slab.store(v3, w, c, z)
            g03, g13, g23 = slab.products(g03, t, w), slab.products(g13, u, w), slab.products(g23, v, w)
        return g03, g13, g23

    return first, second, third


def interior_kernel(side_a, side_b, middle, mats, table, v0, v1, v2, v3, gains, gram, tab):
    comp, _, py, px = middle.shape
    depth = mats.shape[0]
    odd = lax.rem(lax.axis_index("in") + 1, 2) == 1
    kinds = table.shape[1]
    entries = comp * comp
    slab = Slab(comp, py, px)
    mean, scale, centred = spectrum(table[...], comp)
    inverse = jnp.broadcast_to(1.0 / scale, (8, px))
    scaled = centred / scale
    for k in range(kinds):
        tab[pl.ds(k * entries, entries)] = jnp.broadcast_to(scaled[:, k : k + 1], (entries, px))
    for t, value in enumerate((inverse, mean, scale)):
        tab[pl.ds(kinds * entries + 8 * t, 8)] = jnp.broadcast_to(value, (8, px))
    zero = jnp.zeros((8, px), jnp.float32)
    for c in range(comp):
        for at in (ITERS - 1, ITERS + depth):
            slab.store(v0, [zero] * slab.parts, c, at)

    def place(values, z, g00):
        for c in range(comp):
            slab.store(v0, values[c], c, ITERS + z)
            g00 = slab.products(g00, values[c], values[c])
        slab.look_up(slab.natural(mats, z), tab, gains, MAT_DEPTH + z, kinds)
        return g00

    def outer(t, g00):
        a = [slab.natural(side_a, ITERS * c + t) for c in range(comp)]
        b = [slab.natural(side_b, ITERS * c + t) for c in range(comp)]
        low = [[jnp.where(odd, x, y) for x, y in zip(a[c], b[c])] for c in range(comp)]
        g00 = place(low, t, g00)
        high = [[jnp.where(odd, y, x) for x, y in zip(a[c], b[c])] for c in range(comp)]
        return place(high, depth - ITERS + t, g00)

    def centre(m, g00):
        return place([slab.natural(middle, c, m) for c in range(comp)], ITERS + m, g00)
    g00 = lax.fori_loop(0, ITERS, outer, zero)
    g00 = lax.fori_loop(0, depth - 2 * ITERS, centre, g00)

    def partial(i, carry):
        z = i * (depth - 1)
        for c, _, w in slab.applied(v0, z + 3, gains, z + 2, inverse):
            slab.store(v1, w, c, z + 2)
        return carry

    def partial_second(i, carry):
        z = 1 + i * (depth - 3)
        for c, _, w in slab.applied(v1, z + 2, gains, z + 2, inverse):
            slab.store(v2, w, c, z + 1)
        return carry

    def partial_third(i, carry):
        z = 2 + i * (depth - 5)
        for c, _, w in slab.applied(v2, z + 1, gains, z + 2, inverse):
            slab.store(v3, w, c, z)
        return carry

    first, second, third = levels(slab, v0, v1, v2, v3, gains, inverse)
    lax.fori_loop(0, 2, partial, 0)
    g01, g11 = lax.fori_loop(1, depth - 1, first, (zero,) * 2)
    lax.fori_loop(0, 2, partial_second, 0)
    g02, g12, g22 = lax.fori_loop(2, depth - 2, second, (zero,) * 3)
    lax.fori_loop(0, 2, partial_third, 0)
    g03, g13, g23 = lax.fori_loop(3, depth - 3, third, (zero,) * 3)
    for g, value in enumerate((g00, g01, g02, g03, g11, g12, g13, g22, g23)):
        gram[g] = value


def one_side(kinds, slot, halo, tab, gram, v0, v1, v2, v3, gains):
    comp, py, px = v0.shape[0], v0.shape[2], v0.shape[3]
    depth = v3.shape[1]
    slab = Slab(comp, py, px)
    place = lax.axis_index("in")
    low = lax.rem(place + slot, 2) == 0
    alive = jnp.where(low, place > 0, place < lax.axis_size("in") - 1).astype(jnp.float32)
    inverse = tab[pl.ds(kinds * comp * comp, 8)]

    def layer(q):
        return jnp.where(low, q, depth - 1 - q)

    base = jnp.where(low, 0, ITERS + depth)
    for t in range(ITERS):
        for c in range(comp):
            slab.store(v0, slab.natural(halo, ITERS * c + t), c, base + t)

    base_gains = jnp.where(low, 0, MAT_DEPTH + depth)

    def halo_gains(t, carry):
        kind = [x.astype(jnp.int32) for x in slab.natural(halo, ITERS * comp + t)]
        slab.look_up(kind, tab, gains, base_gains + t, kinds)
        return carry
    lax.fori_loop(0, MAT_DEPTH, halo_gains, 0)

    g00, g01, g02, g03, g11, g12, g13, g22, g23 = [gram[g] for g in range(len(PAIRS))]
    first, second, third = levels(slab, v0, v1, v2, v3, gains, inverse)

    def first_halo(i, carry):
        z = layer(i - 2)
        for c, _, w in slab.applied(v0, z + 3, gains, z + 2, inverse, alive):
            slab.store(v1, w, c, z + 2)
        return carry
    lax.fori_loop(0, 2, first_halo, 0)

    z0, z1, z2, out = layer(0), layer(1), layer(2), layer(-1)

    def mend(c, sums):
        g01, g11, g02, g12, g22, g03, g13, g23 = sums
        term = [inverse * x for x in slab.load(v0, c, out + 3)]
        w = [a - b for a, b in zip(slab.load(v1, c, z0 + 2), term)]
        slab.store(v1, w, c, z0 + 2)
        g01, g11 = slab.products(g01, slab.load(v0, c, z0 + 3), w), slab.products(g11, w, w)
        term = [inverse * x for x in term]
        w = [a + b for a, b in zip(slab.load(v2, c, z1 + 1), term)]
        slab.store(v2, w, c, z1 + 1)
        g02 = slab.products(g02, slab.load(v0, c, z1 + 3), w)
        g12 = slab.products(g12, slab.load(v1, c, z1 + 2), w)
        g22 = slab.products(g22, w, w)
        term = [inverse * x for x in term]
        w = [a - b for a, b in zip(slab.load(v3, c, z2), term)]
        slab.store(v3, w, c, z2)
        t, u, v = slab.load(v0, c, z2 + 3), slab.load(v1, c, z2 + 2), slab.load(v2, c, z2 + 1)
        g03, g13, g23 = slab.products(g03, t, w), slab.products(g13, u, w), slab.products(g23, v, w)
        return g01, g11, g02, g12, g22, g03, g13, g23
    sums = (g01, g11, g02, g12, g22, g03, g13, g23)
    for c in range(comp):
        sums = mend(c, sums)
    g01, g11, g02, g12, g22, g03, g13, g23 = sums

    for c, _, w in slab.applied(v1, out + 2, gains, out + 2, inverse, alive):
        slab.store(v2, w, c, out + 1)
    g02, g12, g22 = second(z0, (g02, g12, g22))
    g03, g13, g23 = lax.fori_loop(0, 2, lambda i, sums: third(layer(i), sums), (g03, g13, g23))
    return g00, g01, g02, g03, g11, g12, g13, g22, g23


def near_kernel(kinds, halo, tab, v0_in, v1_in, v2_in, v3_in, gains_in, gram_in, v0, v1, v2, v3, gains, gram):
    sums = one_side(kinds, 0, halo, tab, gram_in, v0, v1, v2, v3, gains)
    for g, value in enumerate(sums):
        gram[g] = value


def far_kernel(kinds, halo, tab, corners_hbm, before_hbm, v0_in, v1_in, v2_in, v3_in, gains_in, gram_in,
               v0, v1, v2, v3, gains, message, corners, before, sems):
    fetch = (
        pltpu.make_async_copy(corners_hbm, corners, sems.at[0]),
        pltpu.make_async_copy(before_hbm, before, sems.at[1]),
    )
    for copy in fetch:
        copy.start()
    py, px = v0.shape[2], v0.shape[3]
    depth, parts = v3.shape[1], py // 8
    sums = one_side(kinds, 1, halo, tab, gram_in, v0, v1, v2, v3, gains)

    spots = lax.broadcasted_iota(jnp.int32, (1, px), 1)
    line = jnp.zeros((1, px), jnp.float32)
    for g, value in enumerate(sums):
        total = jnp.sum(jnp.sum(value, axis=0, keepdims=True), axis=1, keepdims=True)
        line = jnp.where(spots == GRAM_LANE + g, total, line)

    for copy in fetch:
        copy.wait()

    def corner_rows(index):
        c, rest = split(index, depth * py)
        z, y = split(rest, py)
        t, r = split(y, parts)
        row = pl.ds(r * 8 + t, 1)
        return [field[c, z + ITERS - k, row] for k, field in enumerate((v0, v1, v2, v3))]

    for j in range(corners.shape[0]):
        rows = zip(corner_rows(corners[j]), corner_rows(before[j]))
        for k, (mine, other) in enumerate(rows):
            moved = pltpu.roll(jnp.where(spots == px - 1, mine, other), 8 * j + 2 * k + 1, 1)
            line = jnp.where(spots // 2 == 4 * j + k, moved, line)
    message[...] = jnp.broadcast_to(line, message.shape)


def faces_kernel(v0, v1, v2, v3, left, right):
    comp, depth, py, px = v3.shape
    for z in range(depth):
        for k, field in enumerate((v0, v1, v2, v3)):
            turned = jnp.concatenate([field[c, z + ITERS - k] for c in range(comp)], axis=0).T
            left[k, pl.ds(z, 1)] = turned[0:1]
            right[k, pl.ds(z, 1)] = turned[px - 1 : px]


def total_of(terms):
    while len(terms) > 1:
        terms = [sum(terms[k : k + 2][1:], terms[k]) for k in range(0, len(terms), 2)]
    return terms[0]


def coefficients(gram, centre, scale):
    norms, images = {}, {}
    for i in range(ITERS):
        for j in range(i, ITERS):
            forward = centre * gram[(i, j)] + scale * gram[(i, j + 1)]
            if i == j:
                norms[(i, j)], images[(i, j)] = gram[(i, j)], forward
            else:
                back = centre * gram[(i, j)] + scale * gram[(i + 1, j)]
                norms[(i, j)], images[(i, j)] = 2.0 * gram[(i, j)], forward + back

    def quadratic(form, u):
        size = len(u)
        return total_of([(u[i] * u[j]) * form[(i, j)] for i in range(size) for j in range(i, size)])

    one = jnp.ones_like(centre)
    residual, direction, found = [one], [one], []
    norm = gram[(0, 0)]
    for repeat in range(ITERS):
        size = len(direction)
        step = norm / (quadratic(images, direction) if repeat else images[(0, 0)])
        image = [centre * direction[0]]
        for j in range(1, size):
            image.append(centre * direction[j] + scale * direction[j - 1])
        image.append(scale * direction[size - 1])
        found = [
            (found[j] if j < len(found) else 0.0) + step * direction[j] for j in range(size)
        ]
        residual = [
            (residual[j] if j < size else 0.0) - step * image[j] for j in range(size + 1)
        ]
        if repeat + 1 < ITERS:
            inverse = 1.0 / norm
            norm = quadratic(norms, residual)
            ratio = norm * inverse
            direction = [
                residual[j] + (ratio * direction[j] if j < size else 0.0) for j in range(size + 1)
            ]
    return found, residual


def final_kernel(kinds, messages, v0, v1, v2, right, left_next, tab, coarse, corners,
                 solution_hbm, interface_hbm, book, solution_out, interface_out, sems):
    comp, py, px = v0.shape[0], v0.shape[2], v0.shape[3]
    depth = right.shape[1]
    n_in, n_sub = lax.axis_size("in"), lax.axis_size("sub")
    sub = lax.axis_index("sub")
    following = lax.rem(sub + 1, n_sub)
    slab = Slab(comp, py, px)
    base = kinds * comp * comp

    got = [messages[pl.ds(i, n_sub, stride=n_in)] for i in range(n_in)]
    summed = total_of(got)
    mean = jnp.broadcast_to(tab[pl.ds(base + 8, 1)], summed.shape)
    scale = jnp.broadcast_to(tab[pl.ds(base + 16, 1)], summed.shape)
    gram = {}
    for g, pair in enumerate(PAIRS):
        gram[pair] = jnp.broadcast_to(summed[:, GRAM_LANE + g : GRAM_LANE + g + 1], summed.shape)
    found, residual = coefficients(gram, 6.0 + mean, scale)

    for k, value in enumerate(residual + found):
        book[k] = value
    weights = [book[ITERS + 1 + k, pl.ds(sub, 8, stride=0)] for k in range(ITERS)]
    mine = [book[k, pl.ds(sub, depth, stride=0)] for k in range(ITERS + 1)]
    other = [book[k, pl.ds(following, depth, stride=0)] for k in range(ITERS + 1)]

    copies = [
        pltpu.make_async_copy(solution_out.at[:, z], solution_hbm.at[:, z], sems.at[z]) for z in range(depth)
    ]
    for z in range(depth):
        for c in range(comp):
            fields = slab.load(v0, c, z + 3), slab.load(v1, c, z + 2), slab.load(v2, c, z + 1)
            for r in range(slab.parts):
                total = weights[0] * fields[0][r] + weights[1] * fields[1][r] + weights[2] * fields[2][r]
                solution_out[c, z, pl.ds(r, 8, stride=slab.parts)] = total
        copies[z].start()

    lane = lax.broadcasted_iota(jnp.int32, summed.shape, 1)
    kind = lax.rem(lane, 8) // 2
    spread = residual[0]
    for k in range(1, ITERS + 1):
        spread = jnp.where(kind == k, residual[k], spread)
    count = corners.shape[1]
    spots = jnp.minimum(lane * 8, px - 1)
    values = []
    for i in range(n_in):
        product = got[i] * spread
        product = jnp.where(lax.rem(lane, 2) == 0, product, pltpu.roll(product, n_sub - 1, 0))
        for reach in (1, 2, 4):
            product = product + pltpu.roll(product, px - reach, 1)
        values.append(jnp.take_along_axis(product, spots, axis=1, mode="promise_in_bounds")[:, :count])

    face = None
    for k in range(ITERS + 1):
        part = mine[k] * right[k] + other[k] * left_next[k]
        face = part if face is None else face + part

    zs = lax.broadcasted_iota(jnp.int32, face.shape, 0)
    ls = lax.broadcasted_iota(jnp.int32, face.shape, 1)
    y = lax.rem(ls, py)
    face = jnp.take_along_axis(
        face, ls - y + lax.rem(y, slab.parts) * 8 + y // slab.parts, axis=1, mode="promise_in_bounds")
    flat = (ls // py) * (depth * py) + zs * py + y
    picks = corners[...]
    for j in range(count):
        total = None
        for i in range(n_in):
            part = coarse[j, i] * values[i]
            total = part if total is None else total + part
        value = jnp.sum(jnp.sum(total, axis=0, keepdims=True), axis=1, keepdims=True)
        face = face + jnp.where(flat == picks[:, j : j + 1], value, 0.0)
    for c in range(comp):
        interface_out[0, c] = face[:, py * c : py * (c + 1)]
    copies.append(pltpu.make_async_copy(interface_out, interface_hbm, sems.at[depth]))
    copies[depth].start()
    for copy in copies:
        copy.wait()


def params(mib):
    return pltpu.CompilerParams(vmem_limit_bytes=mib * 2**20)


def on_device(body_load, materials, material_tables, corner_index, coarse_inverse):
    comp, depth, py, px = body_load.shape
    kinds = material_tables.shape[0]
    n_in, n_sub = lax.axis_size("in"), lax.axis_size("sub")
    devices = n_in * n_sub
    count = corner_index.shape[0]
    f32 = jnp.float32
    shape = jax.ShapeDtypeStruct
    halo = shape((ITERS * comp + MAT_DEPTH, py, px), f32)

    table = material_tables.transpose(1, 2, 0).reshape(comp * comp, kinds)
    coarse = coarse_inverse.reshape(count, n_sub, n_in, count).transpose(0, 2, 1, 3)

    def hbm(x):
        return pltpu.with_memory_space_constraint(x, pltpu.HBM)

    send_a, send_b, middle, mats, table = pl.pallas_call(
        pack_kernel,
        out_shape=(
            halo, halo, shape((comp, depth - 2 * ITERS, py, px), f32), shape(materials.shape, jnp.int32), shape(table.shape, f32)),
        in_specs=[HBM] * 3,
        out_specs=(VMEM,) * 5,
        scratch_shapes=[
            pltpu.SemaphoreType.DMA((2, comp)),
            pltpu.SemaphoreType.DMA((3,)),
        ],
        compiler_params=params(4),
        name="pack",
    )(hbm(body_load), hbm(materials), hbm(table))

    def swaps(start):
        pairs = [(i, i + 1) for i in range(start, n_in - 1, 2)]
        return pairs + [(j, i) for i, j in pairs]

    halo_a = lax.ppermute(send_a, "in", swaps(1))
    halo_b = lax.ppermute(send_b, "in", swaps(0))
    before = lax.ppermute(corner_index, "sub", [(i, (i + 1) % n_sub) for i in range(n_sub)])

    fields = (
        shape((comp, depth + 2 * ITERS, py, px), f32),
        shape((comp, depth + 2 * ITERS - 2, py, px), f32),
        shape((comp, depth + 2 * ITERS - 4, py, px), f32),
        shape((comp, depth, py, px), f32),
        shape((comp * comp, depth + 2 * MAT_DEPTH, py, px), f32),
        shape((len(PAIRS), 8, px), f32),
    )
    *inner, tab = pl.pallas_call(
        interior_kernel,
        out_shape=(*fields, shape((kinds * comp * comp + 24, px), f32)),
        in_specs=[VMEM] * 5,
        out_specs=(VMEM,) * 7,
        compiler_params=params(4),
        name="interior",
    )(send_a, send_b, middle, mats, table)

    inner = pl.pallas_call(
        functools.partial(near_kernel, kinds),
        out_shape=fields,
        in_specs=[VMEM] * 8,
        out_specs=(VMEM,) * 6,
        input_output_aliases={2 + k: k for k in range(6)},
        compiler_params=params(4),
        name="near",
    )(halo_a, tab, *inner)

    v0, v1, v2, v3, _, message = pl.pallas_call(
        functools.partial(far_kernel, kinds),
        out_shape=(*fields[:5], shape((devices, LANES), f32)),
        in_specs=[VMEM] * 2 + [HBM] * 2 + [VMEM] * 6,
        out_specs=(VMEM,) * 6,
        input_output_aliases={4 + k: k for k in range(5)},
        scratch_shapes=[
            pltpu.SMEM((count,), jnp.int32),
            pltpu.SMEM((count,), jnp.int32),
            pltpu.SemaphoreType.DMA((2,)),
        ],
        compiler_params=params(4),
        name="far",
    )(halo_b, tab, hbm(corner_index), before, *inner)

    messages = lax.all_to_all(message, ("sub", "in"), 0, 0, tiled=True)
    faces = shape((ITERS + 1, depth, comp * py), f32)
    left, right = pl.pallas_call(
        faces_kernel,
        out_shape=(faces, faces),
        in_specs=[VMEM] * 4,
        out_specs=(VMEM, VMEM),
        compiler_params=params(4),
        name="faces",
    )(v0, v1, v2, v3)
    left_next = lax.ppermute(left, "sub", [((i + 1) % n_sub, i) for i in range(n_sub)])

    return pl.pallas_call(
        functools.partial(final_kernel, kinds),
        out_shape=(shape(body_load.shape, f32), shape((1, comp, depth, py), f32)),
        in_specs=[VMEM] * 9,
        out_specs=(HBM, HBM),
        scratch_shapes=[
            pltpu.VMEM((2 * ITERS + 1, n_sub, LANES), f32),
            pltpu.VMEM(body_load.shape, f32),
            pltpu.VMEM((1, comp, depth, py), f32),
            pltpu.SemaphoreType.DMA((depth + 1,)),
        ],
        compiler_params=params(16),
        name="final",
    )(messages, v0, v1, v2, right, left_next, tab, coarse, corner_index.reshape(1, count))


def solution(mesh):
    return jax.shard_map(
        on_device,
        mesh=mesh,
        in_specs=(
            P(None, "in", None, "sub"),
            P("in", None, "sub"),
            P(),
            P(("sub", "in")),
            P(("sub", "in"), None),
        ),
        out_specs=(P(None, "in", None, "sub"), P("sub", None, "in", None)),
        check_vma=False,
    )
```

```python
import functools

import jax
import jax.numpy as jnp
from jax import lax
from jax.experimental import pallas as pl
from jax.experimental.pallas import tpu as pltpu
from jax.sharding import PartitionSpec as P

ITERS = 3
LANES = 128
MAT_DEPTH = ITERS - 1
PAIRS = [(i, j) for i in range(ITERS) for j in range(i, ITERS + 1)]
GRAM_LANE = 64
VMEM = pl.BlockSpec(memory_space=pltpu.VMEM)
SMEM = pl.BlockSpec(memory_space=pltpu.SMEM)
HBM = pl.BlockSpec(memory_space=pl.ANY)


def spectrum(table, comp):
    kinds = table.shape[1]
    rows = lax.broadcasted_iota(jnp.int32, table.shape, 0)
    diagonal = lax.rem(rows, comp + 1) == 0
    picked = jnp.where(diagonal, table, 0.0)
    mean = jnp.sum(jnp.sum(picked, axis=0, keepdims=True), axis=1, keepdims=True) / (comp * kinds)
    centred = jnp.where(diagonal, table - mean, table)
    size = jnp.abs(centred)
    widest = jnp.zeros((1, kinds), jnp.float32)
    for c in range(comp):
        widest = jnp.maximum(widest, jnp.sum(size[comp * c : comp * (c + 1)], axis=0, keepdims=True))
    scale = 6.0 + jnp.max(widest, axis=1, keepdims=True)
    return mean, scale, centred


def split(index, size):
    if size & (size - 1):
        return lax.div(index, size), lax.rem(index, size)
    return lax.shift_right_logical(index, size.bit_length() - 1), index & (size - 1)


def pack_kernel(body, mats, a_out, b_out, kinds, sems):
    comp, depth = body.shape[0], body.shape[1]
    odd = lax.rem(lax.axis_index("in") + 1, 2)
    copies = []
    for slot, (out, low) in enumerate(((a_out, odd), (b_out, 1 - odd))):
        first = (1 - low) * (depth - ITERS)
        for c in range(comp):
            copies.append(pltpu.make_async_copy(
                body.at[c, pl.ds(first, ITERS)], out.at[pl.ds(ITERS * c, ITERS)], sems.at[slot, c]))
        first = (1 - low) * (depth - MAT_DEPTH)
        copies.append(pltpu.make_async_copy(
            mats.at[pl.ds(first, MAT_DEPTH)], kinds.at[slot], sems.at[slot, comp]))
    for copy in copies:
        copy.start()
    for copy in copies:
        copy.wait()
    for slot, out in enumerate((a_out, b_out)):
        out[pl.ds(ITERS * comp, MAT_DEPTH)] = kinds[slot].astype(jnp.float32)


class Slab:
    def __init__(self, comp, py, px):
        self.comp, self.px, self.parts = comp, px, py // 8
        lane = lax.broadcasted_iota(jnp.int32, (8, px), 1)
        row = lax.broadcasted_iota(jnp.int32, (8, px), 0)
        self.lane = lane
        self.first_x, self.last_x = lane == 0, lane == px - 1
        self.first_y, self.last_y = row == 0, row == 7

    def natural(self, ref, *at):
        return [ref[(*at, pl.ds(r, 8, stride=self.parts))] for r in range(self.parts)]

    def load(self, ref, *at):
        return [ref[(*at, pl.ds(8 * r, 8))] for r in range(self.parts)]

    def store(self, ref, values, *at):
        for r in range(self.parts):
            ref[(*at, pl.ds(8 * r, 8))] = values[r]

    def neighbours(self, below, above, value):
        parts, px = self.parts, self.px
        totals = []
        for r in range(parts):
            total = below[r] + above[r]
            total += jnp.where(self.first_x, 0.0, pltpu.roll(value[r], 1, 1))
            total += jnp.where(self.last_x, 0.0, pltpu.roll(value[r], px - 1, 1))
            total += value[r - 1] if r else jnp.where(self.first_y, 0.0, pltpu.roll(value[parts - 1], 1, 0))
            total += value[r + 1] if r + 1 < parts else jnp.where(self.last_y, 0.0, pltpu.roll(value[0], 7, 0))
            totals.append(total)
        return totals

    def applied(self, source, at, gains, gains_at, inverse, alive=None):
        comp, parts = self.comp, self.parts
        values = [self.load(source, c, at) for c in range(comp)]
        for c in range(comp):
            around = self.neighbours(self.load(source, c, at - 1), self.load(source, c, at + 1), values[c])
            out = []
            for r in range(parts):
                total = None
                for d in range(comp):
                    term = gains[comp * c + d, gains_at, pl.ds(8 * r, 8)] * values[d][r]
                    total = term if total is None else total + term
                total = total - inverse * around[r]
                out.append(total if alive is None else alive * total)
            yield c, values[c], out

    def products(self, total, left, right):
        for r in range(self.parts):
            total = total + left[r] * right[r]
        return total

    def look_up(self, kinds, tab, gains, at, count):
        bits = [[(kind & (1 << b)) != 0 for kind in kinds] for b in range((count - 1).bit_length())]
        entries = self.comp * self.comp
        for e in range(entries):
            lines = [tab[pl.ds(k * entries + e, 8, stride=0)] for k in range(count)]
            out = []
            for r in range(self.parts):
                level = lines
                for bit in bits:
                    level = [
                        jnp.where(bit[r], level[k + 1], level[k]) if k + 1 < len(level) else level[k]
                        for k in range(0, len(level), 2)
                    ]
                out.append(level[0])
            self.store(gains, out, e, at)


def levels(slab, v0, v1, v2, v3, gains, inverse):
    def first(z, sums):
        g01, g11 = sums
        for c, v, w in slab.applied(v0, z + 3, gains, z + 2, inverse):
            slab.store(v1, w, c, z + 2)
            g01, g11 = slab.products(g01, v, w), slab.products(g11, w, w)
        return g01, g11

    def second(z, sums):
        g02, g12, g22 = sums
        for c, v, w in slab.applied(v1, z + 2, gains, z + 2, inverse):
            slab.store(v2, w, c, z + 1)
            u = slab.load(v0, c, z + 3)
            g02, g12, g22 = slab.products(g02, u, w), slab.products(g12, v, w), slab.products(g22, w, w)
        return g02, g12, g22

    def third(z, sums):
        g03, g13, g23 = sums
        for c, v, w in slab.applied(v2, z + 1, gains, z + 2, inverse):
            t, u = slab.load(v0, c, z + 3), slab.load(v1, c, z + 2)
            slab.store(v3, w, c, z)
            g03, g13, g23 = slab.products(g03, t, w), slab.products(g13, u, w), slab.products(g23, v, w)
        return g03, g13, g23

    return first, second, third


def interior_kernel(side_a, side_b, body_hbm, mats_hbm, table_hbm, v0, v1, v2, v3, gains, gram, tab,
                    middle, mats, table, sems):
    comp, depth, py, px = body_hbm.shape
    fetch = (
        pltpu.make_async_copy(table_hbm, table, sems.at[0]),
        pltpu.make_async_copy(mats_hbm, mats, sems.at[1]),
        pltpu.make_async_copy(body_hbm.at[:, pl.ds(ITERS, depth - 2 * ITERS)], middle, sems.at[2]),
    )
    for copy in fetch:
        copy.start()
    fetch[0].wait()
    odd = lax.rem(lax.axis_index("in") + 1, 2) == 1
    kinds = table.shape[1]
    entries = comp * comp
    slab = Slab(comp, py, px)
    mean, scale, centred = spectrum(table[...], comp)
    inverse = jnp.broadcast_to(1.0 / scale, (8, px))
    scaled = centred / scale
    for k in range(kinds):
        tab[pl.ds(k * entries, entries)] = jnp.broadcast_to(scaled[:, k : k + 1], (entries, px))
    for t, value in enumerate((inverse, mean, scale)):
        tab[pl.ds(kinds * entries + 8 * t, 8)] = jnp.broadcast_to(value, (8, px))
    zero = jnp.zeros((8, px), jnp.float32)
    for c in range(comp):
        for at in (ITERS - 1, ITERS + depth):
            slab.store(v0, [zero] * slab.parts, c, at)

    for copy in fetch[1:]:
        copy.wait()

    def place(values, z, g00):
        for c in range(comp):
            slab.store(v0, values[c], c, ITERS + z)
            g00 = slab.products(g00, values[c], values[c])
        slab.look_up(slab.natural(mats, z), tab, gains, MAT_DEPTH + z, kinds)
        return g00

    def outer(t, g00):
        a = [slab.natural(side_a, ITERS * c + t) for c in range(comp)]
        b = [slab.natural(side_b, ITERS * c + t) for c in range(comp)]
        low = [[jnp.where(odd, x, y) for x, y in zip(a[c], b[c])] for c in range(comp)]
        g00 = place(low, t, g00)
        high = [[jnp.where(odd, y, x) for x, y in zip(a[c], b[c])] for c in range(comp)]
        return place(high, depth - ITERS + t, g00)

    def centre(m, g00):
        return place([slab.natural(middle, c, m) for c in range(comp)], ITERS + m, g00)
    g00 = lax.fori_loop(0, ITERS, outer, zero)
    g00 = lax.fori_loop(0, depth - 2 * ITERS, centre, g00)

    def partial(i, carry):
        z = i * (depth - 1)
        for c, _, w in slab.applied(v0, z + 3, gains, z + 2, inverse):
            slab.store(v1, w, c, z + 2)
        return carry

    def partial_second(i, carry):
        z = 1 + i * (depth - 3)
        for c, _, w in slab.applied(v1, z + 2, gains, z + 2, inverse):
            slab.store(v2, w, c, z + 1)
        return carry

    def partial_third(i, carry):
        z = 2 + i * (depth - 5)
        for c, _, w in slab.applied(v2, z + 1, gains, z + 2, inverse):
            slab.store(v3, w, c, z)
        return carry

    first, second, third = levels(slab, v0, v1, v2, v3, gains, inverse)
    lax.fori_loop(0, 2, partial, 0)
    g01, g11 = lax.fori_loop(1, depth - 1, first, (zero,) * 2)
    lax.fori_loop(0, 2, partial_second, 0)
    g02, g12, g22 = lax.fori_loop(2, depth - 2, second, (zero,) * 3)
    lax.fori_loop(0, 2, partial_third, 0)
    g03, g13, g23 = lax.fori_loop(3, depth - 3, third, (zero,) * 3)
    for g, value in enumerate((g00, g01, g02, g03, g11, g12, g13, g22, g23)):
        gram[g] = value


def one_side(kinds, slot, halo, tab, gram, v0, v1, v2, v3, gains):
    comp, py, px = v0.shape[0], v0.shape[2], v0.shape[3]
    depth = v3.shape[1]
    slab = Slab(comp, py, px)
    place = lax.axis_index("in")
    low = lax.rem(place + slot, 2) == 0
    alive = jnp.where(low, place > 0, place < lax.axis_size("in") - 1).astype(jnp.float32)
    inverse = tab[pl.ds(kinds * comp * comp, 8)]

    def layer(q):
        return jnp.where(low, q, depth - 1 - q)

    base = jnp.where(low, 0, ITERS + depth)
    for t in range(ITERS):
        for c in range(comp):
            slab.store(v0, slab.natural(halo, ITERS * c + t), c, base + t)

    base_gains = jnp.where(low, 0, MAT_DEPTH + depth)

    def halo_gains(t, carry):
        kind = [x.astype(jnp.int32) for x in slab.natural(halo, ITERS * comp + t)]
        slab.look_up(kind, tab, gains, base_gains + t, kinds)
        return carry
    lax.fori_loop(0, MAT_DEPTH, halo_gains, 0)

    g00, g01, g02, g03, g11, g12, g13, g22, g23 = [gram[g] for g in range(len(PAIRS))]
    first, second, third = levels(slab, v0, v1, v2, v3, gains, inverse)

    def first_halo(i, carry):
        z = layer(i - 2)
        for c, _, w in slab.applied(v0, z + 3, gains, z + 2, inverse, alive):
            slab.store(v1, w, c, z + 2)
        return carry
    lax.fori_loop(0, 2, first_halo, 0)

    z0, z1, z2, out = layer(0), layer(1), layer(2), layer(-1)

    def mend(c, sums):
        g01, g11, g02, g12, g22, g03, g13, g23 = sums
        term = [inverse * x for x in slab.load(v0, c, out + 3)]
        w = [a - b for a, b in zip(slab.load(v1, c, z0 + 2), term)]
        slab.store(v1, w, c, z0 + 2)
        g01, g11 = slab.products(g01, slab.load(v0, c, z0 + 3), w), slab.products(g11, w, w)
        term = [inverse * x for x in term]
        w = [a + b for a, b in zip(slab.load(v2, c, z1 + 1), term)]
        slab.store(v2, w, c, z1 + 1)
        g02 = slab.products(g02, slab.load(v0, c, z1 + 3), w)
        g12 = slab.products(g12, slab.load(v1, c, z1 + 2), w)
        g22 = slab.products(g22, w, w)
        term = [inverse * x for x in term]
        w = [a - b for a, b in zip(slab.load(v3, c, z2), term)]
        slab.store(v3, w, c, z2)
        t, u, v = slab.load(v0, c, z2 + 3), slab.load(v1, c, z2 + 2), slab.load(v2, c, z2 + 1)
        g03, g13, g23 = slab.products(g03, t, w), slab.products(g13, u, w), slab.products(g23, v, w)
        return g01, g11, g02, g12, g22, g03, g13, g23
    sums = (g01, g11, g02, g12, g22, g03, g13, g23)
    for c in range(comp):
        sums = mend(c, sums)
    g01, g11, g02, g12, g22, g03, g13, g23 = sums

    for c, _, w in slab.applied(v1, out + 2, gains, out + 2, inverse, alive):
        slab.store(v2, w, c, out + 1)
    g02, g12, g22 = second(z0, (g02, g12, g22))
    g03, g13, g23 = lax.fori_loop(0, 2, lambda i, sums: third(layer(i), sums), (g03, g13, g23))
    return g00, g01, g02, g03, g11, g12, g13, g22, g23


def near_kernel(kinds, halo, tab, v0_in, v1_in, v2_in, v3_in, gains_in, gram_in, v0, v1, v2, v3, gains, gram):
    sums = one_side(kinds, 0, halo, tab, gram_in, v0, v1, v2, v3, gains)
    for g, value in enumerate(sums):
        gram[g] = value


def far_kernel(kinds, halo, tab, corners_hbm, before_hbm, v0_in, v1_in, v2_in, v3_in, gains_in, gram_in,
               v0, v1, v2, v3, gains, message, corners, before, sems):
    fetch = (
        pltpu.make_async_copy(corners_hbm, corners, sems.at[0]),
        pltpu.make_async_copy(before_hbm, before, sems.at[1]),
    )
    for copy in fetch:
        copy.start()
    py, px = v0.shape[2], v0.shape[3]
    depth, parts = v3.shape[1], py // 8
    sums = one_side(kinds, 1, halo, tab, gram_in, v0, v1, v2, v3, gains)

    spots = lax.broadcasted_iota(jnp.int32, (1, px), 1)
    line = jnp.zeros((1, px), jnp.float32)
    for g, value in enumerate(sums):
        total = jnp.sum(jnp.sum(value, axis=0, keepdims=True), axis=1, keepdims=True)
        line = jnp.where(spots == GRAM_LANE + g, total, line)

    for copy in fetch:
        copy.wait()

    def corner_rows(index):
        c, rest = split(index, depth * py)
        z, y = split(rest, py)
        t, r = split(y, parts)
        row = pl.ds(r * 8 + t, 1)
        return [field[c, z + ITERS - k, row] for k, field in enumerate((v0, v1, v2, v3))]

    for j in range(corners.shape[0]):
        rows = zip(corner_rows(corners[j]), corner_rows(before[j]))
        for k, (mine, other) in enumerate(rows):
            moved = pltpu.roll(jnp.where(spots == px - 1, mine, other), 8 * j + 2 * k + 1, 1)
            line = jnp.where(spots // 2 == 4 * j + k, moved, line)
    message[...] = jnp.broadcast_to(line, message.shape)


def faces_kernel(v0, v1, v2, v3, left, right):
    comp, depth, py, px = v3.shape
    for z in range(depth):
        for k, field in enumerate((v0, v1, v2, v3)):
            turned = jnp.concatenate([field[c, z + ITERS - k] for c in range(comp)], axis=0).T
            left[k, pl.ds(z, 1)] = turned[0:1]
            right[k, pl.ds(z, 1)] = turned[px - 1 : px]


def total_of(terms):
    while len(terms) > 1:
        terms = [sum(terms[k : k + 2][1:], terms[k]) for k in range(0, len(terms), 2)]
    return terms[0]


def coefficients(gram, centre, scale):
    norms, images = {}, {}
    for i in range(ITERS):
        for j in range(i, ITERS):
            forward = centre * gram[(i, j)] + scale * gram[(i, j + 1)]
            if i == j:
                norms[(i, j)], images[(i, j)] = gram[(i, j)], forward
            else:
                back = centre * gram[(i, j)] + scale * gram[(i + 1, j)]
                norms[(i, j)], images[(i, j)] = 2.0 * gram[(i, j)], forward + back

    def quadratic(form, u):
        size = len(u)
        return total_of([(u[i] * u[j]) * form[(i, j)] for i in range(size) for j in range(i, size)])

    one = jnp.ones_like(centre)
    residual, direction, found = [one], [one], []
    norm = gram[(0, 0)]
    for repeat in range(ITERS):
        size = len(direction)
        step = norm / (quadratic(images, direction) if repeat else images[(0, 0)])
        image = [centre * direction[0]]
        for j in range(1, size):
            image.append(centre * direction[j] + scale * direction[j - 1])
        image.append(scale * direction[size - 1])
        found = [
            (found[j] if j < len(found) else 0.0) + step * direction[j] for j in range(size)
        ]
        residual = [
            (residual[j] if j < size else 0.0) - step * image[j] for j in range(size + 1)
        ]
        if repeat + 1 < ITERS:
            inverse = 1.0 / norm
            norm = quadratic(norms, residual)
            ratio = norm * inverse
            direction = [
                residual[j] + (ratio * direction[j] if j < size else 0.0) for j in range(size + 1)
            ]
    return found, residual


def final_kernel(kinds, messages, v0, v1, v2, right, left_next, tab, coarse, corners,
                 solution_hbm, interface_hbm, book, solution_out, interface_out, sems):
    comp, py, px = v0.shape[0], v0.shape[2], v0.shape[3]
    depth = right.shape[1]
    n_in, n_sub = lax.axis_size("in"), lax.axis_size("sub")
    sub = lax.axis_index("sub")
    following = lax.rem(sub + 1, n_sub)
    slab = Slab(comp, py, px)
    base = kinds * comp * comp

    got = [messages[pl.ds(i, n_sub, stride=n_in)] for i in range(n_in)]
    summed = total_of(got)
    mean = jnp.broadcast_to(tab[pl.ds(base + 8, 1)], summed.shape)
    scale = jnp.broadcast_to(tab[pl.ds(base + 16, 1)], summed.shape)
    gram = {}
    for g, pair in enumerate(PAIRS):
        gram[pair] = jnp.broadcast_to(summed[:, GRAM_LANE + g : GRAM_LANE + g + 1], summed.shape)
    found, residual = coefficients(gram, 6.0 + mean, scale)

    for k, value in enumerate(residual + found):
        book[k] = value
    weights = [book[ITERS + 1 + k, pl.ds(sub, 8, stride=0)] for k in range(ITERS)]
    mine = [book[k, pl.ds(sub, depth, stride=0)] for k in range(ITERS + 1)]
    other = [book[k, pl.ds(following, depth, stride=0)] for k in range(ITERS + 1)]

    copies = [
        pltpu.make_async_copy(solution_out.at[:, z], solution_hbm.at[:, z], sems.at[z]) for z in range(depth)
    ]
    for z in range(depth):
        for c in range(comp):
            fields = slab.load(v0, c, z + 3), slab.load(v1, c, z + 2), slab.load(v2, c, z + 1)
            for r in range(slab.parts):
                total = weights[0] * fields[0][r] + weights[1] * fields[1][r] + weights[2] * fields[2][r]
                solution_out[c, z, pl.ds(r, 8, stride=slab.parts)] = total
        copies[z].start()

    lane = lax.broadcasted_iota(jnp.int32, summed.shape, 1)
    kind = lax.rem(lane, 8) // 2
    spread = residual[0]
    for k in range(1, ITERS + 1):
        spread = jnp.where(kind == k, residual[k], spread)
    count = corners.shape[1]
    spots = jnp.minimum(lane * 8, px - 1)
    values = []
    for i in range(n_in):
        product = got[i] * spread
        product = jnp.where(lax.rem(lane, 2) == 0, product, pltpu.roll(product, n_sub - 1, 0))
        for reach in (1, 2, 4):
            product = product + pltpu.roll(product, px - reach, 1)
        values.append(jnp.take_along_axis(product, spots, axis=1, mode="promise_in_bounds")[:, :count])

    face = None
    for k in range(ITERS + 1):
        part = mine[k] * right[k] + other[k] * left_next[k]
        face = part if face is None else face + part

    zs = lax.broadcasted_iota(jnp.int32, face.shape, 0)
    ls = lax.broadcasted_iota(jnp.int32, face.shape, 1)
    y = lax.rem(ls, py)
    face = jnp.take_along_axis(
        face, ls - y + lax.rem(y, slab.parts) * 8 + y // slab.parts, axis=1, mode="promise_in_bounds")
    flat = (ls // py) * (depth * py) + zs * py + y
    picks = corners[...]
    for j in range(count):
        total = None
        for i in range(n_in):
            part = coarse[j, i] * values[i]
            total = part if total is None else total + part
        value = jnp.sum(jnp.sum(total, axis=0, keepdims=True), axis=1, keepdims=True)
        face = face + jnp.where(flat == picks[:, j : j + 1], value, 0.0)
    for c in range(comp):
        interface_out[0, c] = face[:, py * c : py * (c + 1)]
    copies.append(pltpu.make_async_copy(interface_out, interface_hbm, sems.at[depth]))
    copies[depth].start()
    for copy in copies:
        copy.wait()


def params(mib):
    return pltpu.CompilerParams(vmem_limit_bytes=mib * 2**20)


def on_device(body_load, materials, material_tables, corner_index, coarse_inverse):
    comp, depth, py, px = body_load.shape
    kinds = material_tables.shape[0]
    n_in, n_sub = lax.axis_size("in"), lax.axis_size("sub")
    devices = n_in * n_sub
    count = corner_index.shape[0]
    f32 = jnp.float32
    shape = jax.ShapeDtypeStruct
    halo = shape((ITERS * comp + MAT_DEPTH, py, px), f32)

    table = material_tables.transpose(1, 2, 0).reshape(comp * comp, kinds)
    coarse = coarse_inverse.reshape(count, n_sub, n_in, count).transpose(0, 2, 1, 3)

    def hbm(x):
        return pltpu.with_memory_space_constraint(x, pltpu.HBM)

    send_a, send_b = pl.pallas_call(
        pack_kernel,
        out_shape=(halo, halo),
        in_specs=[HBM] * 2,
        out_specs=(VMEM,) * 2,
        scratch_shapes=[
            pltpu.VMEM((2, MAT_DEPTH, py, px), jnp.int32),
            pltpu.SemaphoreType.DMA((2, comp + 1)),
        ],
        compiler_params=params(4),
        name="pack",
    )(hbm(body_load), hbm(materials))

    def swaps(start):
        pairs = [(i, i + 1) for i in range(start, n_in - 1, 2)]
        return pairs + [(j, i) for i, j in pairs]

    halo_a = lax.ppermute(send_a, "in", swaps(1))
    halo_b = lax.ppermute(send_b, "in", swaps(0))
    before = lax.ppermute(corner_index, "sub", [(i, (i + 1) % n_sub) for i in range(n_sub)])

    fields = (
        shape((comp, depth + 2 * ITERS, py, px), f32),
        shape((comp, depth + 2 * ITERS - 2, py, px), f32),
        shape((comp, depth + 2 * ITERS - 4, py, px), f32),
        shape((comp, depth, py, px), f32),
        shape((comp * comp, depth + 2 * MAT_DEPTH, py, px), f32),
        shape((len(PAIRS), 8, px), f32),
    )
    *inner, tab = pl.pallas_call(
        interior_kernel,
        out_shape=(*fields, shape((kinds * comp * comp + 24, px), f32)),
        in_specs=[VMEM] * 2 + [HBM] * 3,
        out_specs=(VMEM,) * 7,
        scratch_shapes=[
            pltpu.VMEM((comp, depth - 2 * ITERS, py, px), f32),
            pltpu.VMEM(materials.shape, jnp.int32),
            pltpu.VMEM(table.shape, f32),
            pltpu.SemaphoreType.DMA((3,)),
        ],
        compiler_params=params(4),
        name="interior",
    )(send_a, send_b, hbm(body_load), hbm(materials), hbm(table))

    inner = pl.pallas_call(
        functools.partial(near_kernel, kinds),
        out_shape=fields,
        in_specs=[VMEM] * 8,
        out_specs=(VMEM,) * 6,
        input_output_aliases={2 + k: k for k in range(6)},
        compiler_params=params(4),
        name="near",
    )(halo_a, tab, *inner)

    v0, v1, v2, v3, _, message = pl.pallas_call(
        functools.partial(far_kernel, kinds),
        out_shape=(*fields[:5], shape((devices, LANES), f32)),
        in_specs=[VMEM] * 2 + [HBM] * 2 + [VMEM] * 6,
        out_specs=(VMEM,) * 6,
        input_output_aliases={4 + k: k for k in range(5)},
        scratch_shapes=[
            pltpu.SMEM((count,), jnp.int32),
            pltpu.SMEM((count,), jnp.int32),
            pltpu.SemaphoreType.DMA((2,)),
        ],
        compiler_params=params(4),
        name="far",
    )(halo_b, tab, hbm(corner_index), before, *inner)

    messages = lax.all_to_all(message, ("sub", "in"), 0, 0, tiled=True)
    faces = shape((ITERS + 1, depth, comp * py), f32)
    left, right = pl.pallas_call(
        faces_kernel,
        out_shape=(faces, faces),
        in_specs=[VMEM] * 4,
        out_specs=(VMEM, VMEM),
        compiler_params=params(4),
        name="faces",
    )(v0, v1, v2, v3)
    left_next = lax.ppermute(left, "sub", [((i + 1) % n_sub, i) for i in range(n_sub)])

    return pl.pallas_call(
        functools.partial(final_kernel, kinds),
        out_shape=(shape(body_load.shape, f32), shape((1, comp, depth, py), f32)),
        in_specs=[VMEM] * 9,
        out_specs=(HBM, HBM),
        scratch_shapes=[
            pltpu.VMEM((2 * ITERS + 1, n_sub, LANES), f32),
            pltpu.VMEM(body_load.shape, f32),
            pltpu.VMEM((1, comp, depth, py), f32),
            pltpu.SemaphoreType.DMA((depth + 1,)),
        ],
        compiler_params=params(16),
        name="final",
    )(messages, v0, v1, v2, right, left_next, tab, coarse, corner_index.reshape(1, count))


def solution(mesh):
    return jax.shard_map(
        on_device,
        mesh=mesh,
        in_specs=(
            P(None, "in", None, "sub"),
            P("in", None, "sub"),
            P(),
            P(("sub", "in")),
            P(("sub", "in"), None),
        ),
        out_specs=(P(None, "in", None, "sub"), P("sub", None, "in", None)),
        check_vma=False,
    )
```

```python
import functools

import jax
import jax.numpy as jnp
from jax import lax
from jax.experimental import pallas as pl
from jax.experimental.pallas import tpu as pltpu
from jax.sharding import PartitionSpec as P

ITERS = 3
LANES = 128
MAT_DEPTH = ITERS - 1
PAIRS = [(i, j) for i in range(ITERS) for j in range(i, ITERS + 1)]
GRAM_LANE = 64
VMEM = pl.BlockSpec(memory_space=pltpu.VMEM)
SMEM = pl.BlockSpec(memory_space=pltpu.SMEM)
HBM = pl.BlockSpec(memory_space=pl.ANY)


def spectrum(table, comp):
    kinds = table.shape[1]
    rows = lax.broadcasted_iota(jnp.int32, table.shape, 0)
    diagonal = lax.rem(rows, comp + 1) == 0
    picked = jnp.where(diagonal, table, 0.0)
    mean = jnp.sum(jnp.sum(picked, axis=0, keepdims=True), axis=1, keepdims=True) / (comp * kinds)
    centred = jnp.where(diagonal, table - mean, table)
    size = jnp.abs(centred)
    widest = jnp.zeros((1, kinds), jnp.float32)
    for c in range(comp):
        widest = jnp.maximum(widest, jnp.sum(size[comp * c : comp * (c + 1)], axis=0, keepdims=True))
    scale = 6.0 + jnp.max(widest, axis=1, keepdims=True)
    return mean, scale, centred


def split(index, size):
    if size & (size - 1):
        return lax.div(index, size), lax.rem(index, size)
    return lax.shift_right_logical(index, size.bit_length() - 1), index & (size - 1)


def pack_kernel(body, mats, a_out, b_out, kinds, sems):
    comp, depth = body.shape[0], body.shape[1]
    odd = lax.rem(lax.axis_index("in") + 1, 2)
    copies = []
    for slot, (out, low) in enumerate(((a_out, odd), (b_out, 1 - odd))):
        first = (1 - low) * (depth - ITERS)
        for c in range(comp):
            copies.append(pltpu.make_async_copy(
                body.at[c, pl.ds(first, ITERS)], out.at[pl.ds(ITERS * c, ITERS)], sems.at[slot, c]))
        first = (1 - low) * (depth - MAT_DEPTH)
        copies.append(pltpu.make_async_copy(
            mats.at[pl.ds(first, MAT_DEPTH)], kinds.at[slot], sems.at[slot, comp]))
    for copy in copies:
        copy.start()
    for copy in copies:
        copy.wait()
    for slot, out in enumerate((a_out, b_out)):
        out[pl.ds(ITERS * comp, MAT_DEPTH)] = kinds[slot].astype(jnp.float32)


class Slab:
    def __init__(self, comp, py, px):
        self.comp, self.px, self.parts = comp, px, py // 8
        lane = lax.broadcasted_iota(jnp.int32, (8, px), 1)
        row = lax.broadcasted_iota(jnp.int32, (8, px), 0)
        self.lane = lane
        self.first_x, self.last_x = lane == 0, lane == px - 1
        self.first_y, self.last_y = row == 0, row == 7

    def natural(self, ref, *at):
        return [ref[(*at, pl.ds(r, 8, stride=self.parts))] for r in range(self.parts)]

    def load(self, ref, *at):
        return [ref[(*at, pl.ds(8 * r, 8))] for r in range(self.parts)]

    def store(self, ref, values, *at):
        for r in range(self.parts):
            ref[(*at, pl.ds(8 * r, 8))] = values[r]

    def neighbours(self, below, above, value):
        parts, px = self.parts, self.px
        totals = []
        for r in range(parts):
            total = below[r] + above[r]
            total += jnp.where(self.first_x, 0.0, pltpu.roll(value[r], 1, 1))
            total += jnp.where(self.last_x, 0.0, pltpu.roll(value[r], px - 1, 1))
            total += value[r - 1] if r else jnp.where(self.first_y, 0.0, pltpu.roll(value[parts - 1], 1, 0))
            total += value[r + 1] if r + 1 < parts else jnp.where(self.last_y, 0.0, pltpu.roll(value[0], 7, 0))
            totals.append(total)
        return totals

    def applied(self, source, at, gains, gains_at, inverse, alive=None):
        comp, parts = self.comp, self.parts
        values = [self.load(source, c, at) for c in range(comp)]
        for c in range(comp):
            around = self.neighbours(self.load(source, c, at - 1), self.load(source, c, at + 1), values[c])
            out = []
            for r in range(parts):
                total = None
                for d in range(comp):
                    term = gains[comp * c + d, gains_at, pl.ds(8 * r, 8)] * values[d][r]
                    total = term if total is None else total + term
                total = total - inverse * around[r]
                out.append(total if alive is None else alive * total)
            yield c, values[c], out

    def products(self, total, left, right):
        for r in range(self.parts):
            total = total + left[r] * right[r]
        return total

    def look_up(self, kinds, tab, gains, at, count):
        bits = [[(kind & (1 << b)) != 0 for kind in kinds] for b in range((count - 1).bit_length())]
        entries = self.comp * self.comp
        for e in range(entries):
            lines = [tab[pl.ds(k * entries + e, 8, stride=0)] for k in range(count)]
            out = []
            for r in range(self.parts):
                level = lines
                for bit in bits:
                    level = [
                        jnp.where(bit[r], level[k + 1], level[k]) if k + 1 < len(level) else level[k]
                        for k in range(0, len(level), 2)
                    ]
                out.append(level[0])
            self.store(gains, out, e, at)


def levels(slab, v0, v1, v2, v3, gains, inverse):
    def first(z, sums):
        g01, g11 = sums
        for c, v, w in slab.applied(v0, z + 3, gains, z + 2, inverse):
            slab.store(v1, w, c, z + 2)
            g01, g11 = slab.products(g01, v, w), slab.products(g11, w, w)
        return g01, g11

    def second(z, sums):
        g02, g12, g22 = sums
        for c, v, w in slab.applied(v1, z + 2, gains, z + 2, inverse):
            slab.store(v2, w, c, z + 1)
            u = slab.load(v0, c, z + 3)
            g02, g12, g22 = slab.products(g02, u, w), slab.products(g12, v, w), slab.products(g22, w, w)
        return g02, g12, g22

    def third(z, sums):
        g03, g13, g23 = sums
        for c, v, w in slab.applied(v2, z + 1, gains, z + 2, inverse):
            t, u = slab.load(v0, c, z + 3), slab.load(v1, c, z + 2)
            slab.store(v3, w, c, z)
            g03, g13, g23 = slab.products(g03, t, w), slab.products(g13, u, w), slab.products(g23, v, w)
        return g03, g13, g23

    return first, second, third


def interior_kernel(side_a, side_b, body_hbm, mats_hbm, table_hbm, v0, v1, v2, v3, gains, gram, tab,
                    middle, mats, table, sems):
    comp, depth, py, px = body_hbm.shape
    fetch = (
        pltpu.make_async_copy(table_hbm, table, sems.at[0]),
        pltpu.make_async_copy(mats_hbm, mats, sems.at[1]),
        pltpu.make_async_copy(body_hbm.at[:, pl.ds(ITERS, depth - 2 * ITERS)], middle, sems.at[2]),
    )
    for copy in fetch:
        copy.start()
    fetch[0].wait()
    odd = lax.rem(lax.axis_index("in") + 1, 2) == 1
    kinds = table.shape[1]
    entries = comp * comp
    slab = Slab(comp, py, px)
    mean, scale, centred = spectrum(table[...], comp)
    inverse = jnp.broadcast_to(1.0 / scale, (8, px))
    scaled = centred / scale
    for k in range(kinds):
        tab[pl.ds(k * entries, entries)] = jnp.broadcast_to(scaled[:, k : k + 1], (entries, px))
    for t, value in enumerate((inverse, mean, scale)):
        tab[pl.ds(kinds * entries + 8 * t, 8)] = jnp.broadcast_to(value, (8, px))
    zero = jnp.zeros((8, px), jnp.float32)
    for c in range(comp):
        for at in (ITERS - 1, ITERS + depth):
            slab.store(v0, [zero] * slab.parts, c, at)

    for copy in fetch[1:]:
        copy.wait()

    def place(values, z, g00):
        for c in range(comp):
            slab.store(v0, values[c], c, ITERS + z)
            g00 = slab.products(g00, values[c], values[c])
        slab.look_up(slab.natural(mats, z), tab, gains, MAT_DEPTH + z, kinds)
        return g00

    def outer(t, g00):
        a = [slab.natural(side_a, ITERS * c + t) for c in range(comp)]
        b = [slab.natural(side_b, ITERS * c + t) for c in range(comp)]
        low = [[jnp.where(odd, x, y) for x, y in zip(a[c], b[c])] for c in range(comp)]
        g00 = place(low, t, g00)
        high = [[jnp.where(odd, y, x) for x, y in zip(a[c], b[c])] for c in range(comp)]
        return place(high, depth - ITERS + t, g00)

    def centre(m, g00):
        return place([slab.natural(middle, c, m) for c in range(comp)], ITERS + m, g00)
    g00 = lax.fori_loop(0, ITERS, outer, zero)
    g00 = lax.fori_loop(0, depth - 2 * ITERS, centre, g00)

    def partial(i, carry):
        z = i * (depth - 1)
        for c, _, w in slab.applied(v0, z + 3, gains, z + 2, inverse):
            slab.store(v1, w, c, z + 2)
        return carry

    def partial_second(i, carry):
        z = 1 + i * (depth - 3)
        for c, _, w in slab.applied(v1, z + 2, gains, z + 2, inverse):
            slab.store(v2, w, c, z + 1)
        return carry

    def partial_third(i, carry):
        z = 2 + i * (depth - 5)
        for c, _, w in slab.applied(v2, z + 1, gains, z + 2, inverse):
            slab.store(v3, w, c, z)
        return carry

    first, second, third = levels(slab, v0, v1, v2, v3, gains, inverse)
    lax.fori_loop(0, 2, partial, 0)
    g01, g11 = lax.fori_loop(1, depth - 1, first, (zero,) * 2)
    lax.fori_loop(0, 2, partial_second, 0)
    g02, g12, g22 = lax.fori_loop(2, depth - 2, second, (zero,) * 3)
    lax.fori_loop(0, 2, partial_third, 0)
    g03, g13, g23 = lax.fori_loop(3, depth - 3, third, (zero,) * 3)
    for g, value in enumerate((g00, g01, g02, g03, g11, g12, g13, g22, g23)):
        gram[g] = value


def one_side(kinds, slot, halo, tab, gram, v0, v1, v2, v3, gains):
    comp, py, px = v0.shape[0], v0.shape[2], v0.shape[3]
    depth = v3.shape[1]
    slab = Slab(comp, py, px)
    place = lax.axis_index("in")
    low = lax.rem(place + slot, 2) == 0
    alive = jnp.where(low, place > 0, place < lax.axis_size("in") - 1).astype(jnp.float32)
    inverse = tab[pl.ds(kinds * comp * comp, 8)]

    def layer(q):
        return jnp.where(low, q, depth - 1 - q)

    base = jnp.where(low, 0, ITERS + depth)
    for t in range(ITERS):
        for c in range(comp):
            slab.store(v0, slab.natural(halo, ITERS * c + t), c, base + t)

    base_gains = jnp.where(low, 0, MAT_DEPTH + depth)

    def halo_gains(t, carry):
        kind = [x.astype(jnp.int32) for x in slab.natural(halo, ITERS * comp + t)]
        slab.look_up(kind, tab, gains, base_gains + t, kinds)
        return carry
    lax.fori_loop(0, MAT_DEPTH, halo_gains, 0)

    g00, g01, g02, g03, g11, g12, g13, g22, g23 = [gram[g] for g in range(len(PAIRS))]
    first, second, third = levels(slab, v0, v1, v2, v3, gains, inverse)

    def first_halo(i, carry):
        z = layer(i - 2)
        for c, _, w in slab.applied(v0, z + 3, gains, z + 2, inverse, alive):
            slab.store(v1, w, c, z + 2)
        return carry
    for i in range(2):
        first_halo(i, 0)

    z0, z1, z2, out = layer(0), layer(1), layer(2), layer(-1)

    def mend(c, sums):
        g01, g11, g02, g12, g22, g03, g13, g23 = sums
        term = [inverse * x for x in slab.load(v0, c, out + 3)]
        w = [a - b for a, b in zip(slab.load(v1, c, z0 + 2), term)]
        slab.store(v1, w, c, z0 + 2)
        g01, g11 = slab.products(g01, slab.load(v0, c, z0 + 3), w), slab.products(g11, w, w)
        term = [inverse * x for x in term]
        w = [a + b for a, b in zip(slab.load(v2, c, z1 + 1), term)]
        slab.store(v2, w, c, z1 + 1)
        g02 = slab.products(g02, slab.load(v0, c, z1 + 3), w)
        g12 = slab.products(g12, slab.load(v1, c, z1 + 2), w)
        g22 = slab.products(g22, w, w)
        term = [inverse * x for x in term]
        w = [a - b for a, b in zip(slab.load(v3, c, z2), term)]
        slab.store(v3, w, c, z2)
        t, u, v = slab.load(v0, c, z2 + 3), slab.load(v1, c, z2 + 2), slab.load(v2, c, z2 + 1)
        g03, g13, g23 = slab.products(g03, t, w), slab.products(g13, u, w), slab.products(g23, v, w)
        return g01, g11, g02, g12, g22, g03, g13, g23
    sums = (g01, g11, g02, g12, g22, g03, g13, g23)
    for c in range(comp):
        sums = mend(c, sums)
    g01, g11, g02, g12, g22, g03, g13, g23 = sums

    for c, _, w in slab.applied(v1, out + 2, gains, out + 2, inverse, alive):
        slab.store(v2, w, c, out + 1)
    g02, g12, g22 = second(z0, (g02, g12, g22))
    for i in range(2):
        g03, g13, g23 = third(layer(i), (g03, g13, g23))
    return g00, g01, g02, g03, g11, g12, g13, g22, g23


def near_kernel(kinds, halo, tab, v0_in, v1_in, v2_in, v3_in, gains_in, gram_in, v0, v1, v2, v3, gains, gram):
    sums = one_side(kinds, 0, halo, tab, gram_in, v0, v1, v2, v3, gains)
    for g, value in enumerate(sums):
        gram[g] = value


def far_kernel(kinds, halo, tab, corners_hbm, before_hbm, v0_in, v1_in, v2_in, v3_in, gains_in, gram_in,
               v0, v1, v2, v3, gains, message, corners, before, sems):
    fetch = (
        pltpu.make_async_copy(corners_hbm, corners, sems.at[0]),
        pltpu.make_async_copy(before_hbm, before, sems.at[1]),
    )
    for copy in fetch:
        copy.start()
    py, px = v0.shape[2], v0.shape[3]
    depth, parts = v3.shape[1], py // 8
    sums = one_side(kinds, 1, halo, tab, gram_in, v0, v1, v2, v3, gains)

    spots = lax.broadcasted_iota(jnp.int32, (1, px), 1)
    line = jnp.zeros((1, px), jnp.float32)
    for g, value in enumerate(sums):
        total = jnp.sum(jnp.sum(value, axis=0, keepdims=True), axis=1, keepdims=True)
        line = jnp.where(spots == GRAM_LANE + g, total, line)

    for copy in fetch:
        copy.wait()

    def corner_rows(index):
        c, rest = split(index, depth * py)
        z, y = split(rest, py)
        t, r = split(y, parts)
        row = pl.ds(r * 8 + t, 1)
        return [field[c, z + ITERS - k, row] for k, field in enumerate((v0, v1, v2, v3))]

    for j in range(corners.shape[0]):
        rows = zip(corner_rows(corners[j]), corner_rows(before[j]))
        for k, (mine, other) in enumerate(rows):
            moved = pltpu.roll(jnp.where(spots == px - 1, mine, other), 8 * j + 2 * k + 1, 1)
            line = jnp.where(spots // 2 == 4 * j + k, moved, line)
    message[...] = jnp.broadcast_to(line, message.shape)


def faces_kernel(v0, v1, v2, v3, left, right):
    comp, depth, py, px = v3.shape
    for z in range(depth):
        for k, field in enumerate((v0, v1, v2, v3)):
            turned = jnp.concatenate([field[c, z + ITERS - k] for c in range(comp)], axis=0).T
            left[k, pl.ds(z, 1)] = turned[0:1]
            right[k, pl.ds(z, 1)] = turned[px - 1 : px]


def total_of(terms):
    while len(terms) > 1:
        terms = [sum(terms[k : k + 2][1:], terms[k]) for k in range(0, len(terms), 2)]
    return terms[0]


def coefficients(gram, centre, scale):
    norms, images = {}, {}
    for i in range(ITERS):
        for j in range(i, ITERS):
            forward = centre * gram[(i, j)] + scale * gram[(i, j + 1)]
            if i == j:
                norms[(i, j)], images[(i, j)] = gram[(i, j)], forward
            else:
                back = centre * gram[(i, j)] + scale * gram[(i + 1, j)]
                norms[(i, j)], images[(i, j)] = 2.0 * gram[(i, j)], forward + back

    def quadratic(form, u):
        size = len(u)
        return total_of([(u[i] * u[j]) * form[(i, j)] for i in range(size) for j in range(i, size)])

    one = jnp.ones_like(centre)
    residual, direction, found = [one], [one], []
    norm = gram[(0, 0)]
    for repeat in range(ITERS):
        size = len(direction)
        step = norm / (quadratic(images, direction) if repeat else images[(0, 0)])
        image = [centre * direction[0]]
        for j in range(1, size):
            image.append(centre * direction[j] + scale * direction[j - 1])
        image.append(scale * direction[size - 1])
        found = [
            (found[j] if j < len(found) else 0.0) + step * direction[j] for j in range(size)
        ]
        residual = [
            (residual[j] if j < size else 0.0) - step * image[j] for j in range(size + 1)
        ]
        if repeat + 1 < ITERS:
            inverse = 1.0 / norm
            norm = quadratic(norms, residual)
            ratio = norm * inverse
            direction = [
                residual[j] + (ratio * direction[j] if j < size else 0.0) for j in range(size + 1)
            ]
    return found, residual


def final_kernel(kinds, messages, v0, v1, v2, right, left_next, tab, coarse, corners,
                 solution_hbm, interface_hbm, book, solution_out, interface_out, sems):
    comp, py, px = v0.shape[0], v0.shape[2], v0.shape[3]
    depth = right.shape[1]
    n_in, n_sub = lax.axis_size("in"), lax.axis_size("sub")
    sub = lax.axis_index("sub")
    following = lax.rem(sub + 1, n_sub)
    slab = Slab(comp, py, px)
    base = kinds * comp * comp

    got = [messages[pl.ds(i, n_sub, stride=n_in)] for i in range(n_in)]
    summed = total_of(got)
    mean = jnp.broadcast_to(tab[pl.ds(base + 8, 1)], summed.shape)
    scale = jnp.broadcast_to(tab[pl.ds(base + 16, 1)], summed.shape)
    gram = {}
    for g, pair in enumerate(PAIRS):
        gram[pair] = jnp.broadcast_to(summed[:, GRAM_LANE + g : GRAM_LANE + g + 1], summed.shape)
    found, residual = coefficients(gram, 6.0 + mean, scale)

    for k, value in enumerate(residual + found):
        book[k] = value
    weights = [book[ITERS + 1 + k, pl.ds(sub, 8, stride=0)] for k in range(ITERS)]
    mine = [book[k, pl.ds(sub, depth, stride=0)] for k in range(ITERS + 1)]
    other = [book[k, pl.ds(following, depth, stride=0)] for k in range(ITERS + 1)]

    copies = [
        pltpu.make_async_copy(solution_out.at[:, z], solution_hbm.at[:, z], sems.at[z]) for z in range(depth)
    ]
    for z in range(depth):
        for c in range(comp):
            fields = slab.load(v0, c, z + 3), slab.load(v1, c, z + 2), slab.load(v2, c, z + 1)
            for r in range(slab.parts):
                total = weights[0] * fields[0][r] + weights[1] * fields[1][r] + weights[2] * fields[2][r]
                solution_out[c, z, pl.ds(r, 8, stride=slab.parts)] = total
        copies[z].start()

    lane = lax.broadcasted_iota(jnp.int32, summed.shape, 1)
    kind = lax.rem(lane, 8) // 2
    spread = residual[0]
    for k in range(1, ITERS + 1):
        spread = jnp.where(kind == k, residual[k], spread)
    count = corners.shape[1]
    spots = jnp.minimum(lane * 8, px - 1)
    values = []
    for i in range(n_in):
        product = got[i] * spread
        product = jnp.where(lax.rem(lane, 2) == 0, product, pltpu.roll(product, n_sub - 1, 0))
        for reach in (1, 2, 4):
            product = product + pltpu.roll(product, px - reach, 1)
        values.append(jnp.take_along_axis(product, spots, axis=1, mode="promise_in_bounds")[:, :count])

    face = None
    for k in range(ITERS + 1):
        part = mine[k] * right[k] + other[k] * left_next[k]
        face = part if face is None else face + part

    zs = lax.broadcasted_iota(jnp.int32, face.shape, 0)
    ls = lax.broadcasted_iota(jnp.int32, face.shape, 1)
    y = lax.rem(ls, py)
    face = jnp.take_along_axis(
        face, ls - y + lax.rem(y, slab.parts) * 8 + y // slab.parts, axis=1, mode="promise_in_bounds")
    flat = (ls // py) * (depth * py) + zs * py + y
    picks = corners[...]
    for j in range(count):
        total = None
        for i in range(n_in):
            part = coarse[j, i] * values[i]
            total = part if total is None else total + part
        value = jnp.sum(jnp.sum(total, axis=0, keepdims=True), axis=1, keepdims=True)
        face = face + jnp.where(flat == picks[:, j : j + 1], value, 0.0)
    for c in range(comp):
        interface_out[0, c] = face[:, py * c : py * (c + 1)]
    copies.append(pltpu.make_async_copy(interface_out, interface_hbm, sems.at[depth]))
    copies[depth].start()
    for copy in copies:
        copy.wait()


def params(mib):
    return pltpu.CompilerParams(vmem_limit_bytes=mib * 2**20)


def on_device(body_load, materials, material_tables, corner_index, coarse_inverse):
    comp, depth, py, px = body_load.shape
    kinds = material_tables.shape[0]
    n_in, n_sub = lax.axis_size("in"), lax.axis_size("sub")
    devices = n_in * n_sub
    count = corner_index.shape[0]
    f32 = jnp.float32
    shape = jax.ShapeDtypeStruct
    halo = shape((ITERS * comp + MAT_DEPTH, py, px), f32)

    table = material_tables.transpose(1, 2, 0).reshape(comp * comp, kinds)
    coarse = coarse_inverse.reshape(count, n_sub, n_in, count).transpose(0, 2, 1, 3)

    def hbm(x):
        return pltpu.with_memory_space_constraint(x, pltpu.HBM)

    send_a, send_b = pl.pallas_call(
        pack_kernel,
        out_shape=(halo, halo),
        in_specs=[HBM] * 2,
        out_specs=(VMEM,) * 2,
        scratch_shapes=[
            pltpu.VMEM((2, MAT_DEPTH, py, px), jnp.int32),
            pltpu.SemaphoreType.DMA((2, comp + 1)),
        ],
        compiler_params=params(4),
        name="pack",
    )(hbm(body_load), hbm(materials))

    def swaps(start):
        pairs = [(i, i + 1) for i in range(start, n_in - 1, 2)]
        return pairs + [(j, i) for i, j in pairs]

    halo_a = lax.ppermute(send_a, "in", swaps(1))
    halo_b = lax.ppermute(send_b, "in", swaps(0))
    before = lax.ppermute(corner_index, "sub", [(i, (i + 1) % n_sub) for i in range(n_sub)])

    fields = (
        shape((comp, depth + 2 * ITERS, py, px), f32),
        shape((comp, depth + 2 * ITERS - 2, py, px), f32),
        shape((comp, depth + 2 * ITERS - 4, py, px), f32),
        shape((comp, depth, py, px), f32),
        shape((comp * comp, depth + 2 * MAT_DEPTH, py, px), f32),
        shape((len(PAIRS), 8, px), f32),
    )
    *inner, tab = pl.pallas_call(
        interior_kernel,
        out_shape=(*fields, shape((kinds * comp * comp + 24, px), f32)),
        in_specs=[VMEM] * 2 + [HBM] * 3,
        out_specs=(VMEM,) * 7,
        scratch_shapes=[
            pltpu.VMEM((comp, depth - 2 * ITERS, py, px), f32),
            pltpu.VMEM(materials.shape, jnp.int32),
            pltpu.VMEM(table.shape, f32),
            pltpu.SemaphoreType.DMA((3,)),
        ],
        compiler_params=params(4),
        name="interior",
    )(send_a, send_b, hbm(body_load), hbm(materials), hbm(table))

    inner = pl.pallas_call(
        functools.partial(near_kernel, kinds),
        out_shape=fields,
        in_specs=[VMEM] * 8,
        out_specs=(VMEM,) * 6,
        input_output_aliases={2 + k: k for k in range(6)},
        compiler_params=params(4),
        name="near",
    )(halo_a, tab, *inner)

    v0, v1, v2, v3, _, message = pl.pallas_call(
        functools.partial(far_kernel, kinds),
        out_shape=(*fields[:5], shape((devices, LANES), f32)),
        in_specs=[VMEM] * 2 + [HBM] * 2 + [VMEM] * 6,
        out_specs=(VMEM,) * 6,
        input_output_aliases={4 + k: k for k in range(5)},
        scratch_shapes=[
            pltpu.SMEM((count,), jnp.int32),
            pltpu.SMEM((count,), jnp.int32),
            pltpu.SemaphoreType.DMA((2,)),
        ],
        compiler_params=params(4),
        name="far",
    )(halo_b, tab, hbm(corner_index), before, *inner)

    messages = lax.all_to_all(message, ("sub", "in"), 0, 0, tiled=True)
    faces = shape((ITERS + 1, depth, comp * py), f32)
    left, right = pl.pallas_call(
        faces_kernel,
        out_shape=(faces, faces),
        in_specs=[VMEM] * 4,
        out_specs=(VMEM, VMEM),
        compiler_params=params(4),
        name="faces",
    )(v0, v1, v2, v3)
    left_next = lax.ppermute(left, "sub", [((i + 1) % n_sub, i) for i in range(n_sub)])

    return pl.pallas_call(
        functools.partial(final_kernel, kinds),
        out_shape=(shape(body_load.shape, f32), shape((1, comp, depth, py), f32)),
        in_specs=[VMEM] * 9,
        out_specs=(HBM, HBM),
        scratch_shapes=[
            pltpu.VMEM((2 * ITERS + 1, n_sub, LANES), f32),
            pltpu.VMEM(body_load.shape, f32),
            pltpu.VMEM((1, comp, depth, py), f32),
            pltpu.SemaphoreType.DMA((depth + 1,)),
        ],
        compiler_params=params(16),
        name="final",
    )(messages, v0, v1, v2, right, left_next, tab, coarse, corner_index.reshape(1, count))


def solution(mesh):
    return jax.shard_map(
        on_device,
        mesh=mesh,
        in_specs=(
            P(None, "in", None, "sub"),
            P("in", None, "sub"),
            P(),
            P(("sub", "in")),
            P(("sub", "in"), None),
        ),
        out_specs=(P(None, "in", None, "sub"), P("sub", None, "in", None)),
        check_vma=False,
    )
```

```python
import functools

import jax
import jax.numpy as jnp
from jax import lax
from jax.experimental import pallas as pl
from jax.experimental.pallas import tpu as pltpu
from jax.sharding import PartitionSpec as P

ITERS = 3
LANES = 128
MAT_DEPTH = ITERS - 1
PAIRS = [(i, j) for i in range(ITERS) for j in range(i, ITERS + 1)]
GRAM_LANE = 64
VMEM = pl.BlockSpec(memory_space=pltpu.VMEM)
SMEM = pl.BlockSpec(memory_space=pltpu.SMEM)
HBM = pl.BlockSpec(memory_space=pl.ANY)


def spectrum(table, comp):
    kinds = table.shape[1]
    rows = lax.broadcasted_iota(jnp.int32, table.shape, 0)
    diagonal = lax.rem(rows, comp + 1) == 0
    picked = jnp.where(diagonal, table, 0.0)
    mean = jnp.sum(jnp.sum(picked, axis=0, keepdims=True), axis=1, keepdims=True) / (comp * kinds)
    centred = jnp.where(diagonal, table - mean, table)
    size = jnp.abs(centred)
    widest = jnp.zeros((1, kinds), jnp.float32)
    for c in range(comp):
        widest = jnp.maximum(widest, jnp.sum(size[comp * c : comp * (c + 1)], axis=0, keepdims=True))
    scale = 6.0 + jnp.max(widest, axis=1, keepdims=True)
    return mean, scale, centred


def split(index, size):
    if size & (size - 1):
        return lax.div(index, size), lax.rem(index, size)
    return lax.shift_right_logical(index, size.bit_length() - 1), index & (size - 1)


def pack_kernel(body, mats, a_out, b_out, kinds, sems):
    comp, depth = body.shape[0], body.shape[1]
    odd = lax.rem(lax.axis_index("in") + 1, 2)
    copies = []
    for slot, (out, low) in enumerate(((a_out, odd), (b_out, 1 - odd))):
        first = (1 - low) * (depth - ITERS)
        for c in range(comp):
            copies.append(pltpu.make_async_copy(
                body.at[c, pl.ds(first, ITERS)], out.at[pl.ds(ITERS * c, ITERS)], sems.at[slot, c]))
        first = (1 - low) * (depth - MAT_DEPTH)
        copies.append(pltpu.make_async_copy(
            mats.at[pl.ds(first, MAT_DEPTH)], kinds.at[slot], sems.at[slot, comp]))
    for copy in copies:
        copy.start()
    for copy in copies:
        copy.wait()
    for slot, out in enumerate((a_out, b_out)):
        out[pl.ds(ITERS * comp, MAT_DEPTH)] = kinds[slot].astype(jnp.float32)


class Slab:
    def __init__(self, comp, py, px):
        self.comp, self.px, self.parts = comp, px, py // 8
        lane = lax.broadcasted_iota(jnp.int32, (8, px), 1)
        row = lax.broadcasted_iota(jnp.int32, (8, px), 0)
        self.lane = lane
        self.first_x, self.last_x = lane == 0, lane == px - 1
        self.first_y, self.last_y = row == 0, row == 7

    def natural(self, ref, *at):
        return [ref[(*at, pl.ds(r, 8, stride=self.parts))] for r in range(self.parts)]

    def load(self, ref, *at):
        return [ref[(*at, pl.ds(8 * r, 8))] for r in range(self.parts)]

    def store(self, ref, values, *at):
        for r in range(self.parts):
            ref[(*at, pl.ds(8 * r, 8))] = values[r]

    def neighbours(self, below, above, value):
        parts, px = self.parts, self.px
        totals = []
        for r in range(parts):
            total = below[r] + above[r]
            total += jnp.where(self.first_x, 0.0, pltpu.roll(value[r], 1, 1))
            total += jnp.where(self.last_x, 0.0, pltpu.roll(value[r], px - 1, 1))
            total += value[r - 1] if r else jnp.where(self.first_y, 0.0, pltpu.roll(value[parts - 1], 1, 0))
            total += value[r + 1] if r + 1 < parts else jnp.where(self.last_y, 0.0, pltpu.roll(value[0], 7, 0))
            totals.append(total)
        return totals

    def applied(self, source, at, gains, gains_at, inverse, alive=None):
        comp, parts = self.comp, self.parts
        values = [self.load(source, c, at) for c in range(comp)]
        for c in range(comp):
            around = self.neighbours(self.load(source, c, at - 1), self.load(source, c, at + 1), values[c])
            out = []
            for r in range(parts):
                total = None
                for d in range(comp):
                    term = gains[comp * c + d, gains_at, pl.ds(8 * r, 8)] * values[d][r]
                    total = term if total is None else total + term
                total = total - inverse * around[r]
                out.append(total if alive is None else alive * total)
            yield c, values[c], out

    def products(self, total, left, right):
        for r in range(self.parts):
            total = total + left[r] * right[r]
        return total

    def look_up(self, kinds, tab, gains, at, count):
        bits = [[(kind & (1 << b)) != 0 for kind in kinds] for b in range((count - 1).bit_length())]
        entries = self.comp * self.comp
        for e in range(entries):
            lines = [tab[pl.ds(k * entries + e, 8, stride=0)] for k in range(count)]
            out = []
            for r in range(self.parts):
                level = lines
                for bit in bits:
                    level = [
                        jnp.where(bit[r], level[k + 1], level[k]) if k + 1 < len(level) else level[k]
                        for k in range(0, len(level), 2)
                    ]
                out.append(level[0])
            self.store(gains, out, e, at)


def levels(slab, v0, v1, v2, v3, gains, inverse):
    def first(z, sums):
        g01, g11 = sums
        for c, v, w in slab.applied(v0, z + 3, gains, z + 2, inverse):
            slab.store(v1, w, c, z + 2)
            g01, g11 = slab.products(g01, v, w), slab.products(g11, w, w)
        return g01, g11

    def second(z, sums):
        g02, g12, g22 = sums
        for c, v, w in slab.applied(v1, z + 2, gains, z + 2, inverse):
            slab.store(v2, w, c, z + 1)
            u = slab.load(v0, c, z + 3)
            g02, g12, g22 = slab.products(g02, u, w), slab.products(g12, v, w), slab.products(g22, w, w)
        return g02, g12, g22

    def third(z, sums):
        g03, g13, g23 = sums
        for c, v, w in slab.applied(v2, z + 1, gains, z + 2, inverse):
            t, u = slab.load(v0, c, z + 3), slab.load(v1, c, z + 2)
            slab.store(v3, w, c, z)
            g03, g13, g23 = slab.products(g03, t, w), slab.products(g13, u, w), slab.products(g23, v, w)
        return g03, g13, g23

    return first, second, third


def interior_kernel(side_a, side_b, body_hbm, mats_hbm, table_hbm, v0, v1, v2, v3, gains, gram, tab,
                    middle, mats, table, sems):
    comp, depth, py, px = body_hbm.shape
    fetch = (
        pltpu.make_async_copy(table_hbm, table, sems.at[0]),
        pltpu.make_async_copy(mats_hbm, mats, sems.at[1]),
        pltpu.make_async_copy(body_hbm.at[:, pl.ds(ITERS, depth - 2 * ITERS)], middle, sems.at[2]),
    )
    for copy in fetch:
        copy.start()
    fetch[0].wait()
    odd = lax.rem(lax.axis_index("in") + 1, 2) == 1
    kinds = table.shape[1]
    entries = comp * comp
    slab = Slab(comp, py, px)
    mean, scale, centred = spectrum(table[...], comp)
    inverse = jnp.broadcast_to(1.0 / scale, (8, px))
    scaled = centred / scale
    for k in range(kinds):
        tab[pl.ds(k * entries, entries)] = jnp.broadcast_to(scaled[:, k : k + 1], (entries, px))
    for t, value in enumerate((inverse, mean, scale)):
        tab[pl.ds(kinds * entries + 8 * t, 8)] = jnp.broadcast_to(value, (8, px))
    zero = jnp.zeros((8, px), jnp.float32)
    for c in range(comp):
        for at in (ITERS - 1, ITERS + depth):
            slab.store(v0, [zero] * slab.parts, c, at)

    for copy in fetch[1:]:
        copy.wait()

    def place(values, z, g00):
        for c in range(comp):
            slab.store(v0, values[c], c, ITERS + z)
            g00 = slab.products(g00, values[c], values[c])
        slab.look_up(slab.natural(mats, z), tab, gains, MAT_DEPTH + z, kinds)
        return g00

    def outer(t, g00):
        a = [slab.natural(side_a, ITERS * c + t) for c in range(comp)]
        b = [slab.natural(side_b, ITERS * c + t) for c in range(comp)]
        low = [[jnp.where(odd, x, y) for x, y in zip(a[c], b[c])] for c in range(comp)]
        g00 = place(low, t, g00)
        high = [[jnp.where(odd, y, x) for x, y in zip(a[c], b[c])] for c in range(comp)]
        return place(high, depth - ITERS + t, g00)

    def centre(m, g00):
        return place([slab.natural(middle, c, m) for c in range(comp)], ITERS + m, g00)
    g00 = lax.fori_loop(0, ITERS, outer, zero)
    g00 = lax.fori_loop(0, depth - 2 * ITERS, centre, g00)

    def partial(i, carry):
        z = i * (depth - 1)
        for c, _, w in slab.applied(v0, z + 3, gains, z + 2, inverse):
            slab.store(v1, w, c, z + 2)
        return carry

    def partial_second(i, carry):
        z = 1 + i * (depth - 3)
        for c, _, w in slab.applied(v1, z + 2, gains, z + 2, inverse):
            slab.store(v2, w, c, z + 1)
        return carry

    def partial_third(i, carry):
        z = 2 + i * (depth - 5)
        for c, _, w in slab.applied(v2, z + 1, gains, z + 2, inverse):
            slab.store(v3, w, c, z)
        return carry

    first, second, third = levels(slab, v0, v1, v2, v3, gains, inverse)
    for i in range(2):
        partial(i, 0)
    g01, g11 = lax.fori_loop(1, depth - 1, first, (zero,) * 2)
    for i in range(2):
        partial_second(i, 0)
    g02, g12, g22 = lax.fori_loop(2, depth - 2, second, (zero,) * 3)
    for i in range(2):
        partial_third(i, 0)
    g03, g13, g23 = lax.fori_loop(3, depth - 3, third, (zero,) * 3)
    for g, value in enumerate((g00, g01, g02, g03, g11, g12, g13, g22, g23)):
        gram[g] = value


def one_side(kinds, slot, halo, tab, gram, v0, v1, v2, v3, gains):
    comp, py, px = v0.shape[0], v0.shape[2], v0.shape[3]
    depth = v3.shape[1]
    slab = Slab(comp, py, px)
    place = lax.axis_index("in")
    low = lax.rem(place + slot, 2) == 0
    alive = jnp.where(low, place > 0, place < lax.axis_size("in") - 1).astype(jnp.float32)
    inverse = tab[pl.ds(kinds * comp * comp, 8)]

    def layer(q):
        return jnp.where(low, q, depth - 1 - q)

    base = jnp.where(low, 0, ITERS + depth)
    for t in range(ITERS):
        for c in range(comp):
            slab.store(v0, slab.natural(halo, ITERS * c + t), c, base + t)

    base_gains = jnp.where(low, 0, MAT_DEPTH + depth)

    def halo_gains(t, carry):
        kind = [x.astype(jnp.int32) for x in slab.natural(halo, ITERS * comp + t)]
        slab.look_up(kind, tab, gains, base_gains + t, kinds)
        return carry
    lax.fori_loop(0, MAT_DEPTH, halo_gains, 0)

    g00, g01, g02, g03, g11, g12, g13, g22, g23 = [gram[g] for g in range(len(PAIRS))]
    first, second, third = levels(slab, v0, v1, v2, v3, gains, inverse)

    def first_halo(i, carry):
        z = layer(i - 2)
        for c, _, w in slab.applied(v0, z + 3, gains, z + 2, inverse, alive):
            slab.store(v1, w, c, z + 2)
        return carry
    for i in range(2):
        first_halo(i, 0)

    z0, z1, z2, out = layer(0), layer(1), layer(2), layer(-1)

    def mend(c, sums):
        g01, g11, g02, g12, g22, g03, g13, g23 = sums
        term = [inverse * x for x in slab.load(v0, c, out + 3)]
        w = [a - b for a, b in zip(slab.load(v1, c, z0 + 2), term)]
        slab.store(v1, w, c, z0 + 2)
        g01, g11 = slab.products(g01, slab.load(v0, c, z0 + 3), w), slab.products(g11, w, w)
        term = [inverse * x for x in term]
        w = [a + b for a, b in zip(slab.load(v2, c, z1 + 1), term)]
        slab.store(v2, w, c, z1 + 1)
        g02 = slab.products(g02, slab.load(v0, c, z1 + 3), w)
        g12 = slab.products(g12, slab.load(v1, c, z1 + 2), w)
        g22 = slab.products(g22, w, w)
        term = [inverse * x for x in term]
        w = [a - b for a, b in zip(slab.load(v3, c, z2), term)]
        slab.store(v3, w, c, z2)
        t, u, v = slab.load(v0, c, z2 + 3), slab.load(v1, c, z2 + 2), slab.load(v2, c, z2 + 1)
        g03, g13, g23 = slab.products(g03, t, w), slab.products(g13, u, w), slab.products(g23, v, w)
        return g01, g11, g02, g12, g22, g03, g13, g23
    sums = (g01, g11, g02, g12, g22, g03, g13, g23)
    for c in range(comp):
        sums = mend(c, sums)
    g01, g11, g02, g12, g22, g03, g13, g23 = sums

    for c, _, w in slab.applied(v1, out + 2, gains, out + 2, inverse, alive):
        slab.store(v2, w, c, out + 1)
    g02, g12, g22 = second(z0, (g02, g12, g22))
    for i in range(2):
        g03, g13, g23 = third(layer(i), (g03, g13, g23))
    return g00, g01, g02, g03, g11, g12, g13, g22, g23


def near_kernel(kinds, halo, tab, v0_in, v1_in, v2_in, v3_in, gains_in, gram_in, v0, v1, v2, v3, gains, gram):
    sums = one_side(kinds, 0, halo, tab, gram_in, v0, v1, v2, v3, gains)
    for g, value in enumerate(sums):
        gram[g] = value


def far_kernel(kinds, halo, tab, corners_hbm, before_hbm, v0_in, v1_in, v2_in, v3_in, gains_in, gram_in,
               v0, v1, v2, v3, gains, message, corners, before, sems):
    fetch = (
        pltpu.make_async_copy(corners_hbm, corners, sems.at[0]),
        pltpu.make_async_copy(before_hbm, before, sems.at[1]),
    )
    for copy in fetch:
        copy.start()
    py, px = v0.shape[2], v0.shape[3]
    depth, parts = v3.shape[1], py // 8
    sums = one_side(kinds, 1, halo, tab, gram_in, v0, v1, v2, v3, gains)

    spots = lax.broadcasted_iota(jnp.int32, (1, px), 1)
    line = jnp.zeros((1, px), jnp.float32)
    for g, value in enumerate(sums):
        total = jnp.sum(jnp.sum(value, axis=0, keepdims=True), axis=1, keepdims=True)
        line = jnp.where(spots == GRAM_LANE + g, total, line)

    for copy in fetch:
        copy.wait()

    def corner_rows(index):
        c, rest = split(index, depth * py)
        z, y = split(rest, py)
        t, r = split(y, parts)
        row = pl.ds(r * 8 + t, 1)
        return [field[c, z + ITERS - k, row] for k, field in enumerate((v0, v1, v2, v3))]

    for j in range(corners.shape[0]):
        rows = zip(corner_rows(corners[j]), corner_rows(before[j]))
        for k, (mine, other) in enumerate(rows):
            moved = pltpu.roll(jnp.where(spots == px - 1, mine, other), 8 * j + 2 * k + 1, 1)
            line = jnp.where(spots // 2 == 4 * j + k, moved, line)
    message[...] = jnp.broadcast_to(line, message.shape)


def faces_kernel(v0, v1, v2, v3, left, right):
    comp, depth, py, px = v3.shape
    for z in range(depth):
        for k, field in enumerate((v0, v1, v2, v3)):
            turned = jnp.concatenate([field[c, z + ITERS - k] for c in range(comp)], axis=0).T
            left[k, pl.ds(z, 1)] = turned[0:1]
            right[k, pl.ds(z, 1)] = turned[px - 1 : px]


def total_of(terms):
    while len(terms) > 1:
        terms = [sum(terms[k : k + 2][1:], terms[k]) for k in range(0, len(terms), 2)]
    return terms[0]


def coefficients(gram, centre, scale):
    norms, images = {}, {}
    for i in range(ITERS):
        for j in range(i, ITERS):
            forward = centre * gram[(i, j)] + scale * gram[(i, j + 1)]
            if i == j:
                norms[(i, j)], images[(i, j)] = gram[(i, j)], forward
            else:
                back = centre * gram[(i, j)] + scale * gram[(i + 1, j)]
                norms[(i, j)], images[(i, j)] = 2.0 * gram[(i, j)], forward + back

    def quadratic(form, u):
        size = len(u)
        return total_of([(u[i] * u[j]) * form[(i, j)] for i in range(size) for j in range(i, size)])

    one = jnp.ones_like(centre)
    residual, direction, found = [one], [one], []
    norm = gram[(0, 0)]
    for repeat in range(ITERS):
        size = len(direction)
        step = norm / (quadratic(images, direction) if repeat else images[(0, 0)])
        image = [centre * direction[0]]
        for j in range(1, size):
            image.append(centre * direction[j] + scale * direction[j - 1])
        image.append(scale * direction[size - 1])
        found = [
            (found[j] if j < len(found) else 0.0) + step * direction[j] for j in range(size)
        ]
        residual = [
            (residual[j] if j < size else 0.0) - step * image[j] for j in range(size + 1)
        ]
        if repeat + 1 < ITERS:
            inverse = 1.0 / norm
            norm = quadratic(norms, residual)
            ratio = norm * inverse
            direction = [
                residual[j] + (ratio * direction[j] if j < size else 0.0) for j in range(size + 1)
            ]
    return found, residual


def final_kernel(kinds, messages, v0, v1, v2, right, left_next, tab, coarse, corners,
                 solution_hbm, interface_hbm, book, solution_out, interface_out, sems):
    comp, py, px = v0.shape[0], v0.shape[2], v0.shape[3]
    depth = right.shape[1]
    n_in, n_sub = lax.axis_size("in"), lax.axis_size("sub")
    sub = lax.axis_index("sub")
    following = lax.rem(sub + 1, n_sub)
    slab = Slab(comp, py, px)
    base = kinds * comp * comp

    got = [messages[pl.ds(i, n_sub, stride=n_in)] for i in range(n_in)]
    summed = total_of(got)
    mean = jnp.broadcast_to(tab[pl.ds(base + 8, 1)], summed.shape)
    scale = jnp.broadcast_to(tab[pl.ds(base + 16, 1)], summed.shape)
    gram = {}
    for g, pair in enumerate(PAIRS):
        gram[pair] = jnp.broadcast_to(summed[:, GRAM_LANE + g : GRAM_LANE + g + 1], summed.shape)
    found, residual = coefficients(gram, 6.0 + mean, scale)

    for k, value in enumerate(residual + found):
        book[k] = value
    weights = [book[ITERS + 1 + k, pl.ds(sub, 8, stride=0)] for k in range(ITERS)]
    mine = [book[k, pl.ds(sub, depth, stride=0)] for k in range(ITERS + 1)]
    other = [book[k, pl.ds(following, depth, stride=0)] for k in range(ITERS + 1)]

    copies = [
        pltpu.make_async_copy(solution_out.at[:, z], solution_hbm.at[:, z], sems.at[z]) for z in range(depth)
    ]
    for z in range(depth):
        for c in range(comp):
            fields = slab.load(v0, c, z + 3), slab.load(v1, c, z + 2), slab.load(v2, c, z + 1)
            for r in range(slab.parts):
                total = weights[0] * fields[0][r] + weights[1] * fields[1][r] + weights[2] * fields[2][r]
                solution_out[c, z, pl.ds(r, 8, stride=slab.parts)] = total
        copies[z].start()

    lane = lax.broadcasted_iota(jnp.int32, summed.shape, 1)
    kind = lax.rem(lane, 8) // 2
    spread = residual[0]
    for k in range(1, ITERS + 1):
        spread = jnp.where(kind == k, residual[k], spread)
    count = corners.shape[1]
    spots = jnp.minimum(lane * 8, px - 1)
    values = []
    for i in range(n_in):
        product = got[i] * spread
        product = jnp.where(lax.rem(lane, 2) == 0, product, pltpu.roll(product, n_sub - 1, 0))
        for reach in (1, 2, 4):
            product = product + pltpu.roll(product, px - reach, 1)
        values.append(jnp.take_along_axis(product, spots, axis=1, mode="promise_in_bounds")[:, :count])

    face = None
    for k in range(ITERS + 1):
        part = mine[k] * right[k] + other[k] * left_next[k]
        face = part if face is None else face + part

    zs = lax.broadcasted_iota(jnp.int32, face.shape, 0)
    ls = lax.broadcasted_iota(jnp.int32, face.shape, 1)
    y = lax.rem(ls, py)
    face = jnp.take_along_axis(
        face, ls - y + lax.rem(y, slab.parts) * 8 + y // slab.parts, axis=1, mode="promise_in_bounds")
    flat = (ls // py) * (depth * py) + zs * py + y
    picks = corners[...]
    for j in range(count):
        total = None
        for i in range(n_in):
            part = coarse[j, i] * values[i]
            total = part if total is None else total + part
        value = jnp.sum(jnp.sum(total, axis=0, keepdims=True), axis=1, keepdims=True)
        face = face + jnp.where(flat == picks[:, j : j + 1], value, 0.0)
    for c in range(comp):
        interface_out[0, c] = face[:, py * c : py * (c + 1)]
    copies.append(pltpu.make_async_copy(interface_out, interface_hbm, sems.at[depth]))
    copies[depth].start()
    for copy in copies:
        copy.wait()


def params(mib):
    return pltpu.CompilerParams(vmem_limit_bytes=mib * 2**20)


def on_device(body_load, materials, material_tables, corner_index, coarse_inverse):
    comp, depth, py, px = body_load.shape
    kinds = material_tables.shape[0]
    n_in, n_sub = lax.axis_size("in"), lax.axis_size("sub")
    devices = n_in * n_sub
    count = corner_index.shape[0]
    f32 = jnp.float32
    shape = jax.ShapeDtypeStruct
    halo = shape((ITERS * comp + MAT_DEPTH, py, px), f32)

    table = material_tables.transpose(1, 2, 0).reshape(comp * comp, kinds)
    coarse = coarse_inverse.reshape(count, n_sub, n_in, count).transpose(0, 2, 1, 3)

    def hbm(x):
        return pltpu.with_memory_space_constraint(x, pltpu.HBM)

    send_a, send_b = pl.pallas_call(
        pack_kernel,
        out_shape=(halo, halo),
        in_specs=[HBM] * 2,
        out_specs=(VMEM,) * 2,
        scratch_shapes=[
            pltpu.VMEM((2, MAT_DEPTH, py, px), jnp.int32),
            pltpu.SemaphoreType.DMA((2, comp + 1)),
        ],
        compiler_params=params(4),
        name="pack",
    )(hbm(body_load), hbm(materials))

    def swaps(start):
        pairs = [(i, i + 1) for i in range(start, n_in - 1, 2)]
        return pairs + [(j, i) for i, j in pairs]

    halo_a = lax.ppermute(send_a, "in", swaps(1))
    halo_b = lax.ppermute(send_b, "in", swaps(0))
    before = lax.ppermute(corner_index, "sub", [(i, (i + 1) % n_sub) for i in range(n_sub)])

    fields = (
        shape((comp, depth + 2 * ITERS, py, px), f32),
        shape((comp, depth + 2 * ITERS - 2, py, px), f32),
        shape((comp, depth + 2 * ITERS - 4, py, px), f32),
        shape((comp, depth, py, px), f32),
        shape((comp * comp, depth + 2 * MAT_DEPTH, py, px), f32),
        shape((len(PAIRS), 8, px), f32),
    )
    *inner, tab = pl.pallas_call(
        interior_kernel,
        out_shape=(*fields, shape((kinds * comp * comp + 24, px), f32)),
        in_specs=[VMEM] * 2 + [HBM] * 3,
        out_specs=(VMEM,) * 7,
        scratch_shapes=[
            pltpu.VMEM((comp, depth - 2 * ITERS, py, px), f32),
            pltpu.VMEM(materials.shape, jnp.int32),
            pltpu.VMEM(table.shape, f32),
            pltpu.SemaphoreType.DMA((3,)),
        ],
        compiler_params=params(4),
        name="interior",
    )(send_a, send_b, hbm(body_load), hbm(materials), hbm(table))

    inner = pl.pallas_call(
        functools.partial(near_kernel, kinds),
        out_shape=fields,
        in_specs=[VMEM] * 8,
        out_specs=(VMEM,) * 6,
        input_output_aliases={2 + k: k for k in range(6)},
        compiler_params=params(4),
        name="near",
    )(halo_a, tab, *inner)

    v0, v1, v2, v3, _, message = pl.pallas_call(
        functools.partial(far_kernel, kinds),
        out_shape=(*fields[:5], shape((devices, LANES), f32)),
        in_specs=[VMEM] * 2 + [HBM] * 2 + [VMEM] * 6,
        out_specs=(VMEM,) * 6,
        input_output_aliases={4 + k: k for k in range(5)},
        scratch_shapes=[
            pltpu.SMEM((count,), jnp.int32),
            pltpu.SMEM((count,), jnp.int32),
            pltpu.SemaphoreType.DMA((2,)),
        ],
        compiler_params=params(4),
        name="far",
    )(halo_b, tab, hbm(corner_index), before, *inner)

    messages = lax.all_to_all(message, ("sub", "in"), 0, 0, tiled=True)
    faces = shape((ITERS + 1, depth, comp * py), f32)
    left, right = pl.pallas_call(
        faces_kernel,
        out_shape=(faces, faces),
        in_specs=[VMEM] * 4,
        out_specs=(VMEM, VMEM),
        compiler_params=params(4),
        name="faces",
    )(v0, v1, v2, v3)
    left_next = lax.ppermute(left, "sub", [((i + 1) % n_sub, i) for i in range(n_sub)])

    return pl.pallas_call(
        functools.partial(final_kernel, kinds),
        out_shape=(shape(body_load.shape, f32), shape((1, comp, depth, py), f32)),
        in_specs=[VMEM] * 9,
        out_specs=(HBM, HBM),
        scratch_shapes=[
            pltpu.VMEM((2 * ITERS + 1, n_sub, LANES), f32),
            pltpu.VMEM(body_load.shape, f32),
            pltpu.VMEM((1, comp, depth, py), f32),
            pltpu.SemaphoreType.DMA((depth + 1,)),
        ],
        compiler_params=params(16),
        name="final",
    )(messages, v0, v1, v2, right, left_next, tab, coarse, corner_index.reshape(1, count))


def solution(mesh):
    return jax.shard_map(
        on_device,
        mesh=mesh,
        in_specs=(
            P(None, "in", None, "sub"),
            P("in", None, "sub"),
            P(),
            P(("sub", "in")),
            P(("sub", "in"), None),
        ),
        out_specs=(P(None, "in", None, "sub"), P("sub", None, "in", None)),
        check_vma=False,
    )
```
